128 devices in a mesh: dap: 4 (over z_lo, core), dp: 32 (over z_hi, y, x).
Axes of the slice: x: 4, y: 4, z: 4 (z_hi: 2, z_lo: 2; z = z_hi * 2 + z_lo), core: 2. Of those that a mesh axis runs over, the one named last changes fastest.
Arguments:
- pair_rep: bfloat16 [32, 128, 128, 128], P('dp', 'dap'), may hold values from -6 to 6
- cotangent: bfloat16 [32, 128, 128, 128], P('dp', 'dap'), may hold values from -6 to 6
- tok_mask: int32 [32, 128], P('dp'), may hold values from 0 to 1, as said below
- tok_types: int32 [32, 128], P('dp'), may hold values from 0 to 3
- pair_mask: int32 [32, 128, 128], P('dp', 'dap'), may hold values 0 or 1
- triangle_gain: float32 [128], replicated, may hold values from 0.5 to 1.5
- triangle_input: bfloat16 [128, 512], replicated, may hold values from -0.5 to 0.5
- triangle_gating: bfloat16 [128, 128], replicated, may hold values from -0.5 to 0.5
- product_gain: float32 [128], replicated, may hold values from 0.5 to 1.5
- triangle_output: bfloat16 [128, 128], replicated, may hold values from -0.5 to 0.5
- attend_gain: float32 [128], replicated, may hold values from 0.5 to 1.5
- attend_bias: bfloat16 [128, 4], replicated, may hold values from -0.5 to 0.5
- attend_input: bfloat16 [128, 512], replicated, may hold values from -0.5 to 0.5
- attend_output: bfloat16 [128, 128], replicated, may hold values from -0.5 to 0.5
- type_table: float32 [4, 4, 4], replicated, may hold values from -4 to 4
Outputs:
- pair_out: bfloat16 [32, 128, 128, 128], P('dp', 'dap')
- pair_grad: bfloat16 [32, 128, 128, 128], P('dp', 'dap')
- grad_triangle_gain: float32 [128], replicated
- grad_triangle_input: float32 [128, 512], replicated
- grad_triangle_gating: float32 [128, 128], replicated
- grad_product_gain: float32 [128], replicated
- grad_triangle_output: float32 [128, 128], replicated
- grad_attend_gain: float32 [128], replicated
- grad_attend_bias: float32 [128, 4], replicated
- grad_attend_input: float32 [128, 512], replicated
- grad_attend_output: float32 [128, 128], replicated
- grad_type_table: float32 [4, 4, 4], replicated
The draws below stay inside these ranges and needn't reach their ends.
Inputs may be any that keep to these rules, and one draw needn't show every extreme that they name: `tok_mask`: each crop's real tokens form a leading run of at least 64 tokens.
All inputs are finite; a program needn't handle non-finite values. No bound on the sum of `pair_mask` on one device may be relied on, other than what follows from the above.
Results may differ from the reference program's by a relative error of at most 0.035.
Values may be sent and summed in bfloat16 or wider, within the bound.
A program may use at most 128 MiB of HBM per device.

```python
from functools import partial
import jax
import jax.numpy as jnp
from jax import lax

C = 128
H = 4
TYPES = 4
N = 128
CROPS = 32
N_DAP = 4
N_DP = 32


def draw_tok_mask(key, part):
    lengths = jax.random.randint(key, (CROPS,), N // 2, N + 1)
    return (jnp.arange(N, dtype=jnp.int32)[None, :] < lengths[:, None]).astype(jnp.int32)


def set_ends(entries, key, least, high):
    dims = entries.shape
    index_at = [jax.random.randint(jax.random.fold_in(key, axis), (), 0, dims[axis]) for axis in range(len(dims))]
    entries = entries.at[tuple(index_at)].set(least)
    longest = dims.index(max(dims))
    index_at[longest] = (index_at[longest] + 1) % dims[longest]
    return entries.at[tuple(index_at)].set(high)


def shard_levels(rng, shape, cuts, least, top_value):
    level = 1.0
    for position, parts in cuts:
        heights = jax.random.uniform(jax.random.fold_in(jax.random.fold_in(rng, 6), position), (parts,), jnp.float32, least / len(cuts), top_value / len(cuts))
        level = level * jnp.repeat(jnp.exp(heights), shape[position] // parts).reshape((-1,) + (1,) * (len(shape) - 1 - position))
    return level


def noise(stream_key, dims, width, most, shards=(), kind=jnp.bfloat16):
    values = jax.random.normal(stream_key, dims, jnp.float32) * width
    if len(shards) > 0:
        values = shard_levels(stream_key, dims, shards, -0.22, 0.18) * values
    return jnp.clip(values, min=-most, max=most).astype(kind)


def setup_inputs(seed: int = 0) -> dict:
    splits = jax.random.split(jax.random.key(seed), 16)
    return {
        "pair_rep": noise(splits[0], (CROPS, N, N, C), 1.0, 6.0, ((0, 32), (1, 4))),
        "cotangent": noise(splits[1], (CROPS, N, N, C), 1.0, 6.0, ((0, 32), (1, 4))),
        "tok_mask": draw_tok_mask(jax.random.fold_in(splits[15], 71), 0),
        "tok_types": set_ends(jax.random.randint(splits[3], (CROPS, N), 0, TYPES), jax.random.fold_in(splits[3], 1), 0, TYPES - 1).astype(jnp.int32),
        "pair_mask": set_ends((jax.random.randint(splits[4], (CROPS, N, N), 0, 8) < 7).astype(jnp.int32), jax.random.fold_in(splits[4], 1), 0, 1),
        "triangle_gain": jnp.clip(1.0 + 0.1 * jax.random.normal(splits[5], (C,), jnp.float32), 0.5, 1.5),
        "triangle_input": noise(splits[6], (C, 4 * C), C ** -0.5, 0.5),
        "triangle_gating": noise(splits[7], (C, C), C ** -0.5, 0.5),
        "product_gain": jnp.clip(1.0 + 0.1 * jax.random.normal(splits[8], (C,), jnp.float32), 0.5, 1.5),
        "triangle_output": noise(splits[9], (C, C), C ** -0.5, 0.5),
        "attend_gain": jnp.clip(1.0 + 0.1 * jax.random.normal(splits[10], (C,), jnp.float32), 0.5, 1.5),
        "attend_bias": noise(splits[11], (C, H), C ** -0.5, 0.5),
        "attend_input": noise(splits[12], (C, 4 * C), C ** -0.5, 0.5),
        "attend_output": noise(splits[13], (C, C), C ** -0.5, 0.5),
        "type_table": noise(splits[14], (H, TYPES, TYPES), 1.0, 4.0, (), jnp.float32),
    }


EPSILON = 1e-05

def layer_norm(values, scales):
    centred = values - lax.optimization_barrier(jnp.mean(values, axis=-1, keepdims=True))
    spread = lax.optimization_barrier(jnp.mean(centred * centred, axis=-1, keepdims=True))
    return centred * lax.rsqrt(spread + EPSILON) * scales

def triangle_first(slab, scales, input_w, gating_w, pair_live):
    channels = slab.shape[-1]
    normed = layer_norm(slab.astype(jnp.float32), scales).astype(jnp.bfloat16)
    projected = jnp.einsum('ijc,cd->ijd', normed.astype(jnp.float32), input_w.astype(jnp.float32))
    masked = pair_live[..., None]
    left_proj = (jax.nn.sigmoid(projected[..., channels:2 * channels]) * projected[..., :channels] * masked).astype(jnp.bfloat16)
    right_proj = (jax.nn.sigmoid(projected[..., 3 * channels:]) * projected[..., 2 * channels:3 * channels] * masked).astype(jnp.bfloat16)
    out_gate = jax.nn.sigmoid(jnp.einsum('ijc,cd->ijd', normed.astype(jnp.float32), gating_w.astype(jnp.float32)))
    return (left_proj, right_proj, out_gate)

def triangle_second(slab, product, out_gate, scales, output_w):
    normed = layer_norm(product, scales).astype(jnp.bfloat16)
    update = out_gate * jnp.einsum('ijc,cd->ijd', normed.astype(jnp.float32), output_w.astype(jnp.float32))
    return (slab.astype(jnp.float32) + update).astype(jnp.bfloat16)

def attend_first(middle, scales, bias_w):
    normed = layer_norm(middle.astype(jnp.float32), scales).astype(jnp.bfloat16)
    bias_rows = jnp.einsum('rjc,ch->hrj', normed.astype(jnp.float32), bias_w.astype(jnp.float32)).astype(jnp.bfloat16)
    return (normed, bias_rows)

def attend_second(middle, normed, bias_all, table, input_w, output_w, one_hot, key_live):
    row_count, length, channels = middle.shape
    head_count = bias_all.shape[0]
    head_size = channels // head_count
    projected = jnp.einsum('ijc,cd->ijd', normed.astype(jnp.float32), input_w.astype(jnp.float32))
    query = projected[..., :channels].astype(jnp.bfloat16).reshape(row_count, length, head_count, head_size)
    keys_all = projected[..., channels:2 * channels].astype(jnp.bfloat16).reshape(row_count, length, head_count, head_size)
    values_all = projected[..., 2 * channels:3 * channels].astype(jnp.bfloat16).reshape(row_count, length, head_count, head_size)
    gate = jax.nn.sigmoid(projected[..., 3 * channels:])
    type_bias = jnp.einsum('ja,hab,kb->hjk', one_hot, table, one_hot)
    scores = jnp.einsum('rjhd,rkhd->rhjk', query.astype(jnp.float32), keys_all.astype(jnp.float32)) / jnp.sqrt(jnp.float32(head_size))
    scores = scores + (bias_all + type_bias)[None]
    exponent = jnp.exp(scores) * key_live[:, None, None, :]
    totals = jnp.maximum(lax.optimization_barrier(jnp.sum(exponent, axis=-1, keepdims=True)), 1.0)
    weights = (exponent / totals).astype(jnp.bfloat16)
    attended = jnp.einsum('rhjk,rkhd->rjhd', weights.astype(jnp.float32), values_all.astype(jnp.float32)).reshape(row_count, length, channels)
    gated = (gate * attended).astype(jnp.bfloat16)
    update = jnp.einsum('ijc,cd->ijd', gated.astype(jnp.float32), output_w.astype(jnp.float32))
    return (middle.astype(jnp.float32) + update).astype(jnp.bfloat16)

def reference(pair_rep, cotangent, tok_mask, tok_types, pair_mask, triangle_gain, triangle_input, triangle_gating, product_gain, triangle_output, attend_gain, attend_bias, attend_input, attend_output, type_table):
    span = N // N_DAP

    def one_crop(inputs):
        slab_all, cot_all, tokens_in, types_in, mask_in = inputs
        tokens = tokens_in.astype(jnp.float32)
        pair_live = mask_in.astype(jnp.float32) * tokens[:, None] * tokens[None, :]
        one_hot = (types_in[:, None] == jnp.arange(TYPES, dtype=jnp.int32)[None, :]).astype(jnp.float32)
        first_backs = []
        left_list = []
        right_list = []
        gate_list = []
        for portion in range(N_DAP):
            lower_row = portion * span
            upper_row = lower_row + span
            outputs, pullback = jax.vjp(partial(triangle_first, pair_live=pair_live[lower_row:upper_row]), slab_all[lower_row:upper_row], triangle_gain, triangle_input, triangle_gating)
            first_backs.append(pullback)
            left_list.append(outputs[0])
            right_list.append(outputs[1])
            gate_list.append(outputs[2])
        right_all = jnp.concatenate(right_list, axis=0)
        second_backs = []
        middle_list = []
        third_backs = []
        normed_list = []
        bias_list = []
        for portion in range(N_DAP):
            lower_row = portion * span
            upper_row = lower_row + span
            product = jnp.einsum('ikc,jkc->ijc', left_list[portion].astype(jnp.float32), right_all.astype(jnp.float32))
            middle, pullback = jax.vjp(triangle_second, slab_all[lower_row:upper_row], product, gate_list[portion], product_gain, triangle_output)
            second_backs.append(pullback)
            middle_list.append(middle)
            outputs, pullback = jax.vjp(attend_first, middle, attend_gain, attend_bias)
            third_backs.append(pullback)
            normed_list.append(outputs[0])
            bias_list.append(outputs[1])
        bias_all = jnp.concatenate(bias_list, axis=1).astype(jnp.float32)
        fourth_backs = []
        out_list = []
        for portion in range(N_DAP):
            lower_row = portion * span
            upper_row = lower_row + span
            result, pullback = jax.vjp(partial(attend_second, one_hot=one_hot, key_live=pair_live[lower_row:upper_row]), middle_list[portion], normed_list[portion], bias_all, type_table, attend_input, attend_output)
            fourth_backs.append(pullback)
            out_list.append(result)
        fourth_grads = [fourth_backs[portion](cot_all[portion * span:(portion + 1) * span]) for portion in range(N_DAP)]
        bias_grad = fourth_grads[0][2]
        for portion in range(1, N_DAP):
            bias_grad = bias_grad + fourth_grads[portion][2]
        bias_grad = bias_grad.astype(jnp.bfloat16)
        grads = [jnp.zeros_like(triangle_gain), jnp.zeros(triangle_input.shape, jnp.float32), jnp.zeros(triangle_gating.shape, jnp.float32), jnp.zeros_like(product_gain), jnp.zeros(triangle_output.shape, jnp.float32), jnp.zeros_like(attend_gain), jnp.zeros(attend_bias.shape, jnp.float32), jnp.zeros(attend_input.shape, jnp.float32), jnp.zeros(attend_output.shape, jnp.float32), jnp.zeros_like(type_table)]
        d_product_list = []
        d_gate_list = []
        d_slab_list = []
        for portion in range(N_DAP):
            lower_row = portion * span
            upper_row = lower_row + span
            d_middle_a, d_normed, unused_bias, d_table, d_att_in, d_att_out = fourth_grads[portion]
            d_middle_b, d_att_gain, d_att_bias = third_backs[portion]((d_normed, bias_grad[:, lower_row:upper_row]))
            d_middle = d_middle_a + d_middle_b
            d_slab_c, d_product, d_gate, d_prod_gain, d_tri_out = second_backs[portion](d_middle)
            d_product_list.append(d_product)
            d_gate_list.append(d_gate)
            d_slab_list.append(d_slab_c)
            grads[3] = grads[3] + d_prod_gain.astype(jnp.float32)
            grads[4] = grads[4] + d_tri_out.astype(jnp.float32)
            grads[5] = grads[5] + d_att_gain.astype(jnp.float32)
            grads[6] = grads[6] + d_att_bias.astype(jnp.float32)
            grads[7] = grads[7] + d_att_in.astype(jnp.float32)
            grads[8] = grads[8] + d_att_out.astype(jnp.float32)
            grads[9] = grads[9] + d_table.astype(jnp.float32)
        d_right_all = jnp.zeros(right_all.shape, jnp.float32)
        for portion in range(N_DAP):
            d_right_all = d_right_all + jnp.einsum('ijc,ikc->jkc', d_product_list[portion], left_list[portion].astype(jnp.float32), precision=lax.Precision.HIGHEST)
        d_right_all = d_right_all.astype(jnp.bfloat16)
        grad_list = []
        for portion in range(N_DAP):
            lower_row = portion * span
            upper_row = lower_row + span
            d_left = jnp.einsum('ijc,jkc->ikc', d_product_list[portion], right_all.astype(jnp.float32), precision=lax.Precision.HIGHEST).astype(jnp.bfloat16)
            d_slab_d, d_tri_gain, d_tri_in, d_tri_gate = first_backs[portion]((d_left, d_right_all[lower_row:upper_row], d_gate_list[portion]))
            grads[0] = grads[0] + d_tri_gain.astype(jnp.float32)
            grads[1] = grads[1] + d_tri_in.astype(jnp.float32)
            grads[2] = grads[2] + d_tri_gate.astype(jnp.float32)
            grad_list.append(d_slab_list[portion] + d_slab_d)
        return (jnp.concatenate(out_list, axis=0), jnp.concatenate(grad_list, axis=0), tuple(grads))
    pair_out, pair_grad, crop_grads = lax.map(one_crop, (pair_rep, cotangent, tok_mask, tok_types, pair_mask))
    factor = jnp.float32((N * N * N_DP) ** (-0.5))
    summed = [lax.optimization_barrier(jnp.sum(member, axis=0)) * factor for member in crop_grads]
    return (pair_out, pair_grad, summed[0], summed[1], summed[2], summed[3], summed[4], summed[5], summed[6], summed[7], summed[8], summed[9])
```

```python
from functools import partial

import jax
import jax.numpy as jnp
from jax import lax
from jax.experimental import pallas as pl
from jax.experimental.pallas import tpu as pltpu
from jax.sharding import PartitionSpec as P

EPSILON = 1e-05
MESH = pl.DeviceIdType.MESH
VM = pltpu.VMEM


def greet(peers):
    barrier = pltpu.get_barrier_semaphore()
    for ids in peers:
        pl.semaphore_signal(barrier, inc=1, device_id=ids, device_id_type=MESH)
    pl.semaphore_wait(barrier, len(peers))


def reduce_kernel(n_dp, factor, tri_in, tri_gate, tri_out, att_in, att_out, small,
                  o_tri_in, o_tri_gate, o_tri_out, o_att_in, o_att_out, o_small,
                  g, part, quarter, pieces, mine, joined, full, sa, ra, sb, rb, sc, rc, sd, rd):
    a = lax.axis_index("dap")
    p = lax.axis_index("dp")
    rows = quarter.shape[0]
    piece = rows // n_dp

    def greet_dp(r, carry):
        pl.semaphore_signal(barrier, inc=1, device_id={"dp": lax.rem(p + r, n_dp)}, device_id_type=MESH)
        return carry

    barrier = pltpu.get_barrier_semaphore()
    for r in range(1, 4):
        pl.semaphore_signal(barrier, inc=1, device_id={"dap": lax.rem(a + r, 4)}, device_id_type=MESH)
    lax.fori_loop(1, n_dp, greet_dp, 0)
    for b in range(4):
        g[b * 128 : (b + 1) * 128, :] = tri_in[:, b * 128 : (b + 1) * 128]
        g[(b + 4) * 128 : (b + 5) * 128, :] = att_in[:, b * 128 : (b + 1) * 128]
    g[1024:1152, :] = tri_gate[...]
    g[1152:1280, :] = tri_out[...]
    g[1280:1408, :] = att_out[...]
    g[1408:1424, :] = small[...]
    g[1424:, :] = jnp.zeros((4 * rows - 1424, 128), jnp.bfloat16)
    pl.semaphore_wait(barrier, 3 + n_dp - 1)

    def copy_a(r):
        peer = lax.rem(a + r, 4)
        return pltpu.make_async_remote_copy(
            src_ref=g.at[pl.ds(pl.multiple_of(peer * rows, rows), rows)], dst_ref=part.at[r - 1],
            send_sem=sa.at[r - 1], recv_sem=ra.at[r - 1], device_id={"dap": peer}, device_id_type=MESH)

    for r in (2, 1, 3):
        copy_a(r).start()
    for r in (1, 2, 3):
        copy_a(r).wait_recv()
    total = g[pl.ds(pl.multiple_of(a * rows, rows), rows), :].astype(jnp.float32)
    for r in range(3):
        total = total + part[r].astype(jnp.float32)
    quarter[...] = total.astype(jnp.bfloat16)

    def copy_b(r):
        peer = lax.rem(p + r, n_dp)
        return pltpu.make_async_remote_copy(
            src_ref=quarter.at[pl.ds(pl.multiple_of(peer * piece, piece), piece)], dst_ref=pieces.at[r - 1],
            send_sem=sb.at[r - 1], recv_sem=rb.at[r - 1], device_id={"dp": peer}, device_id_type=MESH)

    def each(fn):
        def body(r, carry):
            fn(r)
            return carry
        lax.fori_loop(1, n_dp, body, 0)

    each(lambda r: copy_b(r).start())
    each(lambda r: copy_b(r).wait_recv())
    own = pl.ds(pl.multiple_of(p * piece, piece), piece)
    total = quarter[own, :].astype(jnp.float32) + jnp.sum(pieces[...].astype(jnp.float32), axis=0)
    mine[...] = (total * factor).astype(jnp.bfloat16)

    def copy_c(r):
        peer = lax.rem(p + r, n_dp)
        return pltpu.make_async_remote_copy(
            src_ref=mine, dst_ref=joined.at[own],
            send_sem=sc.at[r - 1], recv_sem=rc.at[r - 1], device_id={"dp": peer}, device_id_type=MESH)

    each(lambda r: copy_c(r).start())
    joined[own, :] = mine[...]

    def wait_c(r):
        src = lax.rem(p + n_dp - r, n_dp)
        pltpu.make_async_remote_copy(
            src_ref=mine, dst_ref=joined.at[pl.ds(pl.multiple_of(src * piece, piece), piece)],
            send_sem=sc.at[r - 1], recv_sem=rc.at[r - 1], device_id={"dp": lax.rem(p + r, n_dp)}, device_id_type=MESH).wait_recv()

    each(wait_c)

    def copy_d(k):
        block = (a, a, lax.rem(a + 2, 4))[k]
        target = (lax.rem(a + 2, 4), a + 1 - 2 * lax.rem(a, 2), a + 1 - 2 * lax.rem(a, 2))[k]
        there = pl.ds(pl.multiple_of(block * rows, rows), rows)
        return pltpu.make_async_remote_copy(
            src_ref=joined if k < 2 else full.at[there], dst_ref=full.at[there],
            send_sem=sd.at[k], recv_sem=rd.at[k], device_id={"dap": target}, device_id_type=MESH)

    copy_d(0).start()
    copy_d(1).start()
    full[pl.ds(pl.multiple_of(a * rows, rows), rows), :] = joined[...]
    copy_d(0).wait_recv()
    copy_d(2).start()
    copy_d(1).wait_recv()
    copy_d(2).wait_recv()
    for b in range(4):
        o_tri_in[:, b * 128 : (b + 1) * 128] = full[b * 128 : (b + 1) * 128, :].astype(jnp.float32)
        o_att_in[:, b * 128 : (b + 1) * 128] = full[(b + 4) * 128 : (b + 5) * 128, :].astype(jnp.float32)
    o_tri_gate[...] = full[1024:1152, :].astype(jnp.float32)
    o_tri_out[...] = full[1152:1280, :].astype(jnp.float32)
    o_att_out[...] = full[1280:1408, :].astype(jnp.float32)
    o_small[...] = full[1408:1424, :].astype(jnp.float32)
    for r in (1, 2, 3):
        copy_a(r).wait_send()
    each(lambda r: copy_b(r).wait_send())
    each(lambda r: copy_c(r).wait_send())
    for k in range(3):
        copy_d(k).wait_send()


def reduce_all(n_dp, factor, tri_in, tri_gate, tri_out, att_in, att_out, small):
    rows = 16 * n_dp
    f32, bf = jnp.float32, jnp.bfloat16
    return pl.pallas_call(
        partial(reduce_kernel, n_dp, factor),
        out_shape=[jax.ShapeDtypeStruct(v.shape, f32) for v in (tri_in, tri_gate, tri_out, att_in, att_out, small)],
        in_specs=[pl.BlockSpec(memory_space=VM)] * 6,
        out_specs=[pl.BlockSpec(memory_space=VM)] * 6,
        scratch_shapes=[
            VM((4 * rows, 128), bf), VM((3, rows, 128), bf), VM((rows, 128), bf), VM((n_dp - 1, 16, 128), bf),
            VM((16, 128), bf), VM((rows, 128), bf), VM((4 * rows, 128), bf),
        ] + [pltpu.SemaphoreType.DMA((3,))] * 2 + [pltpu.SemaphoreType.DMA((n_dp - 1,))] * 4
          + [pltpu.SemaphoreType.DMA((3,))] * 2,
        compiler_params=pltpu.CompilerParams(collective_id=0, has_side_effects=True, vmem_limit_bytes=32 << 20),
        name="gradient_sum",
    )(tri_in, tri_gate, tri_out, att_in, att_out, small)


def layer_norm(values, scales):
    centred = values - jnp.mean(values, axis=-1, keepdims=True)
    spread = jnp.mean(centred * centred, axis=-1, keepdims=True)
    return centred * lax.rsqrt(spread + EPSILON) * scales


def triangle_first(slab, scales, input_w, gating_w, pair_live):
    channels = slab.shape[-1]
    normed = layer_norm(slab.astype(jnp.float32), scales).astype(jnp.bfloat16)
    projected = jnp.einsum("ijc,cd->ijd", normed, input_w, preferred_element_type=jnp.float32)
    masked = pair_live[..., None]
    left_proj = (
        jax.nn.sigmoid(projected[..., channels : 2 * channels]) * projected[..., :channels] * masked
    ).astype(jnp.bfloat16)
    right_proj = (
        jax.nn.sigmoid(projected[..., 3 * channels :])
        * projected[..., 2 * channels : 3 * channels]
        * masked
    ).astype(jnp.bfloat16)
    out_gate = jax.nn.sigmoid(
        jnp.einsum("ijc,cd->ijd", normed, gating_w, preferred_element_type=jnp.float32)
    )
    return (left_proj, right_proj, out_gate)


def triangle_second(slab, product, out_gate, scales, output_w):
    normed = layer_norm(product, scales).astype(jnp.bfloat16)
    update = out_gate * jnp.einsum(
        "ijc,cd->ijd", normed, output_w, preferred_element_type=jnp.float32
    )
    return (slab.astype(jnp.float32) + update).astype(jnp.bfloat16)


def attend_first(middle, scales, bias_w):
    normed = layer_norm(middle.astype(jnp.float32), scales).astype(jnp.bfloat16)
    bias_rows = jnp.einsum(
        "rjc,ch->hrj", normed, bias_w, preferred_element_type=jnp.float32
    ).astype(jnp.bfloat16)
    return (normed, bias_rows)


def attend_second(middle, normed, bias_all, table, input_w, output_w, one_hot, key_live):
    row_count, length, channels = middle.shape
    head_count = bias_all.shape[0]
    head_size = channels // head_count
    projected = jnp.einsum("ijc,cd->ijd", normed, input_w, preferred_element_type=jnp.float32)
    query = (
        projected[..., :channels]
        .astype(jnp.bfloat16)
        .reshape(row_count, length, head_count, head_size)
    )
    keys_all = (
        projected[..., channels : 2 * channels]
        .astype(jnp.bfloat16)
        .reshape(row_count, length, head_count, head_size)
    )
    values_all = (
        projected[..., 2 * channels : 3 * channels]
        .astype(jnp.bfloat16)
        .reshape(row_count, length, head_count, head_size)
    )
    gate = jax.nn.sigmoid(projected[..., 3 * channels :])
    type_bias = jnp.einsum("ja,hab,kb->hjk", one_hot, table, one_hot)
    scores = jnp.einsum(
        "rjhd,rkhd->rhjk", query, keys_all, preferred_element_type=jnp.float32
    ) / jnp.sqrt(jnp.float32(head_size))
    scores = scores + (bias_all + type_bias)[None]
    exponent = jnp.exp(scores) * key_live[:, None, None, :]
    totals = jnp.maximum(jnp.sum(exponent, axis=-1, keepdims=True), 1.0)
    weights = (exponent / totals).astype(jnp.bfloat16)
    attended = jnp.einsum(
        "rhjk,rkhd->rjhd", weights, values_all, preferred_element_type=jnp.float32
    ).reshape(row_count, length, channels)
    gated = (gate * attended).astype(jnp.bfloat16)
    update = jnp.einsum("ijc,cd->ijd", gated, output_w, preferred_element_type=jnp.float32)
    return (middle.astype(jnp.float32) + update).astype(jnp.bfloat16)


def per_device(
    pair_rep,
    cotangent,
    tok_mask,
    tok_types,
    pair_mask,
    triangle_gain,
    triangle_input,
    triangle_gating,
    product_gain,
    triangle_output,
    attend_gain,
    attend_bias,
    attend_input,
    attend_output,
    type_table,
):
    slab = pair_rep[0]
    row_count = slab.shape[0]
    length = slab.shape[1]
    tokens = tok_mask[0].astype(jnp.float32)
    first_row = lax.axis_index("dap") * row_count
    row_tokens = lax.dynamic_slice_in_dim(tokens, first_row, row_count)
    pair_live = pair_mask[0].astype(jnp.float32) * row_tokens[:, None] * tokens[None, :]
    one_hot = (
        tok_types[0][:, None] == jnp.arange(type_table.shape[1], dtype=jnp.int32)[None, :]
    ).astype(jnp.float32)
    first_out, first_back = jax.vjp(
        partial(triangle_first, pair_live=pair_live),
        slab,
        triangle_gain,
        triangle_input,
        triangle_gating,
    )
    left_proj, right_proj, out_gate = first_out
    right_all = lax.all_gather(right_proj, "dap", axis=0, tiled=True)
    product = jnp.einsum("ikc,jkc->ijc", left_proj, right_all, preferred_element_type=jnp.float32)
    middle, second_back = jax.vjp(
        triangle_second, slab, product, out_gate, product_gain, triangle_output
    )
    third_out, third_back = jax.vjp(attend_first, middle, attend_gain, attend_bias)
    normed, bias_rows = third_out
    bias_all = lax.all_gather(bias_rows, "dap", axis=1, tiled=True).astype(jnp.float32)
    pair_out, fourth_back = jax.vjp(
        partial(attend_second, one_hot=one_hot, key_live=pair_live),
        middle,
        normed,
        bias_all,
        type_table,
        attend_input,
        attend_output,
    )
    d_middle_a, d_normed, d_bias_all, d_table, d_att_in, d_att_out = fourth_back(cotangent[0])
    d_bias_rows = lax.psum_scatter(
        d_bias_all.astype(jnp.bfloat16), "dap", scatter_dimension=1, tiled=True
    )
    d_middle_b, d_att_gain, d_att_bias = third_back((d_normed, d_bias_rows))
    d_middle = d_middle_a + d_middle_b
    d_slab_c, d_product, d_gate, d_prod_gain, d_tri_out = second_back(d_middle)
    d_left = jnp.einsum(
        "ijc,jkc->ikc", d_product, right_all, preferred_element_type=jnp.float32
    ).astype(jnp.bfloat16)
    d_right = lax.psum_scatter(
        jnp.einsum("ijc,ikc->jkc", d_product, left_proj, preferred_element_type=jnp.float32).astype(
            jnp.bfloat16
        ),
        "dap",
        scatter_dimension=0,
        tiled=True,
    ).astype(jnp.float32)
    d_right = d_right.astype(jnp.bfloat16)
    d_slab_d, d_tri_gain, d_tri_in, d_tri_gate = first_back((d_left, d_right, d_gate))
    d_slab = d_slab_c + d_slab_d
    factor = (length * length * lax.axis_size("dp")) ** (-0.5)
    small = jnp.concatenate(
        [
            d_tri_gain[None],
            d_prod_gain[None],
            d_att_gain[None],
            d_att_bias.astype(jnp.float32).T,
            jnp.pad(d_table.reshape(1, -1), ((0, 0), (0, 64))),
            jnp.zeros((8, 128), jnp.float32),
        ]
    ).astype(jnp.bfloat16)
    g_in, g_gate, g_out, g_att_in, g_att_out, g_small = reduce_all(
        lax.axis_size("dp"), factor, d_tri_in, d_tri_gate, d_tri_out, d_att_in, d_att_out, small
    )
    return (
        pair_out[None],
        d_slab[None],
        g_small[0],
        g_in,
        g_gate,
        g_small[1],
        g_out,
        g_small[2],
        g_small[3:7].T,
        g_att_in,
        g_att_out,
        g_small[7, :64].reshape(type_table.shape),
    )


def solution(mesh):
    return jax.shard_map(
        per_device,
        mesh=mesh,
        in_specs=(
            P("dp", "dap", None, None),
            P("dp", "dap", None, None),
            P("dp", None),
            P("dp", None),
            P("dp", "dap", None),
            P(),
            P(),
            P(),
            P(),
            P(),
            P(),
            P(),
            P(),
            P(),
            P(),
        ),
        out_specs=(
            P("dp", "dap", None, None),
            P("dp", "dap", None, None),
            P(),
            P(),
            P(),
            P(),
            P(),
            P(),
            P(),
            P(),
            P(),
            P(),
        ),
        check_vma=False,
    )
```

```python
from functools import partial

import jax
import jax.numpy as jnp
from jax import lax
from jax.experimental import pallas as pl
from jax.experimental.pallas import tpu as pltpu
from jax.sharding import PartitionSpec as P

EPSILON = 1e-05
MESH = pl.DeviceIdType.MESH
VM = pltpu.VMEM


def mm(x, y):
    return lax.dot_general(x, y, (((1,), (0,)), ((), ())), preferred_element_type=jnp.float32)


def nt(x, y):
    return lax.dot_general(x, y, (((1,), (1,)), ((), ())), preferred_element_type=jnp.float32)


def tn(x, y):
    return lax.dot_general(x, y, (((0,), (0,)), ((), ())), preferred_element_type=jnp.float32)


def eye():
    rows = lax.broadcasted_iota(jnp.int32, (128, 128), 0)
    return (rows == lax.broadcasted_iota(jnp.int32, (128, 128), 1)).astype(jnp.float32).astype(jnp.bfloat16)


def flip(unit, block):
    return nt(unit, block)


def norm_cols(x):
    mean = jnp.sum(x, axis=0, keepdims=True) * (1.0 / 128)
    centred = x - mean
    spread = jnp.sum(centred * centred, axis=0, keepdims=True) * (1.0 / 128)
    scale = lax.rsqrt(spread + EPSILON)
    return centred * scale, scale


def norm_back(grad, unit, scale):
    a = jnp.sum(grad, axis=0, keepdims=True) * (1.0 / 128)
    b = jnp.sum(grad * unit, axis=0, keepdims=True) * (1.0 / 128)
    return scale * (grad - a - unit * b)


def wide(col, lanes):
    return col if lanes == 128 else jnp.concatenate([col] * (lanes // 128), axis=1)


def places():
    a = lax.axis_index("dap")
    return a, a + 1 - 2 * lax.rem(a, 2), lax.rem(a + 2, 4), a // 2


def greet_dap(a):
    barrier = pltpu.get_barrier_semaphore()
    for r in range(1, 4):
        pl.semaphore_signal(barrier, inc=1, device_id={"dap": lax.rem(a + r, 4)}, device_id_type=MESH)
    return barrier


def loop(n, fn, unroll=1):
    def body(i, carry):
        fn(i)
        return carry
    lax.fori_loop(0, n, body, 0, unroll=unroll)


def at(i, size):
    return pl.ds(pl.multiple_of(i * size, size), size)


def forward_kernel(slab, live, g1, g2, g3, w1t, woutt, wbt, mid, prod, right, bias,
                   left_f, right_f, gates, bias_f, bias_b, sem_s, sem_r, bsem_s, bsem_r):
    bf, f32 = jnp.bfloat16, jnp.float32
    a, partner, cross, chip = places()
    barrier = greet_dap(a)
    unit = eye()

    def edge(kind, c):
        block = cross if kind == 2 else a
        spot = right.at[block, at(c, 8)]
        return pltpu.make_async_remote_copy(
            src_ref=spot, dst_ref=spot, send_sem=sem_s.at[kind, c], recv_sem=sem_r.at[kind, c],
            device_id={"dap": cross if kind == 1 else partner}, device_id_type=MESH)

    def project(c, t):
        i = c * 8 + 2 * t
        x = jnp.concatenate([flip(unit, slab[i]), flip(unit, slab[i + 1])], axis=1)
        hat, _ = norm_cols(x)
        n = (hat * wide(g1[...], 256)).astype(bf)
        p = mm(w1t[...], n)
        alive = jnp.concatenate([live[pl.ds(i, 1), :], live[pl.ds(i + 1, 1), :]], axis=1)
        lft = (jax.nn.sigmoid(p[128:256]) * p[:128] * alive).astype(bf)
        rgt = (jax.nn.sigmoid(p[512:]) * p[384:512] * alive).astype(bf)
        gate = jax.nn.sigmoid(p[256:384])
        for r in range(2):
            lane = slice(128 * r, 128 * r + 128)
            left_f[at(i + r, 128), :] = lft[:, lane].astype(f32)
            right[a, i + r] = rgt[:, lane]
            gates[i + r] = gate[:, lane]

    def first(c):
        loop(4, lambda t: project(c, t))
        pl.when(c == 0)(lambda: pl.semaphore_wait(barrier, 3))
        edge(1, c).start()
        edge(0, c).start()

    loop(4, first)

    def unpack(block, base):
        loop(32, lambda j: right_f.__setitem__((at(base + j, 128), slice(None)), right[block, j].astype(f32)), 2)

    def multiply(half):
        def one(ch):
            lft = left_f[pl.ds(ch, 32, stride=128), :].astype(bf)
            rgt = right_f[pl.ds(ch, 64, stride=128), :].astype(bf)
            prod[at(ch, 32), 64 * half : 64 * half + 64] = nt(lft, rgt)
        loop(128, one, 4)

    loop(4, lambda c: edge(0, c).wait_recv())
    low = 2 * chip
    unpack(low, 0)
    unpack(low + 1, 32)
    multiply(0)

    def relay(c):
        edge(1, c).wait_recv()
        edge(2, c).start()

    loop(4, relay)
    loop(4, lambda c: edge(2, c).wait_recv())
    unpack(2 - low, 0)
    unpack(3 - low, 32)
    multiply(1)

    def second(i):
        rows = pl.ds(i, 128, stride=32)
        x = pltpu.roll(prod[rows, :], 64 * chip, axis=1)
        prod[rows, :] = x
        hat, _ = norm_cols(x)
        n = (hat * g2[...]).astype(bf)
        middle = (flip(unit, slab[i]) + gates[i] * mm(woutt[...], n)).astype(bf)
        mid[i] = middle
        hat, _ = norm_cols(middle.astype(f32))
        n = (hat * g3[...]).astype(bf)
        heads = mm(wbt[...], n)
        for h in range(4):
            bias_f[h, pl.ds(i, 1), :] = heads[h : h + 1, :]

    loop(32, second, 2)
    bias_b[...] = bias_f[...].astype(bf)

    def share(r):
        return pltpu.make_async_remote_copy(
            src_ref=bias_b, dst_ref=bias.at[:, at(a, 32), :], send_sem=bsem_s.at[r - 1], recv_sem=bsem_r.at[r - 1],
            device_id={"dap": lax.rem(a + r, 4)}, device_id_type=MESH)

    for r in (2, 1, 3):
        share(r).start()
    bias[:, at(a, 32), :] = bias_b[...]
    for r in (1, 2, 3):
        share(r).wait_recv()
        share(r).wait_send()
    loop(4, lambda c: edge(0, c).wait_send())
    loop(4, lambda c: edge(1, c).wait_send())
    loop(4, lambda c: edge(2, c).wait_send())


DMA = pltpu.SemaphoreType.DMA
SPEC = pl.BlockSpec(memory_space=VM)


def forward(slab, live, g1, g2, g3, w1t, woutt, wbt):
    bf, f32 = jnp.bfloat16, jnp.float32
    return pl.pallas_call(
        forward_kernel,
        out_shape=[
            jax.ShapeDtypeStruct((32, 128, 128), bf), jax.ShapeDtypeStruct((4096, 128), f32),
            jax.ShapeDtypeStruct((4, 32, 128, 128), bf), jax.ShapeDtypeStruct((4, 128, 128), bf),
        ],
        in_specs=[SPEC] * 8, out_specs=[SPEC] * 4,
        scratch_shapes=[
            VM((4096, 128), f32), VM((8192, 128), f32), VM((32, 128, 128), f32), VM((4, 32, 128), f32),
            VM((4, 32, 128), bf), DMA((3, 4)), DMA((3, 4)), DMA((3,)), DMA((3,)),
        ],
        compiler_params=pltpu.CompilerParams(collective_id=1, has_side_effects=True, vmem_limit_bytes=48 << 20),
        name="triangle_forward",
    )(slab, live, g1, g2, g3, w1t, woutt, wbt)


def attend_kernel(mid, cot, alive, bias, types, g3, wat, wa, wo, wot, hot_t,
                  out, dn3, d_bias, d_wa, d_wo, d_table, bt):
    bf, f32 = jnp.bfloat16, jnp.float32
    step = pl.program_id(0)
    unit = eye()
    scale = 32.0 ** -0.5

    @pl.when(step == 0)
    def _():
        for h in range(4):
            bt[:, 128 * h : 128 * h + 128] = flip(unit, bias[h]) + types[h]
        d_bias[...] = jnp.zeros_like(d_bias)
        d_wa[...] = jnp.zeros_like(d_wa)
        d_wo[...] = jnp.zeros_like(d_wo)

    def spread(x):
        zero = jnp.zeros((32, 128), x.dtype)
        cols = [
            jnp.concatenate([x[32 * h : 32 * h + 32] if g == h else zero for g in range(4)], axis=0)
            for h in range(4)
        ]
        return jnp.concatenate(cols, axis=1)

    m = jnp.concatenate([mid[0], mid[1]], axis=1).astype(f32)
    hat, _ = norm_cols(m)
    n = (hat * wide(g3[...], 256)).astype(bf)
    p = mm(wat[...], n)
    pb = p[:384].astype(bf)
    gate = jax.nn.sigmoid(p[384:])
    ct = jnp.concatenate([flip(unit, cot[0]), flip(unit, cot[1])], axis=1).astype(bf)
    d_gated = mm(wo[...], ct).astype(bf).astype(f32)
    d_att = d_gated * gate
    parts, atts = [], []
    for r in range(2):
        lane = slice(128 * r, 128 * r + 128)
        q, k, v = pb[:128, lane], pb[128:256, lane], pb[256:384, lane]
        kv = flip(unit, pb[128:384, lane]).astype(bf)
        q4 = spread(q)
        e = jnp.exp(mm(kv[:, :128], q4) * scale + bt[...])
        e = e * wide(alive[r].astype(f32), 512)
        s = jnp.sum(e, axis=0, keepdims=True)
        w = e * (1.0 / jnp.maximum(s, 1.0))
        ab = w.astype(bf)
        atts.append(jnp.concatenate(
            [mm(v[32 * h : 32 * h + 32], ab[:, 128 * h : 128 * h + 128]) for h in range(4)], axis=0))
        do4 = spread(d_att[:, lane].astype(bf))
        da = mm(kv[:, 128:], do4).astype(bf).astype(f32)
        t = da * w
        total = jnp.sum(t, axis=0, keepdims=True)
        total = jnp.where(s > 1.0, total, jnp.where(s == 1.0, 0.5 * total, 0.0))
        ds = t - w * total
        d_bias[...] += ds
        dsb = ds.astype(bf)
        dv = nt(do4, ab)
        dk = nt(q4, dsb) * scale
        dq = jnp.concatenate(
            [mm(k[32 * h : 32 * h + 32], dsb[:, 128 * h : 128 * h + 128]) for h in range(4)], axis=0) * scale
        parts.append(jnp.concatenate([dq, dk, dv], axis=0).astype(bf))
    att = jnp.concatenate(atts, axis=1)
    d_gate = (d_gated * att * gate * (1.0 - gate)).astype(bf)
    dp = jnp.concatenate([jnp.concatenate(parts, axis=1), d_gate], axis=0)
    dn = mm(wa[...], dp).astype(bf)
    d_wa[...] += nt(dp, n)
    gated = (gate * att).astype(bf)
    d_wo[...] += nt(gated, ct)
    res = (m + mm(wot[...], gated)).astype(bf)
    for r in range(2):
        lane = slice(128 * r, 128 * r + 128)
        dn3[r] = dn[:, lane]
        out[r] = flip(unit, res[:, lane]).astype(bf)

    @pl.when(step == pl.num_programs(0) - 1)
    def _():
        part = mm(hot_t[...], d_bias[...].astype(bf)).astype(bf)
        for h in range(4):
            d_table[h] = nt(hot_t[...], part[:, 128 * h : 128 * h + 128])


def attend(mid, cot, alive, bias, types, g3, wat, wa, wo, wot, hot_t):
    bf, f32 = jnp.bfloat16, jnp.float32
    pair = pl.BlockSpec((2, 128, 128), lambda i: (i, 0, 0))

    def whole(shape):
        return pl.BlockSpec(shape, lambda i: (0,) * len(shape))

    return pl.pallas_call(
        attend_kernel,
        grid=(16,),
        out_shape=[
            jax.ShapeDtypeStruct((32, 128, 128), bf), jax.ShapeDtypeStruct((32, 128, 128), bf),
            jax.ShapeDtypeStruct((128, 512), f32), jax.ShapeDtypeStruct((512, 128), f32),
            jax.ShapeDtypeStruct((128, 128), f32), jax.ShapeDtypeStruct((4, 16, 16), f32),
        ],
        in_specs=[pair, pair, pair] + [whole(v.shape) for v in (bias, types, g3, wat, wa, wo, wot, hot_t)],
        out_specs=[pair, pair, whole((128, 512)), whole((512, 128)), whole((128, 128)), whole((4, 16, 16))],
        scratch_shapes=[VM((128, 512), f32)],
        compiler_params=pltpu.CompilerParams(
            dimension_semantics=("arbitrary",), vmem_limit_bytes=48 << 20),
        name="attention",
    )(mid, cot, alive, bias, types, g3, wat, wa, wo, wot, hot_t)


def backward_kernel(slab, live, cot, mid, dn3, d_bias, prod, right, g1, g2, g3, w1t, w1, woutt, wout, wb,
                    grad, d_w1, d_wout, d_wb, d_gain,
                    db_n, db_in, db_f, normed, pieces, left_f, d_prod, d_mid, d_gate, part, right_f, work,
                    far, far_in, sent, cross_in, near, near_in, gain_sum,
                    sem_bs, sem_br, sem_s, sem_r):
    bf, f32 = jnp.bfloat16, jnp.float32
    a, partner, cross, chip = places()
    core = lax.rem(a, 2)
    barrier = greet_dap(a)
    unit = eye()

    for h in range(4):
        db_n[h] = flip(unit, d_bias[:, 128 * h : 128 * h + 128].astype(bf)).astype(bf)
    pl.semaphore_wait(barrier, 3)

    def share(r):
        peer = lax.rem(a + r, 4)
        return pltpu.make_async_remote_copy(
            src_ref=db_n.at[:, at(peer, 32), :], dst_ref=db_in.at[r - 1], send_sem=sem_bs.at[r - 1],
            recv_sem=sem_br.at[r - 1], device_id={"dap": peer}, device_id_type=MESH)

    for r in (2, 1, 3):
        share(r).start()

    def pair(ref, i):
        return jnp.concatenate([ref[i], ref[i + 1]], axis=1)

    def flipped(ref, i):
        return jnp.concatenate([flip(unit, ref[i]), flip(unit, ref[i + 1])], axis=1)

    def alive_of(i):
        return jnp.concatenate([live[pl.ds(i, 1), :], live[pl.ds(i + 1, 1), :]], axis=1)

    def project(t):
        i = 2 * t
        hat, _ = norm_cols(flipped(slab, i))
        n = (hat * wide(g1[...], 256)).astype(bf)
        p = mm(w1t[...], n)
        sa = jax.nn.sigmoid(p[128:256])
        sb = jax.nn.sigmoid(p[512:])
        gate = jax.nn.sigmoid(p[256:384])
        lft = (sa * p[:128] * alive_of(i)).astype(bf).astype(f32)
        for r in range(2):
            lane = slice(128 * r, 128 * r + 128)
            normed[i + r] = n[:, lane]
            left_f[at(i + r, 128), :] = lft[:, lane]
            pieces[i + r, 0:128] = p[:128, lane]
            pieces[i + r, 128:256] = sa[:, lane]
            pieces[i + r, 256:384] = p[384:512, lane]
            pieces[i + r, 384:512] = sb[:, lane]
            part[i + r] = gate[:, lane]

    loop(16, project)

    for r in (1, 2, 3):
        share(r).wait_recv()
    total = db_n[:, at(a, 32), :].astype(f32)
    for r in range(3):
        total = total + db_in[r].astype(f32)
    db_f[...] = total
    d_w1[...] = jnp.zeros_like(d_w1)
    d_wout[...] = jnp.zeros_like(d_wout)
    d_wb[...] = jnp.zeros_like(d_wb)
    gain_sum[...] = jnp.zeros_like(gain_sum)

    def fold(x):
        return x[:, :128] + x[:, 128:]

    def second(t):
        i = 2 * t
        hat3, scale3 = norm_cols(pair(mid, i).astype(f32))
        gain3, gain2 = wide(g3[...], 256), wide(g2[...], 256)
        n3 = (hat3 * gain3).astype(bf)
        rows = [
            jnp.concatenate([db_f[h, pl.ds(i, 1), :], db_f[h, pl.ds(i + 1, 1), :]], axis=1) for h in range(4)
        ]
        db = jnp.concatenate(rows + [jnp.zeros((12, 256), f32)], axis=0).astype(bf)
        dn = pair(dn3, i).astype(f32) + mm(wb[...], db)
        d_wb[...] += nt(db, n3)
        gain_sum[2] += fold(dn * hat3)
        dm = flipped(cot, i).astype(bf) + norm_back(dn * gain3, hat3, scale3).astype(bf)
        dmf = dm.astype(f32)
        x = jnp.concatenate([prod[pl.ds(i, 128, stride=32), :], prod[pl.ds(i + 1, 128, stride=32), :]], axis=1)
        hat2, scale2 = norm_cols(x)
        n2 = (hat2 * gain2).astype(bf)
        z = mm(woutt[...], n2)
        gate = pair(part, i)
        dz = (dmf * gate).astype(bf)
        d_open = (dmf * z * gate * (1.0 - gate)).astype(bf)
        d_wout[...] += nt(n2, dz)
        dn2 = mm(wout[...], dz).astype(bf).astype(f32)
        gain_sum[1] += fold(dn2 * hat2)
        dp = norm_back(dn2 * gain2, hat2, scale2)
        for r in range(2):
            lane = slice(128 * r, 128 * r + 128)
            d_prod[pl.ds(i + r, 128, stride=32), :] = pltpu.roll(dp[:, lane], 64 * chip, axis=1)
            d_mid[i + r] = dm[:, lane]
            d_gate[i + r] = d_open[:, lane]

    loop(16, second)

    def chunk(ref, q):
        return ref.at[:, at(q, 32), :]

    def move(kind, q):
        src, dst, peer = (
            (far.at[1 - core], far_in, partner), (sent, cross_in, cross), (near.at[1 - core], near_in, partner),
        )[kind]
        return pltpu.make_async_remote_copy(
            src_ref=chunk(src, q), dst_ref=chunk(dst, q), send_sem=sem_s.at[kind, q], recv_sem=sem_r.at[kind, q],
            device_id={"dap": peer}, device_id_type=MESH)

    def right_grads(half, q, store):
        def one(c):
            ch = 32 * q + c
            dp = d_prod[at(ch, 32), 64 * half : 64 * half + 64].astype(bf)
            work[pl.ds(c, 64, stride=32), :] = tn(dp, left_f[pl.ds(ch, 32, stride=128), :].astype(bf))

        loop(32, one, 4)

        def pack(j):
            store[j // 32, lax.rem(j, 32), at(q, 32), :] = work[at(j, 32), :].astype(bf)

        loop(64, pack, 4)

    def add_on(q):
        move(0, q).wait_recv()

        def one(j):
            spot = at(q, 32)
            sent[j, spot, :] = (far[core, j, spot, :].astype(f32) + far_in[j, spot, :].astype(f32)).astype(bf)

        loop(32, one, 4)
        move(1, q).start()

    def out_far(q):
        right_grads(1, q, far)
        move(0, q).start()
        pl.when(q > 0)(lambda: add_on(q - 1))

    loop(4, out_far)

    def out_near(q):
        right_grads(0, q, near)
        move(2, q).start()
        pl.when(q == 0)(lambda: add_on(3))

    loop(4, out_near)

    def unpack(block, base):
        loop(32, lambda j: right_f.__setitem__((at(base + j, 128), slice(None)), right[block, j].astype(f32)), 2)

    low = 2 * chip
    unpack(low, 0)
    unpack(low + 1, 32)
    unpack(2 - low, 64)
    unpack(3 - low, 96)

    def left_grad(ch):
        rgt = right_f[pl.ds(ch, 128, stride=128), :].astype(bf)
        left_f[pl.ds(ch, 32, stride=128), :] = mm(d_prod[at(ch, 32), :].astype(bf), rgt)

    loop(128, left_grad, 4)

    def sides(grad_in, p, s, alive):
        g = grad_in * alive * s
        return g, g * p * (1.0 - s)

    def left_part(t):
        i = 2 * t
        dl = jnp.concatenate([left_f[at(i, 128), :], left_f[at(i + 1, 128), :]], axis=1).astype(bf).astype(f32)
        p = jnp.concatenate([pieces[i, 0:128], pieces[i + 1, 0:128]], axis=1)
        s = jnp.concatenate([pieces[i, 128:256], pieces[i + 1, 128:256]], axis=1)
        dpa, dga = sides(dl, p, s, alive_of(i))
        dp = jnp.concatenate([dpa.astype(bf), dga.astype(bf), pair(d_gate, i)], axis=0)
        d_w1[0:384, :] += nt(dp, pair(normed, i))
        dn = mm(w1[:, 0:384], dp)
        part[i] = dn[:, :128]
        part[i + 1] = dn[:, 128:]

    loop(16, left_part)

    loop(4, lambda q: move(2, q).wait_recv())
    loop(4, lambda q: move(1, q).wait_recv())

    def right_part(t):
        i = 2 * t

        def summed(j):
            v = near[core, j].astype(f32) + near_in[j].astype(f32) + cross_in[j].astype(f32)
            return v.astype(bf).astype(f32)

        dr = jnp.concatenate([summed(i), summed(i + 1)], axis=1)
        p = jnp.concatenate([pieces[i, 256:384], pieces[i + 1, 256:384]], axis=1)
        s = jnp.concatenate([pieces[i, 384:512], pieces[i + 1, 384:512]], axis=1)
        dpb, dgb = sides(dr, p, s, alive_of(i))
        dp = jnp.concatenate([dpb.astype(bf), dgb.astype(bf)], axis=0)
        d_w1[384:640, :] += nt(dp, pair(normed, i))
        dn = (pair(part, i) + mm(w1[:, 384:640], dp)).astype(bf).astype(f32)
        hat, scale = norm_cols(flipped(slab, i))
        gain_sum[0] += fold(dn * hat)
        dx = norm_back(dn * wide(g1[...], 256), hat, scale).astype(bf)
        res = pair(d_mid, i) + dx
        grad[i] = flip(unit, res[:, :128]).astype(bf)
        grad[i + 1] = flip(unit, res[:, 128:]).astype(bf)

    loop(16, right_part)
    ones = jnp.ones((8, 128), f32)
    for k in range(3):
        d_gain[k] = lax.dot_general(
            ones, gain_sum[k], (((1,), (1,)), ((), ())), precision=lax.Precision.HIGHEST,
            preferred_element_type=f32)
    for r in (1, 2, 3):
        share(r).wait_send()
    for kind in range(3):
        loop(4, lambda q: move(kind, q).wait_send())


def backward(*args):
    bf, f32 = jnp.bfloat16, jnp.float32
    block = (32, 128, 128)
    return pl.pallas_call(
        backward_kernel,
        out_shape=[
            jax.ShapeDtypeStruct(block, bf), jax.ShapeDtypeStruct((640, 128), f32),
            jax.ShapeDtypeStruct((128, 128), f32), jax.ShapeDtypeStruct((16, 128), f32),
            jax.ShapeDtypeStruct((3, 8, 128), f32),
        ],
        in_specs=[SPEC] * len(args), out_specs=[SPEC] * 5,
        scratch_shapes=[
            VM((4, 128, 128), bf), VM((3, 4, 32, 128), bf), VM((4, 32, 128), f32), VM(block, bf),
            VM((32, 512, 128), f32), VM((4096, 128), f32), VM((4096, 128), f32), VM(block, bf), VM(block, bf),
            VM(block, f32), VM((16384, 128), f32), VM((2048, 128), f32),
            VM((2,) + block, bf), VM(block, bf), VM(block, bf), VM(block, bf), VM((2,) + block, bf), VM(block, bf),
            VM((3, 128, 128), f32), DMA((3,)), DMA((3,)), DMA((3, 4)), DMA((3, 4)),
        ],
        compiler_params=pltpu.CompilerParams(collective_id=2, has_side_effects=True, vmem_limit_bytes=60 << 20),
        name="triangle_backward",
    )(*args)


def reduce_kernel(n_dp, factor, d_w1, d_wout, d_wa, d_wo, small,
                  o_tri_in, o_tri_gate, o_tri_out, o_att_in, o_att_out, o_small,
                  g, part, quarter, pieces, mine, joined, full, sa, ra, sb, rb, sc, rc, sd, rd):
    a = lax.axis_index("dap")
    p = lax.axis_index("dp")
    rows = quarter.shape[0]
    piece = rows // n_dp

    def greet_dp(r, carry):
        pl.semaphore_signal(barrier, inc=1, device_id={"dp": lax.rem(p + r, n_dp)}, device_id_type=MESH)
        return carry

    barrier = pltpu.get_barrier_semaphore()
    for r in range(1, 4):
        pl.semaphore_signal(barrier, inc=1, device_id={"dap": lax.rem(a + r, 4)}, device_id_type=MESH)
    lax.fori_loop(1, n_dp, greet_dp, 0)
    bf, f32 = jnp.bfloat16, jnp.float32
    g[0:640, :] = d_w1[...].astype(bf)
    g[640:1152, :] = d_wa[...].astype(bf)
    g[1152:1280, :] = d_wout[...].astype(bf)
    g[1280:1408, :] = d_wo[...].astype(bf)
    g[1408:1424, :] = small[...].astype(bf)
    g[1424:, :] = jnp.zeros((4 * rows - 1424, 128), bf)
    pl.semaphore_wait(barrier, 3 + n_dp - 1)

    def copy_a(r):
        peer = lax.rem(a + r, 4)
        return pltpu.make_async_remote_copy(
            src_ref=g.at[pl.ds(pl.multiple_of(peer * rows, rows), rows)], dst_ref=part.at[r - 1],
            send_sem=sa.at[r - 1], recv_sem=ra.at[r - 1], device_id={"dap": peer}, device_id_type=MESH)

    for r in (2, 1, 3):
        copy_a(r).start()
    for r in (1, 2, 3):
        copy_a(r).wait_recv()
    total = g[pl.ds(pl.multiple_of(a * rows, rows), rows), :].astype(jnp.float32)
    for r in range(3):
        total = total + part[r].astype(jnp.float32)
    quarter[...] = total.astype(jnp.bfloat16)

    def copy_b(r):
        peer = lax.rem(p + r, n_dp)
        return pltpu.make_async_remote_copy(
            src_ref=quarter.at[pl.ds(pl.multiple_of(peer * piece, piece), piece)], dst_ref=pieces.at[r - 1],
            send_sem=sb.at[r - 1], recv_sem=rb.at[r - 1], device_id={"dp": peer}, device_id_type=MESH)

    def each(fn):
        def body(r, carry):
            fn(r)
            return carry
        lax.fori_loop(1, n_dp, body, 0)

    each(lambda r: copy_b(r).start())
    each(lambda r: copy_b(r).wait_recv())
    own = pl.ds(pl.multiple_of(p * piece, piece), piece)
    total = quarter[own, :].astype(jnp.float32) + jnp.sum(pieces[...].astype(jnp.float32), axis=0)
    mine[...] = (total * factor).astype(jnp.bfloat16)

    def copy_c(r):
        peer = lax.rem(p + r, n_dp)
        return pltpu.make_async_remote_copy(
            src_ref=mine, dst_ref=joined.at[own],
            send_sem=sc.at[r - 1], recv_sem=rc.at[r - 1], device_id={"dp": peer}, device_id_type=MESH)

    each(lambda r: copy_c(r).start())
    joined[own, :] = mine[...]

    def wait_c(r):
        src = lax.rem(p + n_dp - r, n_dp)
        pltpu.make_async_remote_copy(
            src_ref=mine, dst_ref=joined.at[pl.ds(pl.multiple_of(src * piece, piece), piece)],
            send_sem=sc.at[r - 1], recv_sem=rc.at[r - 1], device_id={"dp": p}, device_id_type=MESH).wait_recv()

    each(wait_c)

    def copy_d(k):
        block = (a, a, lax.rem(a + 2, 4))[k]
        target = (lax.rem(a + 2, 4), a + 1 - 2 * lax.rem(a, 2), a + 1 - 2 * lax.rem(a, 2))[k]
        there = pl.ds(pl.multiple_of(block * rows, rows), rows)
        return pltpu.make_async_remote_copy(
            src_ref=joined if k < 2 else full.at[there], dst_ref=full.at[there],
            send_sem=sd.at[k], recv_sem=rd.at[k], device_id={"dap": target}, device_id_type=MESH)

    copy_d(0).start()
    copy_d(1).start()
    full[pl.ds(pl.multiple_of(a * rows, rows), rows), :] = joined[...]
    copy_d(0).wait_recv()
    copy_d(2).start()
    copy_d(1).wait_recv()
    copy_d(2).wait_recv()
    unit = eye()

    def block(b):
        return full[b * 128 : (b + 1) * 128, :]

    for b, source in enumerate((0, 1, 3, 4)):
        o_tri_in[:, b * 128 : (b + 1) * 128] = flip(unit, block(source))
        o_att_in[:, b * 128 : (b + 1) * 128] = flip(unit, block(5 + b))
    o_tri_gate[...] = flip(unit, block(2))
    o_tri_out[...] = block(9).astype(f32)
    o_att_out[...] = block(10).astype(f32)
    o_small[...] = full[1408:1424, :].astype(f32)
    for r in (1, 2, 3):
        copy_a(r).wait_send()
    each(lambda r: copy_b(r).wait_send())
    each(lambda r: copy_c(r).wait_send())
    for k in range(3):
        copy_d(k).wait_send()


def reduce_all(n_dp, factor, *grads):
    rows = 16 * n_dp
    f32, bf = jnp.float32, jnp.bfloat16
    shapes = ((128, 512), (128, 128), (128, 128), (128, 512), (128, 128), (16, 128))
    return pl.pallas_call(
        partial(reduce_kernel, n_dp, factor),
        out_shape=[jax.ShapeDtypeStruct(s, f32) for s in shapes],
        in_specs=[SPEC] * 5,
        out_specs=[SPEC] * 6,
        scratch_shapes=[
            VM((4 * rows, 128), bf), VM((3, rows, 128), bf), VM((rows, 128), bf), VM((n_dp - 1, 16, 128), bf),
            VM((16, 128), bf), VM((rows, 128), bf), VM((4 * rows, 128), bf),
        ] + [pltpu.SemaphoreType.DMA((3,))] * 2 + [pltpu.SemaphoreType.DMA((n_dp - 1,))] * 4
          + [pltpu.SemaphoreType.DMA((3,))] * 2,
        compiler_params=pltpu.CompilerParams(collective_id=0, has_side_effects=True, vmem_limit_bytes=32 << 20),
        name="gradient_sum",
    )(*grads)


def per_device(
    pair_rep,
    cotangent,
    tok_mask,
    tok_types,
    pair_mask,
    triangle_gain,
    triangle_input,
    triangle_gating,
    product_gain,
    triangle_output,
    attend_gain,
    attend_bias,
    attend_input,
    attend_output,
    type_table,
):
    bf, f32 = jnp.bfloat16, jnp.float32
    slab = pair_rep[0]
    cot = cotangent[0]
    row_count, length, channels = slab.shape
    tokens = tok_mask[0].astype(f32)
    first_row = lax.axis_index("dap") * row_count
    row_tokens = lax.dynamic_slice_in_dim(tokens, first_row, row_count)
    live = pair_mask[0].astype(f32) * row_tokens[:, None] * tokens[None, :]
    alive = jnp.broadcast_to(live.astype(bf)[:, :, None], (row_count, length, 128))
    kinds = jnp.arange(16, dtype=jnp.int32)
    hot_t = (tok_types[0][None, :] == kinds[:, None]).astype(f32)
    table = jnp.pad(type_table, ((0, 0), (0, 12), (0, 12)))
    types = jnp.einsum("bk,hab,aj->hkj", hot_t, table, hot_t, precision=lax.Precision.HIGHEST)

    def column(gain):
        return jnp.broadcast_to(gain[:, None], (channels, 128))

    g1, g2, g3 = column(triangle_gain), column(product_gain), column(attend_gain)
    w1 = jnp.concatenate([triangle_input[:, :256], triangle_gating, triangle_input[:, 256:]], axis=1)
    w1t = w1.T
    wbt = jnp.pad(attend_bias, ((0, 0), (0, 12))).T
    wb = wbt.T
    woutt = triangle_output.T
    mid, prod, right, bias = forward(slab, live, g1, g2, g3, w1t, woutt, wbt)
    out, dn3, d_bias, d_wa, d_wo, d_table = attend(
        mid, cot, alive, bias, types, g3, attend_input.T, attend_input, attend_output, attend_output.T,
        hot_t.astype(bf))
    grad, d_w1, d_wout, d_wb, d_gain = backward(
        slab, live, cot, mid, dn3, d_bias, prod, right, g1, g2, g3, w1t, w1, woutt, triangle_output, wb)
    factor = (length * length * lax.axis_size("dp")) ** (-0.5)
    small = jnp.concatenate(
        [
            d_gain[:, 0],
            d_wb[:4],
            jnp.pad(d_table[:, :4, :4].reshape(1, 64), ((0, 0), (0, 64))),
            jnp.zeros((8, 128), f32),
        ]
    )
    g_in, g_gate, g_out, g_att_in, g_att_out, g_small = reduce_all(
        lax.axis_size("dp"), factor, d_w1, d_wout, d_wa, d_wo, small)
    return (
        out[None],
        grad[None],
        g_small[0],
        g_in,
        g_gate,
        g_small[1],
        g_out,
        g_small[2],
        g_small[3:7].T,
        g_att_in,
        g_att_out,
        g_small[7, :64].reshape(type_table.shape),
    )


def solution(mesh):
    return jax.shard_map(
        per_device,
        mesh=mesh,
        in_specs=(
            P("dp", "dap", None, None),
            P("dp", "dap", None, None),
            P("dp", None),
            P("dp", None),
            P("dp", "dap", None),
            P(),
            P(),
            P(),
            P(),
            P(),
            P(),
            P(),
            P(),
            P(),
            P(),
        ),
        out_specs=(
            P("dp", "dap", None, None),
            P("dp", "dap", None, None),
            P(),
            P(),
            P(),
            P(),
            P(),
            P(),
            P(),
            P(),
            P(),
            P(),
        ),
        check_vma=False,
    )
```

```python
from functools import partial

import jax
import jax.numpy as jnp
from jax import lax
from jax.experimental import pallas as pl
from jax.experimental.pallas import tpu as pltpu
from jax.sharding import PartitionSpec as P

EPSILON = 1e-05
MESH = pl.DeviceIdType.MESH
VM = pltpu.VMEM
DMA = pltpu.SemaphoreType.DMA
BF = jnp.bfloat16
F32 = jnp.float32
EXACT = lax.Precision.HIGHEST


def contract(x, y, dims, precision=None):
    return lax.dot_general(x, y, (dims, ((), ())), precision=precision, preferred_element_type=F32)


def mm(x, y, precision=None):
    return contract(x, y, ((1,), (0,)), precision)


def nt(x, y, precision=None):
    return contract(x, y, ((1,), (1,)), precision)


def tn(x, y, precision=None):
    return contract(x, y, ((0,), (0,)), precision)


def norm_cols(x):
    mean = jnp.sum(x, axis=0, keepdims=True) * (1.0 / 128)
    centred = x - mean
    spread = jnp.sum(centred * centred, axis=0, keepdims=True) * (1.0 / 128)
    scale = lax.rsqrt(spread + EPSILON)
    return centred * scale, scale


def norm_back(grad, unit, scale):
    a = jnp.sum(grad, axis=0, keepdims=True) * (1.0 / 128)
    b = jnp.sum(grad * unit, axis=0, keepdims=True) * (1.0 / 128)
    return scale * (grad - a - unit * b)


def loop(n, fn, unroll=1, first=0):
    def body(i, carry):
        fn(i)
        return carry
    lax.fori_loop(first, n, body, 0, unroll=unroll)


def at(i, size):
    return pl.ds(pl.multiple_of(i * size, size), size)


def halves(x):
    return x[:, :128], x[:, 128:]


def twice(x):
    return jnp.concatenate([x, x], axis=1)


def pair(ref, i):
    return jnp.concatenate([ref[i], ref[i + 1]], axis=1)


def lanes(r):
    return slice(128 * r, 128 * r + 128)


class Sum:
    def __init__(self, n_dp, factor, a, p, refs):
        self.n_dp, self.factor, self.a, self.p = n_dp, factor, a, p
        self.partner, self.cross = a + 1 - 2 * lax.rem(a, 2), lax.rem(a + 2, 4)
        (self.g, self.part, self.quarter, self.pieces, self.mine, self.joined, self.joined_b, self.full,
         self.sa, self.ra, self.sb, self.rb, self.sc, self.rc, self.sd, self.rd) = refs
        self.size = 256 // n_dp

    def remote(self, src, dst, s, r, **peer):
        return pltpu.make_async_remote_copy(
            src_ref=src, dst_ref=dst, send_sem=s, recv_sem=r, device_id=peer, device_id_type=MESH)

    def copy_a(self, r):
        peer = lax.rem(self.a + r, 4)
        return self.remote(self.g.at[at(peer, 256)], self.part.at[r - 1], self.sa.at[r - 1], self.ra.at[r - 1], dap=peer)

    def copy_b(self, r):
        peer = lax.rem(self.p + r, self.n_dp)
        return self.remote(
            self.quarter.at[at(peer, self.size)], self.pieces.at[r - 1], self.sb.at[r - 1], self.rb.at[r - 1], dp=peer)

    def copy_c(self, r, sending=True):
        peer = lax.rem(self.p + r, self.n_dp)
        owner = self.p if sending else lax.rem(self.p + self.n_dp - r, self.n_dp)
        return self.remote(
            self.mine, self.joined.at[at(owner, self.size)], self.sc.at[r - 1], self.rc.at[r - 1], dp=peer)

    def copy_d(self, k):
        there = at(self.cross if k == 2 else self.a, 256)
        src = self.full.at[there] if k == 2 else self.joined_b
        return self.remote(
            src, self.full.at[there], self.sd.at[k], self.rd.at[k], dap=self.cross if k == 0 else self.partner)

    def start_a(self):
        for r in (2, 1, 3):
            self.copy_a(r).start()

    def start_b(self):
        total = self.g[at(self.a, 256), :].astype(F32)
        for r in (1, 2, 3):
            self.copy_a(r).wait_recv()
            total = total + self.part[r - 1].astype(F32)
        self.quarter[...] = total
        loop(self.n_dp, lambda r: self.copy_b(r).start(), first=1)

    def start_c(self):
        loop(self.n_dp, lambda r: self.copy_b(r).wait_recv(), first=1)
        total = self.quarter[at(self.p, self.size), :] + jnp.sum(self.pieces[...], axis=0)
        self.mine[...] = total * self.factor
        loop(self.n_dp, lambda r: self.copy_c(r).start(), first=1)
        self.joined[at(self.p, self.size), :] = self.mine[...]

    def start_d(self):
        loop(self.n_dp, lambda r: self.copy_c(r, False).wait_recv(), first=1)
        self.joined_b[...] = self.joined[...].astype(BF)
        self.copy_d(0).start()
        self.copy_d(1).start()
        self.full[at(self.a, 256), :] = self.joined_b[...]

    def finish(self):
        self.copy_d(0).wait_recv()
        self.copy_d(2).start()
        self.copy_d(1).wait_recv()
        self.copy_d(2).wait_recv()

    def settle(self):
        for r in (1, 2, 3):
            self.copy_a(r).wait_send()
        loop(self.n_dp, lambda r: self.copy_b(r).wait_send(), first=1)
        loop(self.n_dp, lambda r: self.copy_c(r).wait_send(), first=1)
        for k in range(3):
            self.copy_d(k).wait_send()

    @staticmethod
    def scratch(n_dp):
        size = 256 // n_dp
        return [
            VM((1024, 128), BF), VM((3, 256, 128), BF), VM((256, 128), F32), VM((n_dp - 1, size, 128), F32),
            VM((size, 128), F32), VM((256, 128), F32), VM((256, 128), BF), VM((1024, 128), BF),
        ] + [DMA((3,))] * 2 + [DMA((n_dp - 1,))] * 4 + [DMA((3,))] * 2


N_IN, N_OUT, N_SUM = 15, 12, 16


def kernel(n_dp, factor, *refs):
    (slab, cot, tok_mask, tok_types, pair_mask, gain1, tri_in, tri_gate, gain2, tri_out, gain3, att_bias, att_in,
     att_out, table) = refs[:N_IN]
    (out, grad, o_gain1, o_tri_in, o_tri_gate, o_gain2, o_tri_out, o_gain3, o_att_bias, o_att_in, o_att_out,
     o_table) = refs[N_IN : N_IN + N_OUT]
    rest = refs[N_IN + N_OUT :]
    a, p = lax.axis_index("dap"), lax.axis_index("dp")
    partner, cross, chip, core = a + 1 - 2 * lax.rem(a, 2), lax.rem(a + 2, 4), a // 2, lax.rem(a, 2)
    early = Sum(n_dp, factor, a, p, rest[:N_SUM])
    late = Sum(n_dp, factor, a, p, rest[N_SUM : 2 * N_SUM])
    (live, live_t, tok_t, g1, g2, g3, w1, w1t, wat, wot, woutt, wb, wbt, hot, tab, bt,
     mid, dn3, prod, right, left_f, right_f, gates, pieces, normed, bias_f, bias_b, bias,
     d_bias, d_wa, d_wo, d_wout, d_wb, d_w1, gain_sum,
     db_n, db_in, db_f, d_prod, d_mid, d_gate, work, far, far_in, sent, cross_in, near, near_in,
     sem_es, sem_er, sem_is, sem_ir, sem_bs, sem_br, sem_s, sem_r) = rest[2 * N_SUM :]
    part = gates

    barrier = pltpu.get_barrier_semaphore()
    for r in range(1, 4):
        pl.semaphore_signal(barrier, inc=1, device_id={"dap": lax.rem(a + r, 4)}, device_id_type=MESH)
    loop(n_dp, lambda r: pl.semaphore_signal(
        barrier, inc=1, device_id={"dp": lax.rem(p + r, n_dp)}, device_id_type=MESH), first=1)

    rows_i = lax.broadcasted_iota(jnp.int32, (128, 128), 0)
    unit = (rows_i == lax.broadcasted_iota(jnp.int32, (128, 128), 1)).astype(F32).astype(BF)

    def flip(block):
        return nt(unit, block)

    def flipped(ref, i):
        return jnp.concatenate([flip(ref[i]), flip(ref[i + 1])], axis=1)

    def column(row):
        return jnp.broadcast_to(row, (128, 128)).T

    tokens = tok_mask[...].astype(F32)
    tok_t[...] = column(tokens)
    live[...] = pair_mask[...].astype(F32) * tok_t[at(a, 32), :] * tokens
    live_t[...] = tn(live[...].astype(BF), unit[:32, :32]).astype(BF)
    for gain, row in ((g1, gain1), (g2, gain2), (g3, gain3)):
        gain[...] = column(row[...])
    w1[:, 0:256] = tri_in[:, 0:256]
    w1[:, 256:384] = tri_gate[...]
    w1[:, 384:640] = tri_in[:, 256:512]
    for b in range(5):
        w1t[128 * b : 128 * b + 128, :] = flip(w1[:, lanes(b)]).astype(BF)
    for b in range(4):
        wat[128 * b : 128 * b + 128, :] = flip(att_in[:, lanes(b)]).astype(BF)
    wot[...] = flip(att_out[...]).astype(BF)
    woutt[...] = flip(tri_out[...]).astype(BF)
    wb[...] = jnp.zeros_like(wb)
    wb[:, 0:4] = att_bias[...]
    wbt[...] = tn(wb[...], unit).astype(BF)
    tab[...] = jnp.zeros_like(tab)
    tab[:, 0:4, 0:4] = table[...]
    hot[...] = (lax.broadcasted_iota(jnp.int32, (16, 128), 0) == tok_types[...]).astype(F32)

    def alive_of(i):
        return jnp.concatenate([live[pl.ds(i, 1), :], live[pl.ds(i + 1, 1), :]], axis=1)


    def edge(kind, c):
        spot = right.at[cross if kind == 2 else a, at(c, 8)]
        return pltpu.make_async_remote_copy(
            src_ref=spot, dst_ref=spot, send_sem=sem_es.at[kind, c], recv_sem=sem_er.at[kind, c],
            device_id={"dap": cross if kind == 1 else partner}, device_id_type=MESH)

    def project(c, t):
        i = c * 8 + 2 * t
        hat, _ = norm_cols(flipped(slab, i))
        n = (hat * twice(g1[...])).astype(BF)
        q = mm(w1t[...], n)
        alive = alive_of(i)
        sa, sb = jax.nn.sigmoid(q[128:256]), jax.nn.sigmoid(q[512:])
        lft = (sa * q[:128] * alive).astype(BF).astype(F32)
        rgt = (sb * q[384:512] * alive).astype(BF)
        gate = jax.nn.sigmoid(q[256:384])
        for r in range(2):
            normed[i + r] = n[:, lanes(r)]
            left_f[at(i + r, 128), :] = lft[:, lanes(r)]
            right[a, i + r] = rgt[:, lanes(r)]
            gates[i + r] = gate[:, lanes(r)]
            pieces[i + r, 0:128] = q[:128, lanes(r)]
            pieces[i + r, 128:256] = sa[:, lanes(r)]
            pieces[i + r, 256:384] = q[384:512, lanes(r)]
            pieces[i + r, 384:512] = sb[:, lanes(r)]

    def first(c):
        loop(4, lambda t: project(c, t))
        pl.when(c == 0)(lambda: pl.semaphore_wait(barrier, 3 + n_dp - 1))
        edge(1, c).start()
        edge(0, c).start()

    loop(4, first)

    def unpack(block, base):
        loop(32, lambda j: right_f.__setitem__((at(base + j, 128), slice(None)), right[block, j].astype(F32)), 2)

    def multiply(half):
        def one(ch):
            lft = left_f[pl.ds(ch, 32, stride=128), :].astype(BF)
            rgt = right_f[pl.ds(64 * 128 * half + ch, 64, stride=128), :].astype(BF)
            prod[at(ch, 32), 64 * half : 64 * half + 64] = nt(lft, rgt)
        loop(128, one, 4)

    loop(4, lambda c: edge(0, c).wait_recv())
    low = 2 * chip
    unpack(low, 0)
    unpack(low + 1, 32)
    multiply(0)

    def relay(c):
        edge(1, c).wait_recv()
        edge(2, c).start()

    loop(4, relay)
    loop(4, lambda c: edge(2, c).wait_recv())
    unpack(2 - low, 64)
    unpack(3 - low, 96)
    multiply(1)

    def second(t):
        i = 2 * t
        xs = []
        for r in range(2):
            rows = pl.ds(i + r, 128, stride=32)
            x = pltpu.roll(prod[rows, :], 64 * chip, axis=1)
            prod[rows, :] = x
            xs.append(x)
        hat, _ = norm_cols(jnp.concatenate(xs, axis=1))
        n = (hat * twice(g2[...])).astype(BF)
        middle = (flipped(slab, i) + pair(gates, i) * mm(woutt[...], n)).astype(BF)
        hat, _ = norm_cols(middle.astype(F32))
        n = (hat * twice(g3[...])).astype(BF)
        heads = mm(wbt[...], n)
        for r in range(2):
            mid[i + r] = middle[:, lanes(r)]
            for h in range(4):
                bias_f[h, pl.ds(i + r, 1), :] = heads[h : h + 1, lanes(r)]

    loop(16, second)
    bias_b[...] = bias_f[...].astype(BF)

    def share_bias(r):
        return pltpu.make_async_remote_copy(
            src_ref=bias_b, dst_ref=bias.at[:, at(a, 32), :], send_sem=sem_is.at[r - 1], recv_sem=sem_ir.at[r - 1],
            device_id={"dap": lax.rem(a + r, 4)}, device_id_type=MESH)

    for r in (2, 1, 3):
        share_bias(r).start()
    bias[:, at(a, 32), :] = bias_b[...]
    for h in range(4):
        near_types = mm(tab[h].T, hot[...], EXACT)
        bt[:, lanes(h)] = tn(hot[...], near_types, EXACT)
    for ref in (d_bias, d_wa, d_wo, d_wout, d_wb, d_w1, gain_sum):
        ref[...] = jnp.zeros_like(ref)
    for r in (1, 2, 3):
        share_bias(r).wait_recv()
    for h in range(4):
        bt[:, lanes(h)] += flip(bias[h])


    def spread(x):
        zero = jnp.zeros((32, 128), x.dtype)
        cols = [
            jnp.concatenate([x[32 * h : 32 * h + 32] if g == h else zero for g in range(4)], axis=0)
            for h in range(4)
        ]
        return jnp.concatenate(cols, axis=1)

    scale = 32.0 ** -0.5

    def attend(t):
        i = 2 * t
        m = pair(mid, i).astype(F32)
        hat, _ = norm_cols(m)
        n = (hat * twice(g3[...])).astype(BF)
        q3 = mm(wat[...], n)
        qkv = q3[:384].astype(BF)
        gate = jax.nn.sigmoid(q3[384:])
        ct = flipped(cot, i).astype(BF)
        d_gated = mm(att_out[...], ct).astype(BF).astype(F32)
        d_att = d_gated * gate
        picked = lax.broadcasted_iota(jnp.int32, (32, 256), 0) == (
            i + lax.broadcasted_iota(jnp.int32, (32, 256), 1) // 128)
        alive = mm(live_t[...], picked.astype(F32).astype(BF))
        parts, atts = [], []
        for r in range(2):
            q, k, v = (qkv[128 * x : 128 * x + 128, lanes(r)] for x in range(3))
            kv = flip(qkv[128:384, lanes(r)]).astype(BF)
            q4 = spread(q)
            e = jnp.exp(mm(kv[:, :128], q4) * scale + bt[...])
            e = e * jnp.concatenate([alive[:, lanes(r)]] * 4, axis=1)
            s = jnp.sum(e, axis=0, keepdims=True)
            w = e * (1.0 / jnp.maximum(s, 1.0))
            ab = w.astype(BF)
            atts.append(jnp.concatenate([mm(v[32 * h : 32 * h + 32], ab[:, lanes(h)]) for h in range(4)], axis=0))
            do4 = spread(d_att[:, lanes(r)].astype(BF))
            da = mm(kv[:, 128:], do4).astype(BF).astype(F32)
            u = da * w
            total = jnp.sum(u, axis=0, keepdims=True)
            total = jnp.where(s > 1.0, total, jnp.where(s == 1.0, 0.5 * total, 0.0))
            ds = u - w * total
            d_bias[...] += ds
            dsb = ds.astype(BF)
            dv = nt(do4, ab)
            dk = nt(q4, dsb) * scale
            dq = jnp.concatenate(
                [mm(k[32 * h : 32 * h + 32], dsb[:, lanes(h)]) for h in range(4)], axis=0) * scale
            parts.append(jnp.concatenate([dq, dk, dv], axis=0).astype(BF))
        att = jnp.concatenate(atts, axis=1)
        d_open = (d_gated * att * gate * (1.0 - gate)).astype(BF)
        dp = jnp.concatenate([jnp.concatenate(parts, axis=1), d_open], axis=0)
        dn = mm(att_in[...], dp).astype(BF)
        d_wa[...] += nt(dp, n)
        gated = (gate * att).astype(BF)
        d_wo[...] += nt(gated, ct)
        res = (m + mm(wot[...], gated)).astype(BF)
        for r in range(2):
            dn3[i + r] = dn[:, lanes(r)]
            out[i + r] = flip(res[:, lanes(r)]).astype(BF)

    loop(16, attend)

    for h in range(4):
        db_n[h] = flip(d_bias[:, lanes(h)].astype(BF)).astype(BF)

    def share_grad(r):
        peer = lax.rem(a + r, 4)
        return pltpu.make_async_remote_copy(
            src_ref=db_n.at[:, at(peer, 32), :], dst_ref=db_in.at[r - 1], send_sem=sem_bs.at[r - 1],
            recv_sem=sem_br.at[r - 1], device_id={"dap": peer}, device_id_type=MESH)

    for r in (2, 1, 3):
        share_grad(r).start()
    early.g[0:512, :] = d_wa[...].astype(BF)
    early.g[512:640, :] = d_wo[...].astype(BF)
    early.g[640:, :] = jnp.zeros((384, 128), BF)
    for h in range(4):
        near_types = mm(hot[...], d_bias[:, lanes(h)])
        early.g[640 + 16 * h : 656 + 16 * h, 0:16] = nt(hot[...], near_types).astype(BF)
    early.start_a()

    for r in (1, 2, 3):
        share_grad(r).wait_recv()
    total = db_n[:, at(a, 32), :].astype(F32)
    for r in range(3):
        total = total + db_in[r].astype(F32)
    db_f[...] = total


    def fold(x):
        return x[:, :128] + x[:, 128:]

    def second_back(t):
        i = 2 * t
        hat3, scale3 = norm_cols(pair(mid, i).astype(F32))
        gain3, gain2 = twice(g3[...]), twice(g2[...])
        n3 = (hat3 * gain3).astype(BF)
        rows = [
            jnp.concatenate([db_f[h, pl.ds(i, 1), :], db_f[h, pl.ds(i + 1, 1), :]], axis=1) for h in range(4)
        ]
        db = jnp.concatenate(rows + [jnp.zeros((12, 256), F32)], axis=0).astype(BF)
        dn = pair(dn3, i).astype(F32) + mm(wb[...], db)
        d_wb[...] += nt(db, n3)
        gain_sum[2] += fold(dn * hat3)
        dm = flipped(cot, i).astype(BF) + norm_back(dn * gain3, hat3, scale3).astype(BF)
        dmf = dm.astype(F32)
        x = jnp.concatenate([prod[pl.ds(i, 128, stride=32), :], prod[pl.ds(i + 1, 128, stride=32), :]], axis=1)
        hat2, scale2 = norm_cols(x)
        n2 = (hat2 * gain2).astype(BF)
        z = mm(woutt[...], n2)
        gate = pair(gates, i)
        dz = (dmf * gate).astype(BF)
        d_open = (dmf * z * gate * (1.0 - gate)).astype(BF)
        d_wout[...] += nt(n2, dz)
        dn2 = mm(tri_out[...], dz).astype(BF).astype(F32)
        gain_sum[1] += fold(dn2 * hat2)
        dp = norm_back(dn2 * gain2, hat2, scale2)
        for r in range(2):
            d_prod[pl.ds(i + r, 128, stride=32), :] = pltpu.roll(dp[:, lanes(r)], 64 * chip, axis=1)
            d_mid[i + r] = dm[:, lanes(r)]
            d_gate[i + r] = d_open[:, lanes(r)]

    loop(16, second_back)
    early.start_b()

    def chunk(ref, q):
        return ref.at[:, at(q, 32), :]

    def move(kind, q):
        src, dst, peer = (
            (far.at[1 - core], far_in, partner), (sent, cross_in, cross), (near.at[1 - core], near_in, partner),
        )[kind]
        return pltpu.make_async_remote_copy(
            src_ref=chunk(src, q), dst_ref=chunk(dst, q), send_sem=sem_s.at[kind, q], recv_sem=sem_r.at[kind, q],
            device_id={"dap": peer}, device_id_type=MESH)

    def right_grads(half, q, store):
        def one(c):
            ch = 32 * q + c
            dp = d_prod[at(ch, 32), 64 * half : 64 * half + 64].astype(BF)
            work[pl.ds(c, 64, stride=32), :] = tn(dp, left_f[pl.ds(ch, 32, stride=128), :].astype(BF))

        loop(32, one, 4)

        def pack(j):
            store[j // 32, lax.rem(j, 32), at(q, 32), :] = work[at(j, 32), :].astype(BF)

        loop(64, pack, 4)

    def add_on(q):
        move(0, q).wait_recv()

        def one(j):
            spot = at(q, 32)
            sent[j, spot, :] = (far[core, j, spot, :].astype(F32) + far_in[j, spot, :].astype(F32)).astype(BF)

        loop(32, one, 4)
        move(1, q).start()

    def out_far(q):
        right_grads(1, q, far)
        move(0, q).start()
        pl.when(q > 0)(lambda: add_on(q - 1))

    loop(4, out_far)

    def out_near(q):
        right_grads(0, q, near)
        move(2, q).start()
        pl.when(q == 0)(lambda: add_on(3))

    loop(4, out_near)
    early.start_c()

    def left_grad(ch):
        rgt = right_f[pl.ds(ch, 128, stride=128), :].astype(BF)
        left_f[pl.ds(ch, 32, stride=128), :] = mm(d_prod[at(ch, 32), :].astype(BF), rgt)

    loop(128, left_grad, 4)

    def sides(grad_in, x, s, alive):
        g = grad_in * alive * s
        return g, g * x * (1.0 - s)

    def stored(i, k):
        rows = slice(128 * k, 128 * k + 128)
        return jnp.concatenate([pieces[i, rows], pieces[i + 1, rows]], axis=1)

    def left_part(t):
        i = 2 * t
        dl = jnp.concatenate([left_f[at(i, 128), :], left_f[at(i + 1, 128), :]], axis=1).astype(BF).astype(F32)
        dpa, dga = sides(dl, stored(i, 0), stored(i, 1), alive_of(i))
        dp = jnp.concatenate([dpa.astype(BF), dga.astype(BF), pair(d_gate, i)], axis=0)
        d_w1[0:384, :] += nt(dp, pair(normed, i))
        dn = mm(w1[:, 0:384], dp)
        part[i] = dn[:, :128]
        part[i + 1] = dn[:, 128:]

    loop(16, left_part)

    loop(4, lambda q: move(2, q).wait_recv())
    loop(4, lambda q: move(1, q).wait_recv())
    early.start_d()

    def right_part(t):
        i = 2 * t

        def summed(j):
            x = near[core, j].astype(F32) + near_in[j].astype(F32) + cross_in[j].astype(F32)
            return x.astype(BF).astype(F32)

        dr = jnp.concatenate([summed(i), summed(i + 1)], axis=1)
        dpb, dgb = sides(dr, stored(i, 2), stored(i, 3), alive_of(i))
        dp = jnp.concatenate([dpb.astype(BF), dgb.astype(BF)], axis=0)
        d_w1[384:640, :] += nt(dp, pair(normed, i))
        dn = (pair(part, i) + mm(w1[:, 384:640], dp)).astype(BF).astype(F32)
        hat, spread_1 = norm_cols(flipped(slab, i))
        gain_sum[0] += fold(dn * hat)
        dx = norm_back(dn * twice(g1[...]), hat, spread_1).astype(BF)
        res = pair(d_mid, i) + dx
        grad[i] = flip(res[:, :128]).astype(BF)
        grad[i + 1] = flip(res[:, 128:]).astype(BF)

    loop(16, right_part)


    late.g[0:640, :] = d_w1[...].astype(BF)
    late.g[640:768, :] = d_wout[...].astype(BF)
    late.g[768:784, :] = d_wb[...].astype(BF)
    late.g[784:, :] = jnp.zeros((240, 128), BF)
    ones = jnp.ones((16, 128), F32)
    for k in range(3):
        late.g[784 + 16 * k : 800 + 16 * k, :] = nt(ones, gain_sum[k], EXACT).astype(BF)
    late.start_a()
    early.finish()
    for b in range(4):
        o_att_in[:, lanes(b)] = flip(early.full[128 * b : 128 * b + 128, :])
    o_att_out[...] = early.full[512:640, :].astype(F32)
    for h in range(4):
        o_table[h] = early.full[640 + 16 * h : 656 + 16 * h, :].astype(F32)[0:4, 0:4]
    late.start_b()
    early.settle()
    late.start_c()
    for r in (1, 2, 3):
        share_bias(r).wait_send()
        share_grad(r).wait_send()
    for kind in range(3):
        loop(4, lambda c: edge(kind, c).wait_send())
        loop(4, lambda q: move(kind, q).wait_send())
    late.start_d()
    late.finish()
    for b, source in enumerate((0, 1, 3, 4)):
        o_tri_in[:, lanes(b)] = flip(late.full[128 * source : 128 * source + 128, :])
    o_tri_gate[...] = flip(late.full[256:384, :])
    o_tri_out[...] = late.full[640:768, :].astype(F32)
    o_att_bias[...] = flip(jnp.concatenate([late.full[768:784, :], jnp.zeros((112, 128), BF)], axis=0))[:, 0:4]
    for k, ref in enumerate((o_gain1, o_gain2, o_gain3)):
        ref[...] = late.full[784 + 16 * k : 800 + 16 * k, :].astype(F32)[0:1, :]
    late.settle()


def per_device(*args):
    pair_rep, cotangent, tok_mask, tok_types, pair_mask = args[:5]
    params = [v[None] if v.ndim == 1 else v for v in args[5:]]
    n_dp = lax.axis_size("dp")
    factor = (128 * 128 * n_dp) ** (-0.5)
    block = (32, 128, 128)
    shapes = [v.shape for v in params]
    spec = pl.BlockSpec(memory_space=VM)
    scratch = Sum.scratch(n_dp) * 2 + [
        VM((32, 128), F32), VM((128, 32), BF), VM((128, 128), F32),
        VM((128, 128), F32), VM((128, 128), F32), VM((128, 128), F32),
        VM((128, 640), BF), VM((640, 128), BF), VM((512, 128), BF), VM((128, 128), BF), VM((128, 128), BF),
        VM((128, 16), BF), VM((16, 128), BF), VM((16, 128), F32), VM((4, 16, 16), F32), VM((128, 512), F32),
        VM(block, BF), VM(block, BF), VM((4096, 128), F32), VM((4,) + block, BF), VM((4096, 128), F32),
        VM((16384, 128), F32), VM(block, F32), VM((32, 512, 128), F32), VM(block, BF),
        VM((4, 32, 128), F32), VM((4, 32, 128), BF), VM((4, 128, 128), BF),
        VM((128, 512), F32), VM((512, 128), F32), VM((128, 128), F32), VM((128, 128), F32), VM((16, 128), F32),
        VM((640, 128), F32), VM((3, 128, 128), F32),
        VM((4, 128, 128), BF), VM((3, 4, 32, 128), BF), VM((4, 32, 128), F32), VM((4096, 128), F32),
        VM(block, BF), VM(block, BF), VM((2048, 128), F32),
        VM((2,) + block, BF), VM(block, BF), VM(block, BF), VM(block, BF), VM((2,) + block, BF), VM(block, BF),
        DMA((3, 4)), DMA((3, 4)), DMA((3,)), DMA((3,)), DMA((3,)), DMA((3,)), DMA((3, 4)), DMA((3, 4)),
    ]
    results = pl.pallas_call(
        partial(kernel, n_dp, factor),
        out_shape=[jax.ShapeDtypeStruct(block, BF)] * 2 + [jax.ShapeDtypeStruct(s, F32) for s in shapes],
        in_specs=[spec] * N_IN,
        out_specs=[spec] * N_OUT,
        scratch_shapes=scratch,
        compiler_params=pltpu.CompilerParams(collective_id=0, has_side_effects=True, vmem_limit_bytes=63 << 20),
        name="pairformer",
    )(pair_rep[0], cotangent[0], tok_mask, tok_types, pair_mask[0], *params)
    return tuple(
        [results[0][None], results[1][None]]
        + [r[0] if v.ndim == 1 else r for r, v in zip(results[2:], args[5:])]
    )


def solution(mesh):
    return jax.shard_map(
        per_device,
        mesh=mesh,
        in_specs=(
            P("dp", "dap", None, None),
            P("dp", "dap", None, None),
            P("dp", None),
            P("dp", None),
            P("dp", "dap", None),
            P(),
            P(),
            P(),
            P(),
            P(),
            P(),
            P(),
            P(),
            P(),
            P(),
        ),
        out_specs=(
            P("dp", "dap", None, None),
            P("dp", "dap", None, None),
            P(),
            P(),
            P(),
            P(),
            P(),
            P(),
            P(),
            P(),
            P(),
            P(),
        ),
        check_vma=False,
    )
```

```python
from functools import partial

import jax
import jax.numpy as jnp
from jax import lax
from jax.experimental import pallas as pl
from jax.experimental.pallas import tpu as pltpu
from jax.sharding import PartitionSpec as P

EPSILON = 1e-05
MESH = pl.DeviceIdType.MESH
VM = pltpu.VMEM
DMA = pltpu.SemaphoreType.DMA
BF = jnp.bfloat16
F32 = jnp.float32
EXACT = lax.Precision.HIGHEST


def contract(x, y, dims, precision=None):
    return lax.dot_general(x, y, (dims, ((), ())), precision=precision, preferred_element_type=F32)


def mm(x, y, precision=None):
    return contract(x, y, ((1,), (0,)), precision)


def nt(x, y, precision=None):
    return contract(x, y, ((1,), (1,)), precision)


def tn(x, y, precision=None):
    return contract(x, y, ((0,), (0,)), precision)


def norm_cols(x):
    mean = jnp.sum(x, axis=0, keepdims=True) * (1.0 / 128)
    centred = x - mean
    spread = jnp.sum(centred * centred, axis=0, keepdims=True) * (1.0 / 128)
    scale = lax.rsqrt(spread + EPSILON)
    return centred * scale, scale


def norm_back(grad, unit, scale):
    a = jnp.sum(grad, axis=0, keepdims=True) * (1.0 / 128)
    b = jnp.sum(grad * unit, axis=0, keepdims=True) * (1.0 / 128)
    return scale * (grad - a - unit * b)


def loop(n, fn, unroll=1, first=0):
    def body(i, carry):
        fn(i)
        return carry
    lax.fori_loop(first, n, body, 0, unroll=unroll)


def at(i, size):
    return pl.ds(pl.multiple_of(i * size, size), size)


def halves(x):
    return x[:, :128], x[:, 128:]


def twice(x):
    return jnp.concatenate([x, x], axis=1)


def pair(ref, i):
    return jnp.concatenate([ref[i], ref[i + 1]], axis=1)


def lanes(r):
    return slice(128 * r, 128 * r + 128)


class Sum:
    def __init__(self, n_dp, factor, a, p, refs):
        self.n_dp, self.factor, self.a, self.p = n_dp, factor, a, p
        self.partner, self.cross = a + 1 - 2 * lax.rem(a, 2), lax.rem(a + 2, 4)
        (self.g, self.part, self.quarter, self.pieces, self.mine, self.joined, self.joined_b, self.full,
         self.sa, self.ra, self.sb, self.rb, self.sc, self.rc, self.sd, self.rd) = refs
        self.size = 256 // n_dp

    def remote(self, src, dst, s, r, **peer):
        return pltpu.make_async_remote_copy(
            src_ref=src, dst_ref=dst, send_sem=s, recv_sem=r, device_id=peer, device_id_type=MESH)

    def copy_a(self, r):
        peer = lax.rem(self.a + r, 4)
        return self.remote(self.g.at[at(peer, 256)], self.part.at[r - 1], self.sa.at[r - 1], self.ra.at[r - 1], dap=peer)

    def copy_b(self, r):
        peer = lax.rem(self.p + r, self.n_dp)
        return self.remote(
            self.quarter.at[at(peer, self.size)], self.pieces.at[r - 1], self.sb.at[r - 1], self.rb.at[r - 1], dp=peer)

    def copy_c(self, r, sending=True):
        peer = lax.rem(self.p + r, self.n_dp)
        owner = self.p if sending else lax.rem(self.p + self.n_dp - r, self.n_dp)
        return self.remote(
            self.mine, self.joined.at[at(owner, self.size)], self.sc.at[r - 1], self.rc.at[r - 1], dp=peer)

    def copy_d(self, k):
        there = at(self.cross if k == 2 else self.a, 256)
        src = self.full.at[there] if k == 2 else self.joined_b
        return self.remote(
            src, self.full.at[there], self.sd.at[k], self.rd.at[k], dap=self.cross if k == 0 else self.partner)

    def start_a(self):
        for r in (2, 1, 3):
            self.copy_a(r).start()

    def start_b(self):
        total = self.g[at(self.a, 256), :].astype(F32)
        for r in (1, 2, 3):
            self.copy_a(r).wait_recv()
            total = total + self.part[r - 1].astype(F32)
        self.quarter[...] = total
        loop(self.n_dp, lambda r: self.copy_b(r).start(), first=1)

    def start_c(self):
        loop(self.n_dp, lambda r: self.copy_b(r).wait_recv(), first=1)
        total = self.quarter[at(self.p, self.size), :] + jnp.sum(self.pieces[...], axis=0)
        self.mine[...] = total * self.factor
        loop(self.n_dp, lambda r: self.copy_c(r).start(), first=1)
        self.joined[at(self.p, self.size), :] = self.mine[...]

    def start_d(self):
        loop(self.n_dp, lambda r: self.copy_c(r, False).wait_recv(), first=1)
        self.joined_b[...] = self.joined[...].astype(BF)
        self.copy_d(0).start()
        self.copy_d(1).start()
        self.full[at(self.a, 256), :] = self.joined_b[...]

    def finish(self):
        self.copy_d(0).wait_recv()
        self.copy_d(2).start()
        self.copy_d(1).wait_recv()
        self.copy_d(2).wait_recv()

    def settle(self):
        for r in (1, 2, 3):
            self.copy_a(r).wait_send()
        loop(self.n_dp, lambda r: self.copy_b(r).wait_send(), first=1)
        loop(self.n_dp, lambda r: self.copy_c(r).wait_send(), first=1)
        for k in range(3):
            self.copy_d(k).wait_send()

    @staticmethod
    def scratch(n_dp):
        size = 256 // n_dp
        return [
            VM((1024, 128), BF), VM((3, 256, 128), BF), VM((256, 128), F32), VM((n_dp - 1, size, 128), F32),
            VM((size, 128), F32), VM((256, 128), F32), VM((256, 128), BF), VM((1024, 128), BF),
        ] + [DMA((3,))] * 2 + [DMA((n_dp - 1,))] * 4 + [DMA((3,))] * 2


N_IN, N_OUT, N_SUM = 15, 12, 16


def kernel(n_dp, factor, *refs):
    (slab, cot, tok_mask, tok_types, pair_mask, gain1, tri_in, tri_gate, gain2, tri_out, gain3, att_bias, att_in,
     att_out, table) = refs[:N_IN]
    (out, grad, o_gain1, o_tri_in, o_tri_gate, o_gain2, o_tri_out, o_gain3, o_att_bias, o_att_in, o_att_out,
     o_table) = refs[N_IN : N_IN + N_OUT]
    rest = refs[N_IN + N_OUT :]
    a, p = lax.axis_index("dap"), lax.axis_index("dp")
    partner, cross, chip, core = a + 1 - 2 * lax.rem(a, 2), lax.rem(a + 2, 4), a // 2, lax.rem(a, 2)
    early = Sum(n_dp, factor, a, p, rest[:N_SUM])
    late = Sum(n_dp, factor, a, p, rest[N_SUM : 2 * N_SUM])
    (live, live_t, tok_t, g1, g2, g3, w1, w1t, wat, wot, woutt, wb, wbt, hot, tab, bt,
     mid, dn3, prod, right, left_f, right_f, gates, pieces, normed, bias_f, bias_b, bias,
     d_bias, d_wa, d_wo, d_wout, d_wb, d_w1, gain_sum,
     db_n, db_in, db_f, d_prod, d_mid, d_gate, work, far, far_in, sent, cross_in, near, near_in,
     sem_es, sem_er, sem_is, sem_ir, sem_bs, sem_br, sem_s, sem_r) = rest[2 * N_SUM :]
    part = gates

    barrier = pltpu.get_barrier_semaphore()
    for r in range(1, 4):
        pl.semaphore_signal(barrier, inc=1, device_id={"dap": lax.rem(a + r, 4)}, device_id_type=MESH)
    loop(n_dp, lambda r: pl.semaphore_signal(
        barrier, inc=1, device_id={"dp": lax.rem(p + r, n_dp)}, device_id_type=MESH), first=1)

    rows_i = lax.broadcasted_iota(jnp.int32, (128, 128), 0)
    unit = (rows_i == lax.broadcasted_iota(jnp.int32, (128, 128), 1)).astype(F32).astype(BF)

    def flip(block):
        return nt(unit, block)

    def flipped(ref, i):
        return jnp.concatenate([flip(ref[i]), flip(ref[i + 1])], axis=1)

    def column(row):
        return jnp.broadcast_to(row, (128, 128)).T

    tokens = tok_mask[...].astype(F32)
    tok_t[...] = column(tokens)
    live[...] = pair_mask[...].astype(F32) * tok_t[at(a, 32), :] * tokens
    live_t[...] = tn(live[...].astype(BF), unit[:32, :32]).astype(BF)
    for gain, row in ((g1, gain1), (g2, gain2), (g3, gain3)):
        gain[...] = column(row[...])
    w1[:, 0:256] = tri_in[:, 0:256]
    w1[:, 256:384] = tri_gate[...]
    w1[:, 384:640] = tri_in[:, 256:512]
    for b in range(5):
        w1t[128 * b : 128 * b + 128, :] = flip(w1[:, lanes(b)]).astype(BF)
    for b in range(4):
        wat[128 * b : 128 * b + 128, :] = flip(att_in[:, lanes(b)]).astype(BF)
    wot[...] = flip(att_out[...]).astype(BF)
    woutt[...] = flip(tri_out[...]).astype(BF)
    wbt[...] = jnp.concatenate([att_bias[...].astype(F32), jnp.zeros((12, 128), F32)], axis=0).astype(BF)
    wb[...] = flip(wbt[...]).astype(BF)
    tab[...] = jnp.zeros_like(tab)
    tab[:, 0:4, 0:4] = table[...]
    hot[...] = (lax.broadcasted_iota(jnp.int32, (16, 128), 0) == tok_types[...]).astype(F32)

    def alive_of(i):
        return jnp.concatenate([live[pl.ds(i, 1), :], live[pl.ds(i + 1, 1), :]], axis=1)


    def edge(kind, c):
        spot = right.at[cross if kind == 2 else a, at(c, 8)]
        return pltpu.make_async_remote_copy(
            src_ref=spot, dst_ref=spot, send_sem=sem_es.at[kind, c], recv_sem=sem_er.at[kind, c],
            device_id={"dap": cross if kind == 1 else partner}, device_id_type=MESH)

    def project(c, t):
        i = c * 8 + 2 * t
        hat, _ = norm_cols(flipped(slab, i))
        n = (hat * twice(g1[...])).astype(BF)
        q = mm(w1t[...], n)
        alive = alive_of(i)
        sa, sb = jax.nn.sigmoid(q[128:256]), jax.nn.sigmoid(q[512:])
        lft = (sa * q[:128] * alive).astype(BF).astype(F32)
        rgt = (sb * q[384:512] * alive).astype(BF)
        gate = jax.nn.sigmoid(q[256:384])
        for r in range(2):
            normed[i + r] = n[:, lanes(r)]
            left_f[at(i + r, 128), :] = lft[:, lanes(r)]
            right[a, i + r] = rgt[:, lanes(r)]
            gates[i + r] = gate[:, lanes(r)]
            pieces[i + r, 0:128] = q[:128, lanes(r)]
            pieces[i + r, 128:256] = sa[:, lanes(r)]
            pieces[i + r, 256:384] = q[384:512, lanes(r)]
            pieces[i + r, 384:512] = sb[:, lanes(r)]

    def first(c):
        loop(4, lambda t: project(c, t), 2)
        pl.when(c == 0)(lambda: pl.semaphore_wait(barrier, 3 + n_dp - 1))
        edge(1, c).start()
        edge(0, c).start()

    loop(4, first)

    def unpack(block, base):
        loop(32, lambda j: right_f.__setitem__((at(base + j, 128), slice(None)), right[block, j].astype(F32)), 2)

    def multiply(half):
        def one(ch):
            lft = left_f[pl.ds(ch, 32, stride=128), :].astype(BF)
            rgt = right_f[pl.ds(64 * 128 * half + ch, 64, stride=128), :].astype(BF)
            prod[at(ch, 32), 64 * half : 64 * half + 64] = nt(lft, rgt)
        loop(128, one, 16)

    loop(4, lambda c: edge(0, c).wait_recv())
    low = 2 * chip
    unpack(low, 0)
    unpack(low + 1, 32)
    multiply(0)

    def relay(c):
        edge(1, c).wait_recv()
        edge(2, c).start()

    loop(4, relay)
    loop(4, lambda c: edge(2, c).wait_recv())
    unpack(2 - low, 64)
    unpack(3 - low, 96)
    multiply(1)

    def second(t):
        i = 2 * t
        xs = []
        for r in range(2):
            rows = pl.ds(i + r, 128, stride=32)
            x = pltpu.roll(prod[rows, :], 64 * chip, axis=1)
            prod[rows, :] = x
            xs.append(x)
        hat, _ = norm_cols(jnp.concatenate(xs, axis=1))
        n = (hat * twice(g2[...])).astype(BF)
        middle = (flipped(slab, i) + pair(gates, i) * mm(woutt[...], n)).astype(BF)
        hat, _ = norm_cols(middle.astype(F32))
        n = (hat * twice(g3[...])).astype(BF)
        heads = mm(wbt[...], n)
        for r in range(2):
            mid[i + r] = middle[:, lanes(r)]
            for h in range(4):
                bias_f[h, pl.ds(i + r, 1), :] = heads[h : h + 1, lanes(r)]

    loop(16, second, 4)
    bias_b[...] = bias_f[...].astype(BF)

    def share_bias(r):
        return pltpu.make_async_remote_copy(
            src_ref=bias_b, dst_ref=bias.at[:, at(a, 32), :], send_sem=sem_is.at[r - 1], recv_sem=sem_ir.at[r - 1],
            device_id={"dap": lax.rem(a + r, 4)}, device_id_type=MESH)

    for r in (2, 1, 3):
        share_bias(r).start()
    bias[:, at(a, 32), :] = bias_b[...]
    for h in range(4):
        near_types = mm(tab[h].T, hot[...], EXACT)
        bt[:, lanes(h)] = tn(hot[...], near_types, EXACT)
    for ref in (d_bias, d_wa, d_wo, d_wout, d_wb, d_w1, gain_sum):
        ref[...] = jnp.zeros_like(ref)
    for r in (1, 2, 3):
        share_bias(r).wait_recv()
    for h in range(4):
        bt[:, lanes(h)] += flip(bias[h])


    def spread(x):
        zero = jnp.zeros((32, 128), x.dtype)
        cols = [
            jnp.concatenate([x[32 * h : 32 * h + 32] if g == h else zero for g in range(4)], axis=0)
            for h in range(4)
        ]
        return jnp.concatenate(cols, axis=1)

    scale = 32.0 ** -0.5

    def attend(t):
        i = 2 * t
        m = pair(mid, i).astype(F32)
        hat, _ = norm_cols(m)
        n = (hat * twice(g3[...])).astype(BF)
        q3 = mm(wat[...], n)
        qkv = q3[:384].astype(BF)
        gate = jax.nn.sigmoid(q3[384:])
        ct = flipped(cot, i).astype(BF)
        d_gated = mm(att_out[...], ct).astype(BF).astype(F32)
        d_att = d_gated * gate
        picked = lax.broadcasted_iota(jnp.int32, (32, 256), 0) == (
            i + lax.broadcasted_iota(jnp.int32, (32, 256), 1) // 128)
        alive = mm(live_t[...], picked.astype(F32).astype(BF))
        parts, atts = [], []
        for r in range(2):
            q, k, v = (qkv[128 * x : 128 * x + 128, lanes(r)] for x in range(3))
            kv = flip(qkv[128:384, lanes(r)]).astype(BF)
            q4 = spread(q)
            e = jnp.exp(mm(kv[:, :128], q4) * scale + bt[...])
            e = e * jnp.concatenate([alive[:, lanes(r)]] * 4, axis=1)
            s = jnp.sum(e, axis=0, keepdims=True)
            w = e * (1.0 / jnp.maximum(s, 1.0))
            ab = w.astype(BF)
            atts.append(jnp.concatenate([mm(v[32 * h : 32 * h + 32], ab[:, lanes(h)]) for h in range(4)], axis=0))
            do4 = spread(d_att[:, lanes(r)].astype(BF))
            da = mm(kv[:, 128:], do4).astype(BF).astype(F32)
            u = da * w
            total = jnp.sum(u, axis=0, keepdims=True)
            total = jnp.where(s > 1.0, total, jnp.where(s == 1.0, 0.5 * total, 0.0))
            ds = u - w * total
            d_bias[...] += ds
            dsb = ds.astype(BF)
            dv = nt(do4, ab)
            dk = nt(q4, dsb) * scale
            dq = jnp.concatenate(
                [mm(k[32 * h : 32 * h + 32], dsb[:, lanes(h)]) for h in range(4)], axis=0) * scale
            parts.append(jnp.concatenate([dq, dk, dv], axis=0).astype(BF))
        att = jnp.concatenate(atts, axis=1)
        d_open = (d_gated * att * gate * (1.0 - gate)).astype(BF)
        dp = jnp.concatenate([jnp.concatenate(parts, axis=1), d_open], axis=0)
        dn = mm(att_in[...], dp).astype(BF)
        d_wa[...] += nt(dp, n)
        gated = (gate * att).astype(BF)
        d_wo[...] += nt(gated, ct)
        res = (m + mm(wot[...], gated)).astype(BF)
        for r in range(2):
            dn3[i + r] = dn[:, lanes(r)]
            out[i + r] = flip(res[:, lanes(r)]).astype(BF)

    loop(16, attend, 2)

    for h in range(4):
        db_n[h] = flip(d_bias[:, lanes(h)].astype(BF)).astype(BF)

    def share_grad(r):
        peer = lax.rem(a + r, 4)
        return pltpu.make_async_remote_copy(
            src_ref=db_n.at[:, at(peer, 32), :], dst_ref=db_in.at[r - 1], send_sem=sem_bs.at[r - 1],
            recv_sem=sem_br.at[r - 1], device_id={"dap": peer}, device_id_type=MESH)

    for r in (2, 1, 3):
        share_grad(r).start()
    early.g[0:512, :] = d_wa[...].astype(BF)
    early.g[512:640, :] = d_wo[...].astype(BF)
    early.g[640:, :] = jnp.zeros((384, 128), BF)
    for h in range(4):
        near_types = mm(hot[...], d_bias[:, lanes(h)])
        early.g[640 + 16 * h : 656 + 16 * h, 0:16] = nt(hot[...], near_types).astype(BF)
    early.start_a()

    for r in (1, 2, 3):
        share_grad(r).wait_recv()
    total = db_n[:, at(a, 32), :].astype(F32)
    for r in range(3):
        total = total + db_in[r].astype(F32)
    db_f[...] = total


    def fold(x):
        return x[:, :128] + x[:, 128:]

    def second_back(t):
        i = 2 * t
        hat3, scale3 = norm_cols(pair(mid, i).astype(F32))
        gain3, gain2 = twice(g3[...]), twice(g2[...])
        n3 = (hat3 * gain3).astype(BF)
        rows = [
            jnp.concatenate([db_f[h, pl.ds(i, 1), :], db_f[h, pl.ds(i + 1, 1), :]], axis=1) for h in range(4)
        ]
        db = jnp.concatenate(rows + [jnp.zeros((12, 256), F32)], axis=0).astype(BF)
        dn = pair(dn3, i).astype(F32) + mm(wb[...], db)
        d_wb[...] += nt(db, n3)
        gain_sum[2] += fold(dn * hat3)
        dm = flipped(cot, i).astype(BF) + norm_back(dn * gain3, hat3, scale3).astype(BF)
        dmf = dm.astype(F32)
        x = jnp.concatenate([prod[pl.ds(i, 128, stride=32), :], prod[pl.ds(i + 1, 128, stride=32), :]], axis=1)
        hat2, scale2 = norm_cols(x)
        n2 = (hat2 * gain2).astype(BF)
        z = mm(woutt[...], n2)
        gate = pair(gates, i)
        dz = (dmf * gate).astype(BF)
        d_open = (dmf * z * gate * (1.0 - gate)).astype(BF)
        d_wout[...] += nt(n2, dz)
        dn2 = mm(tri_out[...], dz).astype(BF).astype(F32)
        gain_sum[1] += fold(dn2 * hat2)
        dp = norm_back(dn2 * gain2, hat2, scale2)
        for r in range(2):
            d_prod[pl.ds(i + r, 128, stride=32), :] = pltpu.roll(dp[:, lanes(r)], 64 * chip, axis=1)
            d_mid[i + r] = dm[:, lanes(r)]
            d_gate[i + r] = d_open[:, lanes(r)]

    loop(16, second_back, 4)
    early.start_b()

    def chunk(ref, q):
        return ref.at[:, at(q, 32), :]

    def move(kind, q):
        src, dst, peer = (
            (far.at[1 - core], far_in, partner), (sent, cross_in, cross), (near.at[1 - core], near_in, partner),
        )[kind]
        return pltpu.make_async_remote_copy(
            src_ref=chunk(src, q), dst_ref=chunk(dst, q), send_sem=sem_s.at[kind, q], recv_sem=sem_r.at[kind, q],
            device_id={"dap": peer}, device_id_type=MESH)

    def right_grads(half, q, store):
        def one(c):
            ch = 32 * q + c
            dp = d_prod[at(ch, 32), 64 * half : 64 * half + 64].astype(BF)
            work[pl.ds(c, 64, stride=32), :] = tn(dp, left_f[pl.ds(ch, 32, stride=128), :].astype(BF))

        loop(32, one, 16)

        def pack(j):
            store[j // 32, lax.rem(j, 32), at(q, 32), :] = work[at(j, 32), :].astype(BF)

        loop(64, pack, 4)

    def add_on(q):
        move(0, q).wait_recv()

        def one(j):
            spot = at(q, 32)
            sent[j, spot, :] = (far[core, j, spot, :].astype(F32) + far_in[j, spot, :].astype(F32)).astype(BF)

        loop(32, one, 4)
        move(1, q).start()

    def out_far(q):
        right_grads(1, q, far)
        move(0, q).start()
        pl.when(q > 0)(lambda: add_on(q - 1))

    loop(4, out_far)

    def out_near(q):
        right_grads(0, q, near)
        move(2, q).start()
        pl.when(q == 0)(lambda: add_on(3))

    loop(4, out_near)
    early.start_c()

    def left_grad(ch):
        rgt = right_f[pl.ds(ch, 128, stride=128), :].astype(BF)
        left_f[pl.ds(ch, 32, stride=128), :] = mm(d_prod[at(ch, 32), :].astype(BF), rgt)

    loop(128, left_grad, 16)

    def sides(grad_in, x, s, alive):
        g = grad_in * alive * s
        return g, g * x * (1.0 - s)

    def stored(i, k):
        rows = slice(128 * k, 128 * k + 128)
        return jnp.concatenate([pieces[i, rows], pieces[i + 1, rows]], axis=1)

    def left_part(t):
        i = 2 * t
        dl = jnp.concatenate([left_f[at(i, 128), :], left_f[at(i + 1, 128), :]], axis=1).astype(BF).astype(F32)
        dpa, dga = sides(dl, stored(i, 0), stored(i, 1), alive_of(i))
        dp = jnp.concatenate([dpa.astype(BF), dga.astype(BF), pair(d_gate, i)], axis=0)
        d_w1[0:384, :] += nt(dp, pair(normed, i))
        dn = mm(w1[:, 0:384], dp)
        part[i] = dn[:, :128]
        part[i + 1] = dn[:, 128:]

    loop(16, left_part, 4)

    loop(4, lambda q: move(2, q).wait_recv())
    loop(4, lambda q: move(1, q).wait_recv())
    early.start_d()

    def right_part(t):
        i = 2 * t

        def summed(j):
            x = near[core, j].astype(F32) + near_in[j].astype(F32) + cross_in[j].astype(F32)
            return x.astype(BF).astype(F32)

        dr = jnp.concatenate([summed(i), summed(i + 1)], axis=1)
        dpb, dgb = sides(dr, stored(i, 2), stored(i, 3), alive_of(i))
        dp = jnp.concatenate([dpb.astype(BF), dgb.astype(BF)], axis=0)
        d_w1[384:640, :] += nt(dp, pair(normed, i))
        dn = (pair(part, i) + mm(w1[:, 384:640], dp)).astype(BF).astype(F32)
        hat, spread_1 = norm_cols(flipped(slab, i))
        gain_sum[0] += fold(dn * hat)
        dx = norm_back(dn * twice(g1[...]), hat, spread_1).astype(BF)
        res = pair(d_mid, i) + dx
        grad[i] = flip(res[:, :128]).astype(BF)
        grad[i + 1] = flip(res[:, 128:]).astype(BF)

    loop(16, right_part, 4)


    late.g[0:640, :] = d_w1[...].astype(BF)
    late.g[640:768, :] = d_wout[...].astype(BF)
    late.g[768:784, :] = d_wb[...].astype(BF)
    late.g[784:, :] = jnp.zeros((240, 128), BF)
    ones = jnp.ones((16, 128), F32)
    for k in range(3):
        late.g[784 + 16 * k : 800 + 16 * k, :] = nt(ones, gain_sum[k], EXACT).astype(BF)
    late.start_a()
    early.finish()
    for b in range(4):
        o_att_in[:, lanes(b)] = flip(early.full[128 * b : 128 * b + 128, :])
    o_att_out[...] = early.full[512:640, :].astype(F32)
    for h in range(4):
        o_table[h] = early.full[640 + 16 * h : 656 + 16 * h, :].astype(F32)[0:4, 0:4]
    late.start_b()
    early.settle()
    late.start_c()
    for r in (1, 2, 3):
        share_bias(r).wait_send()
        share_grad(r).wait_send()
    for kind in range(3):
        loop(4, lambda c: edge(kind, c).wait_send())
        loop(4, lambda q: move(kind, q).wait_send())
    late.start_d()
    late.finish()
    for b, source in enumerate((0, 1, 3, 4)):
        o_tri_in[:, lanes(b)] = flip(late.full[128 * source : 128 * source + 128, :])
    o_tri_gate[...] = flip(late.full[256:384, :])
    o_tri_out[...] = late.full[640:768, :].astype(F32)
    o_att_bias[...] = late.full[768:784, :].astype(F32)[0:4, :]
    for k, ref in enumerate((o_gain1, o_gain2, o_gain3)):
        ref[...] = late.full[784 + 16 * k : 800 + 16 * k, :].astype(F32)[0:1, :]
    late.settle()


def hand_over(*refs):
    held, sems = refs[2 * N_OUT : 3 * N_OUT], refs[3 * N_OUT]
    parts = [(k, pl.ds(8 * c, 8), 4 * k + c) for k in range(2) for c in range(4)]
    parts += [(k, slice(None), 6 + k) for k in range(2, N_OUT)]
    reads = [pltpu.make_async_copy(refs[k].at[s], held[k].at[s], sems.at[0, n]) for k, s, n in parts]
    writes = [pltpu.make_async_copy(held[k].at[s], refs[N_OUT + k].at[s], sems.at[1, n]) for k, s, n in parts]
    for copy in reads:
        copy.start()
    for read, write in zip(reads, writes):
        read.wait()
        write.start()
    for copy in writes:
        copy.wait()


def per_device(*args):
    pair_rep, cotangent, tok_mask, tok_types, pair_mask = args[:5]
    params = [v[None] if v.ndim == 1 else v for v in args[5:]]
    params[6] = params[6].T
    n_dp = lax.axis_size("dp")
    factor = (128 * 128 * n_dp) ** (-0.5)
    block = (32, 128, 128)
    shapes = [v.shape for v in params]
    spec = pl.BlockSpec(memory_space=VM)
    scratch = Sum.scratch(n_dp) * 2 + [
        VM((32, 128), F32), VM((128, 32), BF), VM((128, 128), F32),
        VM((128, 128), F32), VM((128, 128), F32), VM((128, 128), F32),
        VM((128, 640), BF), VM((640, 128), BF), VM((512, 128), BF), VM((128, 128), BF), VM((128, 128), BF),
        VM((128, 16), BF), VM((16, 128), BF), VM((16, 128), F32), VM((4, 16, 16), F32), VM((128, 512), F32),
        VM(block, BF), VM(block, BF), VM((4096, 128), F32), VM((4,) + block, BF), VM((4096, 128), F32),
        VM((16384, 128), F32), VM(block, F32), VM((32, 512, 128), F32), VM(block, BF),
        VM((4, 32, 128), F32), VM((4, 32, 128), BF), VM((4, 128, 128), BF),
        VM((128, 512), F32), VM((512, 128), F32), VM((128, 128), F32), VM((128, 128), F32), VM((16, 128), F32),
        VM((640, 128), F32), VM((3, 128, 128), F32),
        VM((4, 128, 128), BF), VM((3, 4, 32, 128), BF), VM((4, 32, 128), F32), VM((4096, 128), F32),
        VM(block, BF), VM(block, BF), VM((2048, 128), F32),
        VM((2,) + block, BF), VM(block, BF), VM(block, BF), VM(block, BF), VM((2,) + block, BF), VM(block, BF),
        DMA((3, 4)), DMA((3, 4)), DMA((3,)), DMA((3,)), DMA((3,)), DMA((3,)), DMA((3, 4)), DMA((3, 4)),
    ]
    results = pl.pallas_call(
        partial(kernel, n_dp, factor),
        out_shape=[jax.ShapeDtypeStruct(block, BF)] * 2 + [jax.ShapeDtypeStruct(s, F32) for s in shapes],
        in_specs=[spec] * N_IN,
        out_specs=[spec] * N_OUT,
        scratch_shapes=scratch,
        compiler_params=pltpu.CompilerParams(collective_id=0, has_side_effects=True, vmem_limit_bytes=63 << 20),
        name="pairformer",
    )(pair_rep[0], cotangent[0], tok_mask, tok_types, pair_mask[0], *params)
    anywhere = pl.BlockSpec(memory_space=pl.ANY)
    results = pl.pallas_call(
        hand_over,
        out_shape=[jax.ShapeDtypeStruct(r.shape, r.dtype) for r in results],
        in_specs=[anywhere] * N_OUT,
        out_specs=[anywhere] * N_OUT,
        scratch_shapes=[VM(r.shape, r.dtype) for r in results] + [DMA((2, N_OUT + 6))],
        name="hand_over",
    )(*results)
    results = list(results)
    results[8] = results[8].T
    return tuple(
        [results[0][None], results[1][None]]
        + [r[0] if v.ndim == 1 else r for r, v in zip(results[2:], args[5:])]
    )


def solution(mesh):
    return jax.shard_map(
        per_device,
        mesh=mesh,
        in_specs=(
            P("dp", "dap", None, None),
            P("dp", "dap", None, None),
            P("dp", None),
            P("dp", None),
            P("dp", "dap", None),
            P(),
            P(),
            P(),
            P(),
            P(),
            P(),
            P(),
            P(),
            P(),
            P(),
        ),
        out_specs=(
            P("dp", "dap", None, None),
            P("dp", "dap", None, None),
            P(),
            P(),
            P(),
            P(),
            P(),
            P(),
            P(),
            P(),
            P(),
            P(),
        ),
        check_vma=False,
    )
```

```python
from functools import partial

import jax
import jax.numpy as jnp
from jax import lax
from jax.experimental import pallas as pl
from jax.experimental.pallas import tpu as pltpu
from jax.sharding import PartitionSpec as P

EPSILON = 1e-05
MESH = pl.DeviceIdType.MESH
VM = pltpu.VMEM
DMA = pltpu.SemaphoreType.DMA
BF = jnp.bfloat16
F32 = jnp.float32
EXACT = lax.Precision.HIGHEST


def contract(x, y, dims, precision=None):
    return lax.dot_general(x, y, (dims, ((), ())), precision=precision, preferred_element_type=F32)


def mm(x, y, precision=None):
    return contract(x, y, ((1,), (0,)), precision)


def nt(x, y, precision=None):
    return contract(x, y, ((1,), (1,)), precision)


def tn(x, y, precision=None):
    return contract(x, y, ((0,), (0,)), precision)


def norm_cols(x):
    mean = jnp.sum(x, axis=0, keepdims=True) * (1.0 / 128)
    centred = x - mean
    spread = jnp.sum(centred * centred, axis=0, keepdims=True) * (1.0 / 128)
    scale = lax.rsqrt(spread + EPSILON)
    return centred * scale, scale


def norm_back(grad, unit, scale):
    a = jnp.sum(grad, axis=0, keepdims=True) * (1.0 / 128)
    b = jnp.sum(grad * unit, axis=0, keepdims=True) * (1.0 / 128)
    return scale * (grad - a - unit * b)


def loop(n, fn, unroll=1, first=0):
    def body(i, carry):
        fn(i)
        return carry
    lax.fori_loop(first, n, body, 0, unroll=unroll)


def at(i, size):
    return pl.ds(pl.multiple_of(i * size, size), size)


def halves(x):
    return x[:, :128], x[:, 128:]


def twice(x):
    return jnp.concatenate([x, x], axis=1)


def pair(ref, i):
    return jnp.concatenate([ref[i], ref[i + 1]], axis=1)


def lanes(r):
    return slice(128 * r, 128 * r + 128)


class Sum:
    def __init__(self, n_dp, factor, a, p, refs):
        self.n_dp, self.factor, self.a, self.p = n_dp, factor, a, p
        self.partner, self.cross = a + 1 - 2 * lax.rem(a, 2), lax.rem(a + 2, 4)
        (self.g, self.part, self.quarter, self.pieces, self.mine, self.joined, self.joined_b, self.full,
         self.sa, self.ra, self.sb, self.rb, self.sc, self.rc, self.sd, self.rd) = refs
        self.size = 256 // n_dp

    def remote(self, src, dst, s, r, **peer):
        return pltpu.make_async_remote_copy(
            src_ref=src, dst_ref=dst, send_sem=s, recv_sem=r, device_id=peer, device_id_type=MESH)

    def copy_a(self, r):
        peer = lax.rem(self.a + r, 4)
        return self.remote(self.g.at[at(peer, 256)], self.part.at[r - 1], self.sa.at[r - 1], self.ra.at[r - 1], dap=peer)

    def copy_b(self, r):
        peer = lax.rem(self.p + r, self.n_dp)
        return self.remote(
            self.quarter.at[at(peer, self.size)], self.pieces.at[r - 1], self.sb, self.rb, dp=peer)

    def copy_c(self, r):
        peer = lax.rem(self.p + r, self.n_dp)
        return self.remote(self.mine, self.joined.at[at(self.p, self.size)], self.sc, self.rc, dp=peer)

    def all_of(self, ref, s, r):
        return self.remote(ref, ref, s, r, dp=lax.rem(self.p + 1, self.n_dp))

    def others(self, ref):
        return ref.at[pl.ds(0, (self.n_dp - 1) * self.size)]

    def copy_d(self, k):
        there = at(self.cross if k == 2 else self.a, 256)
        src = self.full.at[there] if k == 2 else self.joined_b
        return self.remote(
            src, self.full.at[there], self.sd.at[k], self.rd.at[k], dap=self.cross if k == 0 else self.partner)

    def start_a(self):
        for r in (2, 1, 3):
            self.copy_a(r).start()

    def start_b(self):
        total = self.g[at(self.a, 256), :].astype(F32)
        for r in (1, 2, 3):
            self.copy_a(r).wait_recv()
            total = total + self.part[r - 1].astype(F32)
        self.quarter[...] = total
        for r in range(1, self.n_dp):
            self.copy_b(r).start()

    def start_c(self):
        self.all_of(self.pieces, self.sb, self.rb).wait_recv()
        total = self.quarter[at(self.p, self.size), :] + jnp.sum(self.pieces[...], axis=0)
        self.mine[...] = total * self.factor
        for r in range(1, self.n_dp):
            self.copy_c(r).start()
        self.joined[at(self.p, self.size), :] = self.mine[...]

    def start_d(self):
        self.all_of(self.others(self.joined), self.sc, self.rc).wait_recv()
        self.joined_b[...] = self.joined[...].astype(BF)
        self.copy_d(0).start()
        self.copy_d(1).start()
        self.full[at(self.a, 256), :] = self.joined_b[...]

    def finish(self):
        self.copy_d(0).wait_recv()
        self.copy_d(2).start()
        self.copy_d(1).wait_recv()
        self.copy_d(2).wait_recv()

    def settle(self):
        for r in (1, 2, 3):
            self.copy_a(r).wait_send()
        self.all_of(self.pieces, self.sb, self.rb).wait_send()
        self.all_of(self.others(self.joined), self.sc, self.rc).wait_send()
        for k in range(3):
            self.copy_d(k).wait_send()

    @staticmethod
    def scratch(n_dp):
        size = 256 // n_dp
        return [
            VM((1024, 128), BF), VM((3, 256, 128), BF), VM((256, 128), F32), VM((n_dp - 1, size, 128), F32),
            VM((size, 128), F32), VM((256, 128), F32), VM((256, 128), BF), VM((1024, 128), BF),
        ] + [DMA((3,))] * 2 + [DMA] * 4 + [DMA((3,))] * 2


N_IN, N_OUT, N_SUM = 15, 12, 16
GROUP = 4


def kernel(n_dp, factor, *refs):
    (slab, cot, tok_mask, tok_types, pair_mask, gain1, tri_in, tri_gate, gain2, tri_out, gain3, att_bias, att_in,
     att_out, table) = refs[:N_IN]
    (out, grad, o_gain1, o_tri_in, o_tri_gate, o_gain2, o_tri_out, o_gain3, o_att_bias, o_att_in, o_att_out,
     o_table) = refs[N_IN : N_IN + N_OUT]
    rest = refs[N_IN + N_OUT :]
    a, p = lax.axis_index("dap"), lax.axis_index("dp")
    partner, cross, chip, core = a + 1 - 2 * lax.rem(a, 2), lax.rem(a + 2, 4), a // 2, lax.rem(a, 2)
    early = Sum(n_dp, factor, a, p, rest[:N_SUM])
    late = Sum(n_dp, factor, a, p, rest[N_SUM : 2 * N_SUM])
    (live, live_t, tok_t, g1, g2, g3, w1, w1t, wat, wot, woutt, wb, wbt, hot, tab, bt,
     mid, dn3, prod, right, left_f, right_f, gates, pieces, normed, bias_f, bias_b, bias,
     d_bias, d_wa, d_wo, d_wout, d_wb, d_w1, gain_sum,
     db_n, db_in, db_f, d_prod, d_mid, d_gate, work, far, far_in, sent, cross_in, near, near_in,
     sem_es, sem_er, sem_is, sem_ir, sem_bs, sem_br, sem_s, sem_r) = rest[2 * N_SUM :]
    part = gates

    barrier = pltpu.get_barrier_semaphore()
    for r in range(1, 4):
        pl.semaphore_signal(barrier, inc=1, device_id={"dap": lax.rem(a + r, 4)}, device_id_type=MESH)
    for r in range(1, n_dp):
        pl.semaphore_signal(barrier, inc=1, device_id={"dp": lax.rem(p + r, n_dp)}, device_id_type=MESH)

    rows_i = lax.broadcasted_iota(jnp.int32, (128, 128), 0)
    unit = (rows_i == lax.broadcasted_iota(jnp.int32, (128, 128), 1)).astype(F32).astype(BF)

    def flip(block):
        return nt(unit, block)

    def flipped(ref, i):
        return jnp.concatenate([flip(ref[i]), flip(ref[i + 1])], axis=1)

    def column(row):
        return jnp.broadcast_to(row, (128, 128)).T

    tokens = tok_mask[...].astype(F32)
    tok_t[...] = column(tokens)
    live[...] = pair_mask[...].astype(F32) * tok_t[at(a, 32), :] * tokens
    live_t[...] = tn(live[...].astype(BF), unit[:32, :32]).astype(BF)
    for gain, row in ((g1, gain1), (g2, gain2), (g3, gain3)):
        gain[...] = column(row[...])
    w1[:, 0:256] = tri_in[:, 0:256]
    w1[:, 256:384] = tri_gate[...]
    w1[:, 384:640] = tri_in[:, 256:512]
    for b in range(5):
        w1t[128 * b : 128 * b + 128, :] = flip(w1[:, lanes(b)]).astype(BF)
    for b in range(4):
        wat[128 * b : 128 * b + 128, :] = flip(att_in[:, lanes(b)]).astype(BF)
    wot[...] = flip(att_out[...]).astype(BF)
    woutt[...] = flip(tri_out[...]).astype(BF)
    wbt[...] = jnp.concatenate([att_bias[...].astype(F32), jnp.zeros((12, 128), F32)], axis=0).astype(BF)
    wb[...] = flip(wbt[...]).astype(BF)
    tab[...] = jnp.zeros_like(tab)
    tab[:, 0:4, 0:4] = table[...]
    hot[...] = (lax.broadcasted_iota(jnp.int32, (16, 128), 0) == tok_types[...]).astype(F32)

    def alive_of(i):
        return jnp.concatenate([live[pl.ds(i, 1), :], live[pl.ds(i + 1, 1), :]], axis=1)


    def edge(kind, c):
        block = right.at[cross if kind == 2 else a]
        spot = block.at[8 * c : 8 * c + 8] if c < 2 else block.at[16:32, 64 * (c - 2) : 64 * (c - 1), :]
        return pltpu.make_async_remote_copy(
            src_ref=spot, dst_ref=spot, send_sem=sem_es.at[kind, c], recv_sem=sem_er.at[kind, c],
            device_id={"dap": cross if kind == 1 else partner}, device_id_type=MESH)

    def project(t):
        i = 2 * t
        hat, _ = norm_cols(flipped(slab, i))
        n = (hat * twice(g1[...])).astype(BF)
        q = mm(w1t[...], n)
        alive = alive_of(i)
        sa, sb = jax.nn.sigmoid(q[128:256]), jax.nn.sigmoid(q[512:])
        lft = (sa * q[:128] * alive).astype(BF).astype(F32)
        rgt = (sb * q[384:512] * alive).astype(BF)
        gate = jax.nn.sigmoid(q[256:384])
        for r in range(2):
            normed[i + r] = n[:, lanes(r)]
            left_f[at(i + r, 128), :] = lft[:, lanes(r)]
            right[a, i + r] = rgt[:, lanes(r)]
            gates[i + r] = gate[:, lanes(r)]
            pieces[i + r, 0:128] = q[:128, lanes(r)]
            pieces[i + r, 128:256] = sa[:, lanes(r)]
            pieces[i + r, 256:384] = q[384:512, lanes(r)]
            pieces[i + r, 384:512] = sb[:, lanes(r)]

    loop(4, project, 2)
    pl.semaphore_wait(barrier, 3 + n_dp - 1)
    for c, (low_t, high_t) in enumerate(((0, 0), (4, 8), (8, 16), (0, 0))):
        if high_t > low_t:
            loop(high_t, project, 2, first=low_t)
        edge(1, c).start()
        edge(0, c).start()

    def unpack(block, base, rows=(0, 32), chans=(0, 128)):
        span = slice(*chans)

        def one(j):
            start = pl.multiple_of((base + j) * 128 + chans[0], 64)
            right_f[pl.ds(start, chans[1] - chans[0]), :] = right[block, j, span].astype(F32)

        loop(rows[1], one, 4, first=rows[0])

    def multiply(half, chans=(0, 128)):
        def one(ch):
            lft = left_f[pl.ds(ch, 32, stride=128), :].astype(BF)
            rgt = right_f[pl.ds(64 * 128 * half + ch, 64, stride=128), :].astype(BF)
            prod[at(ch, 32), 64 * half : 64 * half + 64] = nt(lft, rgt)
        loop(chans[1], one, 16, first=chans[0])

    for c in range(4):
        edge(0, c).wait_recv()
    low = 2 * chip
    unpack(low, 0)
    unpack(low + 1, 32)
    multiply(0)

    beside = cross + 1 - 2 * core
    for c in range(4):
        rows, chans = ((8 * c, 8 * c + 8), (0, 128)) if c < 2 else ((16, 32), (64 * (c - 2), 64 * (c - 1)))
        edge(1, c).wait_recv()
        edge(2, c).start()
        unpack(cross, 64 + 32 * core, rows, chans)
        edge(2, c).wait_recv()
        unpack(beside, 96 - 32 * core, rows, chans)
        if c >= 2:
            multiply(1, chans)

    def second(t):
        i = 2 * t
        xs = []
        for r in range(2):
            rows = pl.ds(i + r, 128, stride=32)
            x = pltpu.roll(prod[rows, :], 64 * chip, axis=1)
            prod[rows, :] = x
            xs.append(x)
        hat, _ = norm_cols(jnp.concatenate(xs, axis=1))
        n = (hat * twice(g2[...])).astype(BF)
        middle = (flipped(slab, i) + pair(gates, i) * mm(woutt[...], n)).astype(BF)
        hat, _ = norm_cols(middle.astype(F32))
        n = (hat * twice(g3[...])).astype(BF)
        heads = mm(wbt[...], n)
        for r in range(2):
            mid[i + r] = middle[:, lanes(r)]
            for h in range(4):
                bias_f[h, pl.ds(i + r, 1), :] = heads[h : h + 1, lanes(r)]

    loop(16, second, 4)
    bias_b[...] = bias_f[...].astype(BF)

    def share_bias(r):
        return pltpu.make_async_remote_copy(
            src_ref=bias_b, dst_ref=bias.at[:, at(a, 32), :], send_sem=sem_is.at[r - 1], recv_sem=sem_ir.at[r - 1],
            device_id={"dap": lax.rem(a + r, 4)}, device_id_type=MESH)

    for r in (2, 1, 3):
        share_bias(r).start()
    bias[:, at(a, 32), :] = bias_b[...]
    for h in range(4):
        near_types = mm(tab[h].T, hot[...], EXACT)
        bt[:, lanes(h)] = tn(hot[...], near_types, EXACT)
    for ref in (d_bias, d_wa, d_wo, d_wout, d_wb, d_w1, gain_sum):
        ref[...] = jnp.zeros_like(ref)
    for r in (1, 2, 3):
        share_bias(r).wait_recv()
    for h in range(4):
        bt[:, lanes(h)] += flip(bias[h])


    def spread(x, h0):
        zero = jnp.zeros((32, 128), x.dtype)
        cols = [
            jnp.concatenate([x[32 * h : 32 * h + 32] if g == h else zero for g in range(4)], axis=0)
            for h in range(h0, h0 + GROUP)
        ]
        return jnp.concatenate(cols, axis=1)

    scale = 32.0 ** -0.5

    def attend(t):
        i = 2 * t
        m = pair(mid, i).astype(F32)
        hat, _ = norm_cols(m)
        n = (hat * twice(g3[...])).astype(BF)
        q3 = mm(wat[...], n)
        qkv = q3[:384].astype(BF)
        gate = jax.nn.sigmoid(q3[384:])
        ct = flipped(cot, i).astype(BF)
        d_gated = mm(att_out[...], ct).astype(BF).astype(F32)
        d_att = d_gated * gate
        picked = lax.broadcasted_iota(jnp.int32, (32, 256), 0) == (
            i + lax.broadcasted_iota(jnp.int32, (32, 256), 1) // 128)
        alive = mm(live_t[...], picked.astype(F32).astype(BF))
        both = range(2)
        qs, ks, vs = ([qkv[128 * x : 128 * x + 128, lanes(r)] for r in both] for x in range(3))
        kvs = [flip(qkv[128:384, lanes(r)]).astype(BF) for r in both]
        dos = [d_att[:, lanes(r)].astype(BF) for r in both]
        scores = [mm(kvs[r][:, :128], spread(qs[r], 0)) for r in both]
        das = [mm(kvs[r][:, 128:], spread(dos[r], 0)).astype(BF) for r in both]
        exps = [
            jnp.exp(scores[r] * scale + bt[...]) * jnp.concatenate([alive[:, lanes(r)]] * 4, axis=1) for r in both
        ]
        sums = [jnp.sum(e, axis=0, keepdims=True) for e in exps]
        ws = [e * (1.0 / jnp.maximum(s, 1.0)) for e, s in zip(exps, sums)]
        abs_ = [w.astype(BF) for w in ws]
        us = [da.astype(F32) * w for da, w in zip(das, ws)]
        totals = [jnp.sum(u, axis=0, keepdims=True) for u in us]
        totals = [
            jnp.where(s > 1.0, x, jnp.where(s == 1.0, 0.5 * x, 0.0)) for s, x in zip(sums, totals)
        ]
        dss = [u - w * x for u, w, x in zip(us, ws, totals)]
        d_bias[...] += dss[0] + dss[1]
        dsbs = [ds.astype(BF) for ds in dss]

        def heads_of(fn):
            return jnp.concatenate([fn(slice(32 * h, 32 * h + 32), lanes(h)) for h in range(4)], axis=0)

        atts = [heads_of(lambda h, l: mm(vs[r][h], abs_[r][:, l])) for r in both]
        dvs = [heads_of(lambda h, l: nt(dos[r][h], abs_[r][:, l])) for r in both]
        dks = [heads_of(lambda h, l: nt(qs[r][h], dsbs[r][:, l])) * scale for r in both]
        dqs = [heads_of(lambda h, l: mm(ks[r][h], dsbs[r][:, l])) * scale for r in both]
        parts = [jnp.concatenate([dqs[r], dks[r], dvs[r]], axis=0).astype(BF) for r in both]
        att = jnp.concatenate(atts, axis=1)
        d_open = (d_gated * att * gate * (1.0 - gate)).astype(BF)
        dp = jnp.concatenate([jnp.concatenate(parts, axis=1), d_open], axis=0)
        dn = mm(att_in[...], dp).astype(BF)
        d_wa[...] += nt(dp, n)
        gated = (gate * att).astype(BF)
        d_wo[...] += nt(gated, ct)
        res = (m + mm(wot[...], gated)).astype(BF)
        for r in range(2):
            dn3[i + r] = dn[:, lanes(r)]
            out[i + r] = flip(res[:, lanes(r)]).astype(BF)

    loop(16, attend, 2)

    for h in range(4):
        db_n[h] = flip(d_bias[:, lanes(h)].astype(BF)).astype(BF)

    def share_grad(r):
        peer = lax.rem(a + r, 4)
        return pltpu.make_async_remote_copy(
            src_ref=db_n.at[:, at(peer, 32), :], dst_ref=db_in.at[r - 1], send_sem=sem_bs.at[r - 1],
            recv_sem=sem_br.at[r - 1], device_id={"dap": peer}, device_id_type=MESH)

    for r in (2, 1, 3):
        share_grad(r).start()
    early.g[0:512, :] = d_wa[...].astype(BF)
    early.g[512:640, :] = d_wo[...].astype(BF)
    early.g[640:, :] = jnp.zeros((384, 128), BF)
    for h in range(4):
        near_types = mm(hot[...], d_bias[:, lanes(h)])
        early.g[640 + 16 * h : 656 + 16 * h, 0:16] = nt(hot[...], near_types).astype(BF)
    early.start_a()

    for r in (1, 2, 3):
        share_grad(r).wait_recv()
    total = db_n[:, at(a, 32), :].astype(F32)
    for r in range(3):
        total = total + db_in[r].astype(F32)
    db_f[...] = total


    def fold(x):
        return x[:, :128] + x[:, 128:]

    def second_back(t):
        i = 2 * t
        hat3, scale3 = norm_cols(pair(mid, i).astype(F32))
        gain3, gain2 = twice(g3[...]), twice(g2[...])
        n3 = (hat3 * gain3).astype(BF)
        rows = [
            jnp.concatenate([db_f[h, pl.ds(i, 1), :], db_f[h, pl.ds(i + 1, 1), :]], axis=1) for h in range(4)
        ]
        db = jnp.concatenate(rows + [jnp.zeros((12, 256), F32)], axis=0).astype(BF)
        dn = pair(dn3, i).astype(F32) + mm(wb[...], db)
        d_wb[...] += nt(db, n3)
        gain_sum[2] += fold(dn * hat3)
        dm = flipped(cot, i).astype(BF) + norm_back(dn * gain3, hat3, scale3).astype(BF)
        dmf = dm.astype(F32)
        x = jnp.concatenate([prod[pl.ds(i, 128, stride=32), :], prod[pl.ds(i + 1, 128, stride=32), :]], axis=1)
        hat2, scale2 = norm_cols(x)
        n2 = (hat2 * gain2).astype(BF)
        z = mm(woutt[...], n2)
        gate = pair(gates, i)
        dz = (dmf * gate).astype(BF)
        d_open = (dmf * z * gate * (1.0 - gate)).astype(BF)
        d_wout[...] += nt(n2, dz)
        dn2 = mm(tri_out[...], dz).astype(BF).astype(F32)
        gain_sum[1] += fold(dn2 * hat2)
        dp = norm_back(dn2 * gain2, hat2, scale2)
        for r in range(2):
            d_prod[pl.ds(i + r, 128, stride=32), :] = pltpu.roll(dp[:, lanes(r)], 64 * chip, axis=1)
            d_mid[i + r] = dm[:, lanes(r)]
            d_gate[i + r] = d_open[:, lanes(r)]

    loop(16, second_back, 4)
    early.start_b()

    def chunk(ref, q):
        return ref.at[:, at(q, 32), :]

    def move(kind, q):
        src, dst, peer = (
            (far.at[1 - core], far_in, partner), (sent, cross_in, cross), (near.at[1 - core], near_in, partner),
        )[kind]
        return pltpu.make_async_remote_copy(
            src_ref=chunk(src, q), dst_ref=chunk(dst, q), send_sem=sem_s.at[kind, q], recv_sem=sem_r.at[kind, q],
            device_id={"dap": peer}, device_id_type=MESH)

    def right_grads(half, q, store):
        def one(c):
            ch = 32 * q + c
            dp = d_prod[at(ch, 32), 64 * half : 64 * half + 64].astype(BF)
            work[pl.ds(c, 64, stride=32), :] = tn(dp, left_f[pl.ds(ch, 32, stride=128), :].astype(BF))

        loop(32, one, 16)

        def pack(j):
            store[j // 32, lax.rem(j, 32), at(q, 32), :] = work[at(j, 32), :].astype(BF)

        loop(64, pack, 4)

    def add_on(q):
        move(0, q).wait_recv()

        def one(j):
            spot = at(q, 32)
            sent[j, spot, :] = (far[core, j, spot, :].astype(F32) + far_in[j, spot, :].astype(F32)).astype(BF)

        loop(32, one, 4)
        move(1, q).start()

    def out_far(q):
        right_grads(1, q, far)
        move(0, q).start()
        pl.when(q > 0)(lambda: add_on(q - 1))

    loop(4, out_far)

    def out_near(q):
        right_grads(0, q, near)
        move(2, q).start()
        pl.when(q == 0)(lambda: add_on(3))

    loop(4, out_near)
    early.start_c()

    def left_grad(ch):
        rgt = right_f[pl.ds(ch, 128, stride=128), :].astype(BF)
        left_f[pl.ds(ch, 32, stride=128), :] = mm(d_prod[at(ch, 32), :].astype(BF), rgt)

    loop(128, left_grad, 16)

    def sides(grad_in, x, s, alive):
        g = grad_in * alive * s
        return g, g * x * (1.0 - s)

    def stored(i, k):
        rows = slice(128 * k, 128 * k + 128)
        return jnp.concatenate([pieces[i, rows], pieces[i + 1, rows]], axis=1)

    def left_part(t):
        i = 2 * t
        dl = jnp.concatenate([left_f[at(i, 128), :], left_f[at(i + 1, 128), :]], axis=1).astype(BF).astype(F32)
        dpa, dga = sides(dl, stored(i, 0), stored(i, 1), alive_of(i))
        dp = jnp.concatenate([dpa.astype(BF), dga.astype(BF), pair(d_gate, i)], axis=0)
        d_w1[0:384, :] += nt(dp, pair(normed, i))
        dn = mm(w1[:, 0:384], dp)
        part[i] = dn[:, :128]
        part[i + 1] = dn[:, 128:]

    loop(16, left_part, 4)

    loop(4, lambda q: move(2, q).wait_recv())
    loop(4, lambda q: move(1, q).wait_recv())
    early.start_d()

    def right_part(t):
        i = 2 * t

        def summed(j):
            x = near[core, j].astype(F32) + near_in[j].astype(F32) + cross_in[j].astype(F32)
            return x.astype(BF).astype(F32)

        dr = jnp.concatenate([summed(i), summed(i + 1)], axis=1)
        dpb, dgb = sides(dr, stored(i, 2), stored(i, 3), alive_of(i))
        dp = jnp.concatenate([dpb.astype(BF), dgb.astype(BF)], axis=0)
        d_w1[384:640, :] += nt(dp, pair(normed, i))
        dn = (pair(part, i) + mm(w1[:, 384:640], dp)).astype(BF).astype(F32)
        hat, spread_1 = norm_cols(flipped(slab, i))
        gain_sum[0] += fold(dn * hat)
        dx = norm_back(dn * twice(g1[...]), hat, spread_1).astype(BF)
        res = pair(d_mid, i) + dx
        grad[i] = flip(res[:, :128]).astype(BF)
        grad[i + 1] = flip(res[:, 128:]).astype(BF)

    loop(16, right_part, 4)


    late.g[0:640, :] = d_w1[...].astype(BF)
    late.g[640:768, :] = d_wout[...].astype(BF)
    late.g[768:784, :] = d_wb[...].astype(BF)
    late.g[784:, :] = jnp.zeros((240, 128), BF)
    ones = jnp.ones((16, 128), F32)
    for k in range(3):
        late.g[784 + 16 * k : 800 + 16 * k, :] = nt(ones, gain_sum[k], EXACT).astype(BF)
    late.start_a()
    early.finish()
    for b in range(4):
        o_att_in[:, lanes(b)] = flip(early.full[128 * b : 128 * b + 128, :])
    o_att_out[...] = early.full[512:640, :].astype(F32)
    for h in range(4):
        o_table[h] = early.full[640 + 16 * h : 656 + 16 * h, :].astype(F32)[0:4, 0:4]
    late.start_b()
    early.settle()
    late.start_c()
    for r in (1, 2, 3):
        share_bias(r).wait_send()
        share_grad(r).wait_send()
    for kind in range(3):
        for c in range(4):
            edge(kind, c).wait_send()
        loop(4, lambda q: move(kind, q).wait_send())
    late.start_d()
    late.finish()
    for b, source in enumerate((0, 1, 3, 4)):
        o_tri_in[:, lanes(b)] = flip(late.full[128 * source : 128 * source + 128, :])
    o_tri_gate[...] = flip(late.full[256:384, :])
    o_tri_out[...] = late.full[640:768, :].astype(F32)
    o_att_bias[...] = late.full[768:784, :].astype(F32)[0:4, :]
    for k, ref in enumerate((o_gain1, o_gain2, o_gain3)):
        ref[...] = late.full[784 + 16 * k : 800 + 16 * k, :].astype(F32)[0:1, :]
    late.settle()


def hand_over(*refs):
    held, sems = refs[2 * N_OUT : 3 * N_OUT], refs[3 * N_OUT]
    parts = [(k, pl.ds(8 * c, 8), 4 * k + c) for k in range(2) for c in range(4)]
    parts += [(k, slice(None), 6 + k) for k in range(2, N_OUT)]
    reads = [pltpu.make_async_copy(refs[k].at[s], held[k].at[s], sems.at[0, n]) for k, s, n in parts]
    writes = [pltpu.make_async_copy(held[k].at[s], refs[N_OUT + k].at[s], sems.at[1, n]) for k, s, n in parts]
    for copy in reads:
        copy.start()
    for read, write in zip(reads, writes):
        read.wait()
        write.start()
    for copy in writes:
        copy.wait()


def per_device(*args):
    pair_rep, cotangent, tok_mask, tok_types, pair_mask = args[:5]
    params = [v[None] if v.ndim == 1 else v for v in args[5:]]
    params[6] = params[6].T
    n_dp = lax.axis_size("dp")
    factor = (128 * 128 * n_dp) ** (-0.5)
    block = (32, 128, 128)
    shapes = [v.shape for v in params]
    spec = pl.BlockSpec(memory_space=VM)
    scratch = Sum.scratch(n_dp) * 2 + [
        VM((32, 128), F32), VM((128, 32), BF), VM((128, 128), F32),
        VM((128, 128), F32), VM((128, 128), F32), VM((128, 128), F32),
        VM((128, 640), BF), VM((640, 128), BF), VM((512, 128), BF), VM((128, 128), BF), VM((128, 128), BF),
        VM((128, 16), BF), VM((16, 128), BF), VM((16, 128), F32), VM((4, 16, 16), F32), VM((128, 512), F32),
        VM(block, BF), VM(block, BF), VM((4096, 128), F32), VM((4,) + block, BF), VM((4096, 128), F32),
        VM((16384, 128), F32), VM(block, F32), VM((32, 512, 128), F32), VM(block, BF),
        VM((4, 32, 128), F32), VM((4, 32, 128), BF), VM((4, 128, 128), BF),
        VM((128, 512), F32), VM((512, 128), F32), VM((128, 128), F32), VM((128, 128), F32), VM((16, 128), F32),
        VM((640, 128), F32), VM((3, 128, 128), F32),
        VM((4, 128, 128), BF), VM((3, 4, 32, 128), BF), VM((4, 32, 128), F32), VM((4096, 128), F32),
        VM(block, BF), VM(block, BF), VM((2048, 128), F32),
        VM((2,) + block, BF), VM(block, BF), VM(block, BF), VM(block, BF), VM((2,) + block, BF), VM(block, BF),
        DMA((3, 4)), DMA((3, 4)), DMA((3,)), DMA((3,)), DMA((3,)), DMA((3,)), DMA((3, 4)), DMA((3, 4)),
    ]
    results = pl.pallas_call(
        partial(kernel, n_dp, factor),
        out_shape=[jax.ShapeDtypeStruct(block, BF)] * 2 + [jax.ShapeDtypeStruct(s, F32) for s in shapes],
        in_specs=[spec] * N_IN,
        out_specs=[spec] * N_OUT,
        scratch_shapes=scratch,
        compiler_params=pltpu.CompilerParams(collective_id=0, has_side_effects=True, vmem_limit_bytes=63 << 20),
        name="pairformer",
    )(pair_rep[0], cotangent[0], tok_mask, tok_types, pair_mask[0], *params)
    anywhere = pl.BlockSpec(memory_space=pl.ANY)
    results = pl.pallas_call(
        hand_over,
        out_shape=[jax.ShapeDtypeStruct(r.shape, r.dtype) for r in results],
        in_specs=[anywhere] * N_OUT,
        out_specs=[anywhere] * N_OUT,
        scratch_shapes=[VM(r.shape, r.dtype) for r in results] + [DMA((2, N_OUT + 6))],
        name="hand_over",
    )(*results)
    results = list(results)
    results[8] = results[8].T
    return tuple(
        [results[0][None], results[1][None]]
        + [r[0] if v.ndim == 1 else r for r, v in zip(results[2:], args[5:])]
    )


def solution(mesh):
    return jax.shard_map(
        per_device,
        mesh=mesh,
        in_specs=(
            P("dp", "dap", None, None),
            P("dp", "dap", None, None),
            P("dp", None),
            P("dp", None),
            P("dp", "dap", None),
            P(),
            P(),
            P(),
            P(),
            P(),
            P(),
            P(),
            P(),
            P(),
            P(),
        ),
        out_specs=(
            P("dp", "dap", None, None),
            P("dp", "dap", None, None),
            P(),
            P(),
            P(),
            P(),
            P(),
            P(),
            P(),
            P(),
            P(),
            P(),
        ),
        check_vma=False,
    )
```

```python
from functools import partial

import jax
import jax.numpy as jnp
from jax import lax
from jax.experimental import pallas as pl
from jax.experimental.pallas import tpu as pltpu
from jax.sharding import PartitionSpec as P

EPSILON = 1e-05
MESH = pl.DeviceIdType.MESH
VM = pltpu.VMEM
DMA = pltpu.SemaphoreType.DMA
BF = jnp.bfloat16
F32 = jnp.float32
EXACT = lax.Precision.HIGHEST


def contract(x, y, dims, precision=None):
    return lax.dot_general(x, y, (dims, ((), ())), precision=precision, preferred_element_type=F32)


def mm(x, y, precision=None):
    return contract(x, y, ((1,), (0,)), precision)


def nt(x, y, precision=None):
    return contract(x, y, ((1,), (1,)), precision)


def tn(x, y, precision=None):
    return contract(x, y, ((0,), (0,)), precision)


def norm_cols(x):
    mean = jnp.sum(x, axis=0, keepdims=True) * (1.0 / 128)
    centred = x - mean
    spread = jnp.sum(centred * centred, axis=0, keepdims=True) * (1.0 / 128)
    scale = lax.rsqrt(spread + EPSILON)
    return centred * scale, scale


def norm_back(grad, unit, scale):
    a = jnp.sum(grad, axis=0, keepdims=True) * (1.0 / 128)
    b = jnp.sum(grad * unit, axis=0, keepdims=True) * (1.0 / 128)
    return scale * (grad - a - unit * b)


def loop(n, fn, unroll=1, first=0):
    def body(i, carry):
        fn(i)
        return carry
    lax.fori_loop(first, n, body, 0, unroll=unroll)


def at(i, size):
    return pl.ds(pl.multiple_of(i * size, size), size)


def halves(x):
    return x[:, :128], x[:, 128:]


def twice(x):
    return jnp.concatenate([x, x], axis=1)


def pair(ref, i):
    return jnp.concatenate([ref[i], ref[i + 1]], axis=1)


def lanes(r):
    return slice(128 * r, 128 * r + 128)


class Sum:
    def __init__(self, n_dp, factor, a, p, refs):
        self.n_dp, self.factor, self.a, self.p = n_dp, factor, a, p
        self.partner, self.cross = a + 1 - 2 * lax.rem(a, 2), lax.rem(a + 2, 4)
        (self.g, self.part, self.quarter, self.pieces, self.mine, self.joined, self.joined_b, self.full,
         self.sa, self.ra, self.sb, self.rb, self.sc, self.rc, self.sd, self.rd) = refs
        self.size = 256 // n_dp

    def remote(self, src, dst, s, r, **peer):
        return pltpu.make_async_remote_copy(
            src_ref=src, dst_ref=dst, send_sem=s, recv_sem=r, device_id=peer, device_id_type=MESH)

    def copy_a(self, r):
        peer = lax.rem(self.a + r, 4)
        return self.remote(self.g.at[at(peer, 256)], self.part.at[r - 1], self.sa.at[r - 1], self.ra.at[r - 1], dap=peer)

    def copy_b(self, r):
        peer = lax.rem(self.p + r, self.n_dp)
        return self.remote(
            self.quarter.at[at(peer, self.size)], self.pieces.at[r - 1], self.sb, self.rb, dp=peer)

    def copy_c(self, r):
        peer = lax.rem(self.p + r, self.n_dp)
        return self.remote(self.mine, self.joined.at[at(self.p, self.size)], self.sc, self.rc, dp=peer)

    def all_of(self, ref, s, r):
        return self.remote(ref, ref, s, r, dp=lax.rem(self.p + 1, self.n_dp))

    def others(self, ref):
        return ref.at[pl.ds(0, (self.n_dp - 1) * self.size)]

    def copy_d(self, k):
        there = at(self.cross if k == 2 else self.a, 256)
        src = self.full.at[there] if k == 2 else self.joined_b
        return self.remote(
            src, self.full.at[there], self.sd.at[k], self.rd.at[k], dap=self.cross if k == 0 else self.partner)

    def start_a(self):
        for r in (2, 1, 3):
            self.copy_a(r).start()

    def start_b(self):
        total = self.g[at(self.a, 256), :].astype(F32)
        for r in (1, 2, 3):
            self.copy_a(r).wait_recv()
            total = total + self.part[r - 1].astype(F32)
        self.quarter[...] = total
        for r in range(1, self.n_dp):
            self.copy_b(r).start()

    def start_c(self):
        self.all_of(self.pieces, self.sb, self.rb).wait_recv()
        total = self.quarter[at(self.p, self.size), :] + jnp.sum(self.pieces[...], axis=0)
        self.mine[...] = total * self.factor
        for r in range(1, self.n_dp):
            self.copy_c(r).start()
        self.joined[at(self.p, self.size), :] = self.mine[...]

    def start_d(self):
        self.all_of(self.others(self.joined), self.sc, self.rc).wait_recv()
        self.joined_b[...] = self.joined[...].astype(BF)
        self.copy_d(0).start()
        self.copy_d(1).start()
        self.full[at(self.a, 256), :] = self.joined_b[...]

    def finish(self):
        self.copy_d(0).wait_recv()
        self.copy_d(2).start()
        self.copy_d(1).wait_recv()
        self.copy_d(2).wait_recv()

    def settle(self):
        for r in (1, 2, 3):
            self.copy_a(r).wait_send()
        self.all_of(self.pieces, self.sb, self.rb).wait_send()
        self.all_of(self.others(self.joined), self.sc, self.rc).wait_send()
        for k in range(3):
            self.copy_d(k).wait_send()

    @staticmethod
    def scratch(n_dp):
        size = 256 // n_dp
        return [
            VM((1024, 128), BF), VM((3, 256, 128), BF), VM((256, 128), F32), VM((n_dp - 1, size, 128), F32),
            VM((size, 128), F32), VM((256, 128), F32), VM((256, 128), BF), VM((1024, 128), BF),
        ] + [DMA((3,))] * 2 + [DMA] * 4 + [DMA((3,))] * 2


N_IN, N_OUT, N_SUM = 15, 12, 16
STRIP, SPLIT = 16, 8


def kernel(n_dp, factor, *refs):
    (slab, cot, tok_mask, tok_types, pair_mask, gain1, tri_in, tri_gate, gain2, tri_out, gain3, att_bias, att_in,
     att_out, table) = refs[:N_IN]
    (out, grad, o_gain1, o_tri_in, o_tri_gate, o_gain2, o_tri_out, o_gain3, o_att_bias, o_att_in, o_att_out,
     o_table) = refs[N_IN : N_IN + N_OUT]
    rest = refs[N_IN + N_OUT :]
    a, p = lax.axis_index("dap"), lax.axis_index("dp")
    partner, cross, chip, core = a + 1 - 2 * lax.rem(a, 2), lax.rem(a + 2, 4), a // 2, lax.rem(a, 2)
    early = Sum(n_dp, factor, a, p, rest[:N_SUM])
    late = Sum(n_dp, factor, a, p, rest[N_SUM : 2 * N_SUM])
    (live, live_t, tok_t, g1, g2, g3, w1, w1t, wat, wot, woutt, wb, wbt, hot, tab, bt,
     mid, dn3, prod, right, left_f, right_f, gates, pieces, normed, bias_f, bias_b, bias,
     d_bias, d_wa, d_wo, d_wout, d_wb, d_w1, gain_sum,
     db_n, db_in, db_f, d_prod, d_mid, d_gate, work, far, far_in, sent, cross_in, near, near_in,
     slab_t, cot_t, d_gated_t, scales, sem_es, sem_er, sem_is, sem_ir, sem_bs, sem_br, sem_s, sem_r) = rest[2 * N_SUM :]
    part = gates

    barrier = pltpu.get_barrier_semaphore()
    for r in range(1, 4):
        pl.semaphore_signal(barrier, inc=1, device_id={"dap": lax.rem(a + r, 4)}, device_id_type=MESH)
    for r in range(1, n_dp):
        pl.semaphore_signal(barrier, inc=1, device_id={"dp": lax.rem(p + r, n_dp)}, device_id_type=MESH)

    rows_i = lax.broadcasted_iota(jnp.int32, (128, 128), 0)
    unit = (rows_i == lax.broadcasted_iota(jnp.int32, (128, 128), 1)).astype(F32).astype(BF)

    def flip(block):
        return nt(unit, block)

    def flipped(ref, i):
        return jnp.concatenate([flip(ref[i]), flip(ref[i + 1])], axis=1)

    def column(row):
        return jnp.broadcast_to(row, (128, 128)).T

    tokens = tok_mask[...].astype(F32)
    tok_t[...] = column(tokens)
    live[...] = pair_mask[...].astype(F32) * tok_t[at(a, 32), :] * tokens
    live_t[...] = tn(live[...].astype(BF), unit[:32, :32]).astype(BF)
    for gain, row in ((g1, gain1), (g2, gain2), (g3, gain3)):
        gain[...] = column(row[...])
    w1[:, 0:256] = tri_in[:, 0:256]
    w1[:, 256:384] = tri_gate[...]
    w1[:, 384:640] = tri_in[:, 256:512]
    for b in range(5):
        w1t[128 * b : 128 * b + 128, :] = flip(w1[:, lanes(b)]).astype(BF)
    for b in range(4):
        wat[128 * b : 128 * b + 128, :] = flip(att_in[:, lanes(b)]).astype(BF)
    wot[...] = flip(att_out[...]).astype(BF)
    woutt[...] = flip(tri_out[...]).astype(BF)
    wbt[...] = jnp.concatenate([att_bias[...].astype(F32), jnp.zeros((12, 128), F32)], axis=0).astype(BF)
    wb[...] = flip(wbt[...]).astype(BF)
    tab[...] = jnp.zeros_like(tab)
    tab[:, 0:4, 0:4] = table[...]
    hot[...] = (lax.broadcasted_iota(jnp.int32, (16, 128), 0) == tok_types[...]).astype(F32)

    def alive_of(i):
        return jnp.concatenate([live[pl.ds(i, 1), :], live[pl.ds(i + 1, 1), :]], axis=1)


    def edge(kind, c):
        block = right.at[cross if kind == 2 else a]
        spot = block.at[8 * c : 8 * c + 8] if c < 2 else block.at[16:32, 64 * (c - 2) : 64 * (c - 1), :]
        return pltpu.make_async_remote_copy(
            src_ref=spot, dst_ref=spot, send_sem=sem_es.at[kind, c], recv_sem=sem_er.at[kind, c],
            device_id={"dap": cross if kind == 1 else partner}, device_id_type=MESH)

    def project(t):
        i = 2 * t
        x = flipped(slab, i)
        hat, _ = norm_cols(x)
        n = (hat * twice(g1[...])).astype(BF)
        q = mm(w1t[...], n)
        alive = alive_of(i)
        sa, sb = jax.nn.sigmoid(q[128:256]), jax.nn.sigmoid(q[512:])
        fa, fb = sa * alive, sb * alive
        lft, rgt = fa * q[:128], fb * q[384:512]
        ga, gb = lft * (1.0 - sa), rgt * (1.0 - sb)
        lft, rgt = lft.astype(BF).astype(F32), rgt.astype(BF)
        x = x.astype(BF)
        gate = jax.nn.sigmoid(q[256:384])
        for r in range(2):
            normed[i + r] = n[:, lanes(r)]
            slab_t[i + r] = x[:, lanes(r)]
            left_f[at(i + r, 128), :] = lft[:, lanes(r)]
            right[a, i + r] = rgt[:, lanes(r)]
            gates[i + r] = gate[:, lanes(r)]
            pieces[i + r, 0:128] = fa[:, lanes(r)]
            pieces[i + r, 128:256] = ga[:, lanes(r)]
            pieces[i + r, 256:384] = fb[:, lanes(r)]
            pieces[i + r, 384:512] = gb[:, lanes(r)]

    loop(4, project, 2)
    pl.semaphore_wait(barrier, 3 + n_dp - 1)
    for c, (low_t, high_t) in enumerate(((0, 0), (4, 8), (8, 16), (0, 0))):
        if high_t > low_t:
            loop(high_t, project, 2, first=low_t)
        edge(1, c).start()
        edge(0, c).start()

    def unpack(block, base, rows=(0, 32), chans=(0, 128)):
        span = slice(*chans)

        def one(j):
            start = pl.multiple_of((base + j) * 128 + chans[0], 64)
            right_f[pl.ds(start, chans[1] - chans[0]), :] = right[block, j, span].astype(F32)

        loop(rows[1], one, 4, first=rows[0])

    def multiply(half, chans=(0, 128)):
        def one(ch):
            lft = left_f[pl.ds(ch, 32, stride=128), :].astype(BF)
            rgt = right_f[pl.ds(64 * 128 * half + ch, 64, stride=128), :].astype(BF)
            prod[at(ch, 32), 64 * half : 64 * half + 64] = nt(lft, rgt)
        loop(chans[1], one, 16, first=chans[0])

    for c in range(4):
        edge(0, c).wait_recv()
    low = 2 * chip
    unpack(low, 0)
    unpack(low + 1, 32)
    multiply(0)

    def prepare(t):
        i = 2 * t
        ct = flipped(cot, i).astype(BF)
        dg = mm(att_out[...], ct).astype(BF)
        for r in range(2):
            cot_t[i + r] = ct[:, lanes(r)]
            d_gated_t[i + r] = dg[:, lanes(r)]

    loop(16, prepare, 4)

    beside = cross + 1 - 2 * core
    for c in range(4):
        rows, chans = ((8 * c, 8 * c + 8), (0, 128)) if c < 2 else ((16, 32), (64 * (c - 2), 64 * (c - 1)))
        edge(1, c).wait_recv()
        edge(2, c).start()
        unpack(cross, 64 + 32 * core, rows, chans)
        edge(2, c).wait_recv()
        unpack(beside, 96 - 32 * core, rows, chans)
        if c >= 2:
            multiply(1, chans)

    def second(t):
        i = 2 * t
        xs = []
        for r in range(2):
            rows = pl.ds(i + r, 128, stride=32)
            x = pltpu.roll(prod[rows, :], 64 * chip, axis=1)
            prod[rows, :] = x
            xs.append(x)
        hat, _ = norm_cols(jnp.concatenate(xs, axis=1))
        n = (hat * twice(g2[...])).astype(BF)
        middle = (pair(slab_t, i).astype(F32) + pair(gates, i) * mm(woutt[...], n)).astype(BF)
        hat, _ = norm_cols(middle.astype(F32))
        n = (hat * twice(g3[...])).astype(BF)
        heads = mm(wbt[...], n)
        for r in range(2):
            mid[i + r] = middle[:, lanes(r)]
            for h in range(4):
                bias_f[h, pl.ds(i + r, 1), :] = heads[h : h + 1, lanes(r)]

    loop(16, second, 4)
    bias_b[...] = bias_f[...].astype(BF)

    def share_bias(r):
        return pltpu.make_async_remote_copy(
            src_ref=bias_b, dst_ref=bias.at[:, at(a, 32), :], send_sem=sem_is.at[r - 1], recv_sem=sem_ir.at[r - 1],
            device_id={"dap": lax.rem(a + r, 4)}, device_id_type=MESH)

    for r in (2, 1, 3):
        share_bias(r).start()
    bias[:, at(a, 32), :] = bias_b[...]
    for h in range(4):
        near_types = mm(tab[h].T, hot[...], EXACT)
        bt[:, lanes(h)] = tn(hot[...], near_types, EXACT)
    for ref in (d_bias, d_wa, d_wo, d_wout, d_wb, d_w1, gain_sum):
        ref[...] = jnp.zeros_like(ref)
    for r in (1, 2, 3):
        share_bias(r).wait_recv()
    for h in range(4):
        bt[:, lanes(h)] += flip(bias[h])


    def spread(x):
        zero = jnp.zeros((32, 128), x.dtype)
        cols = [
            jnp.concatenate([x[32 * h : 32 * h + 32] if g == h else zero for g in range(4)], axis=0)
            for h in range(4)
        ]
        return jnp.concatenate(cols, axis=1)

    scale = 32.0 ** -0.5

    def attend(t):
        i = 2 * t
        m = pair(mid, i).astype(F32)
        hat, _ = norm_cols(m)
        n = (hat * twice(g3[...])).astype(BF)
        q3 = mm(wat[...], n)
        qkv = q3[:384].astype(BF)
        gate = jax.nn.sigmoid(q3[384:])
        ct = pair(cot_t, i)
        d_gated = pair(d_gated_t, i).astype(F32)
        d_att = d_gated * gate
        picked = lax.broadcasted_iota(jnp.int32, (32, 256), 0) == (
            i + lax.broadcasted_iota(jnp.int32, (32, 256), 1) // 128)
        alive = mm(live_t[...], picked.astype(F32).astype(BF))
        both = range(2)
        qs, ks, vs = ([qkv[128 * x : 128 * x + 128, lanes(r)] for r in both] for x in range(3))
        kvs = [flip(qkv[128:384, lanes(r)]).astype(BF) for r in both]
        dos = [d_att[:, lanes(r)].astype(BF) for r in both]
        scores = [mm(kvs[r][:, :128], spread(qs[r])) for r in both]
        das = [mm(kvs[r][:, 128:], spread(dos[r])).astype(BF) for r in both]
        exps = [
            jnp.exp(scores[r] * scale + bt[...]) * jnp.concatenate([alive[:, lanes(r)]] * 4, axis=1) for r in both
        ]
        sums = [jnp.sum(e, axis=0, keepdims=True) for e in exps]
        ws = [e * (1.0 / jnp.maximum(s, 1.0)) for e, s in zip(exps, sums)]
        abs_ = [w.astype(BF) for w in ws]
        us = [da.astype(F32) * w for da, w in zip(das, ws)]
        totals = [jnp.sum(u, axis=0, keepdims=True) for u in us]
        totals = [
            jnp.where(s > 1.0, x, jnp.where(s == 1.0, 0.5 * x, 0.0)) for s, x in zip(sums, totals)
        ]
        dss = [u - w * x for u, w, x in zip(us, ws, totals)]
        d_bias[...] += dss[0] + dss[1]
        dsbs = [ds.astype(BF) for ds in dss]

        def heads_of(fn):
            return jnp.concatenate([fn(slice(32 * h, 32 * h + 32), lanes(h)) for h in range(4)], axis=0)

        atts = [heads_of(lambda h, l: mm(vs[r][h], abs_[r][:, l])) for r in both]
        dvs = [heads_of(lambda h, l: nt(dos[r][h], abs_[r][:, l])) for r in both]
        dks = [heads_of(lambda h, l: nt(qs[r][h], dsbs[r][:, l])) * scale for r in both]
        dqs = [heads_of(lambda h, l: mm(ks[r][h], dsbs[r][:, l])) * scale for r in both]
        parts = [jnp.concatenate([dqs[r], dks[r], dvs[r]], axis=0).astype(BF) for r in both]
        att = jnp.concatenate(atts, axis=1)
        d_open = (d_gated * att * gate * (1.0 - gate)).astype(BF)
        dp = jnp.concatenate([jnp.concatenate(parts, axis=1), d_open], axis=0)
        dn = mm(att_in[...], dp).astype(BF)
        d_wa[...] += nt(dp, n)
        gated = (gate * att).astype(BF)
        d_wo[...] += nt(gated, ct)
        res = (m + mm(wot[...], gated)).astype(BF)
        for r in range(2):
            dn3[i + r] = dn[:, lanes(r)]
            out[i + r] = flip(res[:, lanes(r)]).astype(BF)

    loop(16, attend, 2)

    for h in range(4):
        db_n[h] = flip(d_bias[:, lanes(h)].astype(BF)).astype(BF)

    def share_grad(r):
        peer = lax.rem(a + r, 4)
        return pltpu.make_async_remote_copy(
            src_ref=db_n.at[:, at(peer, 32), :], dst_ref=db_in.at[r - 1], send_sem=sem_bs.at[r - 1],
            recv_sem=sem_br.at[r - 1], device_id={"dap": peer}, device_id_type=MESH)

    for r in (2, 1, 3):
        share_grad(r).start()
    early.g[0:512, :] = d_wa[...].astype(BF)
    early.g[512:640, :] = d_wo[...].astype(BF)
    early.g[640:, :] = jnp.zeros((384, 128), BF)
    for h in range(4):
        near_types = mm(hot[...], d_bias[:, lanes(h)])
        early.g[640 + 16 * h : 656 + 16 * h, 0:16] = nt(hot[...], near_types).astype(BF)
    early.start_a()

    for r in (1, 2, 3):
        share_grad(r).wait_recv()
    total = db_n[:, at(a, 32), :].astype(F32)
    for r in range(3):
        total = total + db_in[r].astype(F32)
    db_f[...] = total


    def fold(x):
        return x[:, :128] + x[:, 128:]

    def second_back(t):
        i = 2 * t
        hat3, scale3 = norm_cols(pair(mid, i).astype(F32))
        gain3, gain2 = twice(g3[...]), twice(g2[...])
        n3 = (hat3 * gain3).astype(BF)
        rows = [
            jnp.concatenate([db_f[h, pl.ds(i, 1), :], db_f[h, pl.ds(i + 1, 1), :]], axis=1) for h in range(4)
        ]
        db = jnp.concatenate(rows + [jnp.zeros((12, 256), F32)], axis=0).astype(BF)
        dn = pair(dn3, i).astype(F32) + mm(wb[...], db)
        d_wb[...] += nt(db, n3)
        gain_sum[2] += fold(dn * hat3)
        dm = pair(cot_t, i) + norm_back(dn * gain3, hat3, scale3).astype(BF)
        dmf = dm.astype(F32)
        x = jnp.concatenate([prod[pl.ds(i, 128, stride=32), :], prod[pl.ds(i + 1, 128, stride=32), :]], axis=1)
        hat2, scale2 = norm_cols(x)
        n2 = (hat2 * gain2).astype(BF)
        z = mm(woutt[...], n2)
        gate = pair(gates, i)
        dz = (dmf * gate).astype(BF)
        d_open = (dmf * z * gate * (1.0 - gate)).astype(BF)
        d_wout[...] += nt(n2, dz)
        dn2 = mm(tri_out[...], dz).astype(BF).astype(F32)
        gain_sum[1] += fold(dn2 * hat2)
        dp = norm_back(dn2 * gain2, hat2, scale2)
        for r in range(2):
            d_prod[pl.ds(i + r, 128, stride=32), :] = pltpu.roll(dp[:, lanes(r)], 64 * chip, axis=1)
            d_mid[i + r] = dm[:, lanes(r)]
            d_gate[i + r] = d_open[:, lanes(r)]

    loop(16, second_back, 4)
    early.start_b()

    def chunk(ref, q):
        return ref.at[:, at(q, STRIP), :]

    def move(kind, q):
        src, dst, peer = (
            (far.at[1 - core], far_in, partner), (sent, cross_in, cross), (near.at[1 - core], near_in, partner),
        )[kind]
        return pltpu.make_async_remote_copy(
            src_ref=chunk(src, q), dst_ref=chunk(dst, q), send_sem=sem_s.at[kind, q], recv_sem=sem_r.at[kind, q],
            device_id={"dap": peer}, device_id_type=MESH)

    def right_grads(half, q, store):
        def one(c):
            ch = STRIP * q + c
            dp = d_prod[at(ch, 32), 64 * half : 64 * half + 64].astype(BF)
            work[pl.ds(c, 64, stride=STRIP), :] = tn(dp, left_f[pl.ds(ch, 32, stride=128), :].astype(BF))

        loop(STRIP, one, 16)

        def pack(j):
            store[j // 32, lax.rem(j, 32), at(q, STRIP), :] = work[at(j, STRIP), :].astype(BF)

        loop(64, pack, 8)

    def add_on(q):
        move(0, q).wait_recv()

        def one(j):
            spot = at(q, STRIP)
            sent[j, spot, :] = (far[core, j, spot, :].astype(F32) + far_in[j, spot, :].astype(F32)).astype(BF)

        loop(32, one, 8)
        move(1, q).start()

    def out_far(q):
        right_grads(1, q, far)
        move(0, q).start()
        pl.when(q > 0)(lambda: add_on(q - 1))

    loop(SPLIT, out_far)

    def out_near(q):
        right_grads(0, q, near)
        move(2, q).start()
        pl.when(q == 0)(lambda: add_on(SPLIT - 1))

    loop(SPLIT, out_near)
    early.start_c()

    def left_grad(ch):
        rgt = right_f[pl.ds(ch, 128, stride=128), :].astype(BF)
        left_f[pl.ds(ch, 32, stride=128), :] = mm(d_prod[at(ch, 32), :].astype(BF), rgt)

    loop(128, left_grad, 16)

    def stored(i, k):
        rows = slice(128 * k, 128 * k + 128)
        return jnp.concatenate([pieces[i, rows], pieces[i + 1, rows]], axis=1)

    def left_part(t):
        i = 2 * t
        dl = jnp.concatenate([left_f[at(i, 128), :], left_f[at(i + 1, 128), :]], axis=1).astype(BF).astype(F32)
        dp = jnp.concatenate(
            [(dl * stored(i, 0)).astype(BF), (dl * stored(i, 1)).astype(BF), pair(d_gate, i)], axis=0)
        d_w1[0:384, :] += nt(dp, pair(normed, i))
        dn = mm(w1[:, 0:384], dp)
        part[i] = dn[:, :128]
        part[i + 1] = dn[:, 128:]

    loop(16, left_part, 4)

    loop(SPLIT, lambda q: move(2, q).wait_recv())

    def settle_near(t):
        i = 2 * t
        hat, scale_1 = norm_cols(pair(slab_t, i).astype(F32))
        for r in range(2):
            right_f[at(i + r, 128), :] = near[core, i + r].astype(F32) + near_in[i + r].astype(F32)
            right_f[at(32 + i + r, 128), :] = hat[:, lanes(r)]
            scales[pl.ds(i + r, 1), :] = scale_1[:, lanes(r)]

    loop(16, settle_near, 2)
    loop(SPLIT, lambda q: move(1, q).wait_recv())
    early.start_d()

    def right_part(t):
        i = 2 * t

        def held(j):
            return jnp.concatenate([right_f[at(j, 128), :], right_f[at(j + 1, 128), :]], axis=1)

        dr = (held(i) + pair(cross_in, i).astype(F32)).astype(BF).astype(F32)
        dp = jnp.concatenate([(dr * stored(i, 2)).astype(BF), (dr * stored(i, 3)).astype(BF)], axis=0)
        d_w1[384:640, :] += nt(dp, pair(normed, i))
        dn = (pair(part, i) + mm(w1[:, 384:640], dp)).astype(BF).astype(F32)
        hat = held(32 + i)
        spread_1 = jnp.concatenate([scales[pl.ds(i, 1), :], scales[pl.ds(i + 1, 1), :]], axis=1)
        gain_sum[0] += fold(dn * hat)
        dx = norm_back(dn * twice(g1[...]), hat, spread_1).astype(BF)
        res = pair(d_mid, i) + dx
        grad[i] = flip(res[:, :128]).astype(BF)
        grad[i + 1] = flip(res[:, 128:]).astype(BF)

    loop(16, right_part, 4)


    late.g[0:640, :] = d_w1[...].astype(BF)
    late.g[640:768, :] = d_wout[...].astype(BF)
    late.g[768:784, :] = d_wb[...].astype(BF)
    late.g[784:, :] = jnp.zeros((240, 128), BF)
    ones = jnp.ones((16, 128), F32)
    for k in range(3):
        late.g[784 + 16 * k : 800 + 16 * k, :] = nt(ones, gain_sum[k], EXACT).astype(BF)
    late.start_a()
    early.finish()
    for b in range(4):
        o_att_in[:, lanes(b)] = flip(early.full[128 * b : 128 * b + 128, :])
    o_att_out[...] = early.full[512:640, :].astype(F32)
    for h in range(4):
        o_table[h] = early.full[640 + 16 * h : 656 + 16 * h, :].astype(F32)[0:4, 0:4]
    late.start_b()
    early.settle()
    late.start_c()
    for r in (1, 2, 3):
        share_bias(r).wait_send()
        share_grad(r).wait_send()
    for kind in range(3):
        for c in range(4):
            edge(kind, c).wait_send()
        loop(SPLIT, lambda q: move(kind, q).wait_send())
    late.start_d()
    late.finish()
    for b, source in enumerate((0, 1, 3, 4)):
        o_tri_in[:, lanes(b)] = flip(late.full[128 * source : 128 * source + 128, :])
    o_tri_gate[...] = flip(late.full[256:384, :])
    o_tri_out[...] = late.full[640:768, :].astype(F32)
    o_att_bias[...] = late.full[768:784, :].astype(F32)[0:4, :]
    for k, ref in enumerate((o_gain1, o_gain2, o_gain3)):
        ref[...] = late.full[784 + 16 * k : 800 + 16 * k, :].astype(F32)[0:1, :]
    late.settle()


def hand_over(*refs):
    held, sems = refs[2 * N_OUT : 3 * N_OUT], refs[3 * N_OUT]
    parts = [(k, pl.ds(8 * c, 8), 4 * k + c) for k in range(2) for c in range(4)]
    parts += [(k, slice(None), 6 + k) for k in range(2, N_OUT)]
    reads = [pltpu.make_async_copy(refs[k].at[s], held[k].at[s], sems.at[0, n]) for k, s, n in parts]
    writes = [pltpu.make_async_copy(held[k].at[s], refs[N_OUT + k].at[s], sems.at[1, n]) for k, s, n in parts]
    for copy in reads:
        copy.start()
    for read, write in zip(reads, writes):
        read.wait()
        write.start()
    for copy in writes:
        copy.wait()


def per_device(*args):
    pair_rep, cotangent, tok_mask, tok_types, pair_mask = args[:5]
    params = [v[None] if v.ndim == 1 else v for v in args[5:]]
    params[6] = params[6].T
    n_dp = lax.axis_size("dp")
    factor = (128 * 128 * n_dp) ** (-0.5)
    block = (32, 128, 128)
    shapes = [v.shape for v in params]
    spec = pl.BlockSpec(memory_space=VM)
    scratch = Sum.scratch(n_dp) * 2 + [
        VM((32, 128), F32), VM((128, 32), BF), VM((128, 128), F32),
        VM((128, 128), F32), VM((128, 128), F32), VM((128, 128), F32),
        VM((128, 640), BF), VM((640, 128), BF), VM((512, 128), BF), VM((128, 128), BF), VM((128, 128), BF),
        VM((128, 16), BF), VM((16, 128), BF), VM((16, 128), F32), VM((4, 16, 16), F32), VM((128, 512), F32),
        VM(block, BF), VM(block, BF), VM((4096, 128), F32), VM((4,) + block, BF), VM((4096, 128), F32),
        VM((16384, 128), F32), VM(block, F32), VM((32, 512, 128), F32), VM(block, BF),
        VM((4, 32, 128), F32), VM((4, 32, 128), BF), VM((4, 128, 128), BF),
        VM((128, 512), F32), VM((512, 128), F32), VM((128, 128), F32), VM((128, 128), F32), VM((16, 128), F32),
        VM((640, 128), F32), VM((3, 128, 128), F32),
        VM((4, 128, 128), BF), VM((3, 4, 32, 128), BF), VM((4, 32, 128), F32), VM((4096, 128), F32),
        VM(block, BF), VM(block, BF), VM((64 * STRIP, 128), F32),
        VM((2,) + block, BF), VM(block, BF), VM(block, BF), VM(block, BF), VM((2,) + block, BF), VM(block, BF),
        VM(block, BF), VM(block, BF), VM(block, BF), VM((32, 128), F32),
        DMA((3, 4)), DMA((3, 4)), DMA((3,)), DMA((3,)), DMA((3,)), DMA((3,)), DMA((3, SPLIT)), DMA((3, SPLIT)),
    ]
    results = pl.pallas_call(
        partial(kernel, n_dp, factor),
        out_shape=[jax.ShapeDtypeStruct(block, BF)] * 2 + [jax.ShapeDtypeStruct(s, F32) for s in shapes],
        in_specs=[spec] * N_IN,
        out_specs=[spec] * N_OUT,
        scratch_shapes=scratch,
        compiler_params=pltpu.CompilerParams(collective_id=0, has_side_effects=True, vmem_limit_bytes=63 << 20),
        name="pairformer",
    )(pair_rep[0], cotangent[0], tok_mask, tok_types, pair_mask[0], *params)
    anywhere = pl.BlockSpec(memory_space=pl.ANY)
    results = pl.pallas_call(
        hand_over,
        out_shape=[jax.ShapeDtypeStruct(r.shape, r.dtype) for r in results],
        in_specs=[anywhere] * N_OUT,
        out_specs=[anywhere] * N_OUT,
        scratch_shapes=[VM(r.shape, r.dtype) for r in results] + [DMA((2, N_OUT + 6))],
        name="hand_over",
    )(*results)
    results = list(results)
    results[8] = results[8].T
    return tuple(
        [results[0][None], results[1][None]]
        + [r[0] if v.ndim == 1 else r for r, v in zip(results[2:], args[5:])]
    )


def solution(mesh):
    return jax.shard_map(
        per_device,
        mesh=mesh,
        in_specs=(
            P("dp", "dap", None, None),
            P("dp", "dap", None, None),
            P("dp", None),
            P("dp", None),
            P("dp", "dap", None),
            P(),
            P(),
            P(),
            P(),
            P(),
            P(),
            P(),
            P(),
            P(),
            P(),
        ),
        out_specs=(
            P("dp", "dap", None, None),
            P("dp", "dap", None, None),
            P(),
            P(),
            P(),
            P(),
            P(),
            P(),
            P(),
            P(),
            P(),
            P(),
        ),
        check_vma=False,
    )
```

```python
from functools import partial

import jax
import jax.numpy as jnp
from jax import lax
from jax.experimental import pallas as pl
from jax.experimental.pallas import tpu as pltpu
from jax.sharding import PartitionSpec as P

EPSILON = 1e-05
MESH = pl.DeviceIdType.MESH
VM = pltpu.VMEM
DMA = pltpu.SemaphoreType.DMA
BF = jnp.bfloat16
F32 = jnp.float32
EXACT = lax.Precision.HIGHEST


def contract(x, y, dims, precision=None):
    return lax.dot_general(x, y, (dims, ((), ())), precision=precision, preferred_element_type=F32)


def mm(x, y, precision=None):
    return contract(x, y, ((1,), (0,)), precision)


def nt(x, y, precision=None):
    return contract(x, y, ((1,), (1,)), precision)


def tn(x, y, precision=None):
    return contract(x, y, ((0,), (0,)), precision)


def norm_cols(x):
    mean = jnp.sum(x, axis=0, keepdims=True) * (1.0 / 128)
    centred = x - mean
    spread = jnp.sum(centred * centred, axis=0, keepdims=True) * (1.0 / 128)
    scale = lax.rsqrt(spread + EPSILON)
    return centred * scale, scale


def norm_back(grad, unit, scale):
    a = jnp.sum(grad, axis=0, keepdims=True) * (1.0 / 128)
    b = jnp.sum(grad * unit, axis=0, keepdims=True) * (1.0 / 128)
    return scale * (grad - a - unit * b)


def loop(n, fn, unroll=1, first=0):
    def body(i, carry):
        fn(i)
        return carry
    lax.fori_loop(first, n, body, 0, unroll=unroll)


def at(i, size):
    return pl.ds(pl.multiple_of(i * size, size), size)


def halves(x):
    return x[:, :128], x[:, 128:]


def twice(x):
    return jnp.concatenate([x, x], axis=1)


def pair(ref, i):
    return jnp.concatenate([ref[i], ref[i + 1]], axis=1)


def lanes(r):
    return slice(128 * r, 128 * r + 128)


class Sum:
    def __init__(self, n_dp, factor, a, p, refs):
        self.n_dp, self.factor, self.a, self.p = n_dp, factor, a, p
        self.partner, self.cross = a + 1 - 2 * lax.rem(a, 2), lax.rem(a + 2, 4)
        (self.g, self.part, self.quarter, self.pieces, self.mine, self.joined, self.joined_b, self.full,
         self.sa, self.ra, self.sb, self.rb, self.sc, self.rc, self.sd, self.rd) = refs
        self.size = 256 // n_dp

    def remote(self, src, dst, s, r, **peer):
        return pltpu.make_async_remote_copy(
            src_ref=src, dst_ref=dst, send_sem=s, recv_sem=r, device_id=peer, device_id_type=MESH)

    def copy_a(self, r):
        peer = lax.rem(self.a + r, 4)
        return self.remote(self.g.at[at(peer, 256)], self.part.at[r - 1], self.sa.at[r - 1], self.ra.at[r - 1], dap=peer)

    def copy_b(self, r):
        peer = lax.rem(self.p + r, self.n_dp)
        return self.remote(
            self.quarter.at[at(peer, self.size)], self.pieces.at[r - 1], self.sb, self.rb, dp=peer)

    def copy_c(self, r):
        peer = lax.rem(self.p + r, self.n_dp)
        return self.remote(self.mine, self.joined.at[at(self.p, self.size)], self.sc, self.rc, dp=peer)

    def all_of(self, ref, s, r):
        return self.remote(ref, ref, s, r, dp=lax.rem(self.p + 1, self.n_dp))

    def others(self, ref):
        return ref.at[pl.ds(0, (self.n_dp - 1) * self.size)]

    def copy_d(self, k):
        there = at(self.cross if k == 2 else self.a, 256)
        src = self.full.at[there] if k == 2 else self.joined_b
        return self.remote(
            src, self.full.at[there], self.sd.at[k], self.rd.at[k], dap=self.cross if k == 0 else self.partner)

    def start_a(self):
        for r in (2, 1, 3):
            self.copy_a(r).start()

    def start_b(self):
        total = self.g[at(self.a, 256), :].astype(F32)
        for r in (1, 2, 3):
            self.copy_a(r).wait_recv()
            total = total + self.part[r - 1].astype(F32)
        self.quarter[...] = total
        for r in range(1, self.n_dp):
            self.copy_b(r).start()

    def start_c(self):
        self.all_of(self.pieces, self.sb, self.rb).wait_recv()
        total = self.quarter[at(self.p, self.size), :] + jnp.sum(self.pieces[...], axis=0)
        self.mine[...] = total * self.factor
        for r in range(1, self.n_dp):
            self.copy_c(r).start()
        self.joined[at(self.p, self.size), :] = self.mine[...]

    def start_d(self):
        self.all_of(self.others(self.joined), self.sc, self.rc).wait_recv()
        self.joined_b[...] = self.joined[...].astype(BF)
        self.copy_d(0).start()
        self.copy_d(1).start()
        self.full[at(self.a, 256), :] = self.joined_b[...]

    def finish(self):
        self.copy_d(0).wait_recv()
        self.copy_d(2).start()
        self.copy_d(1).wait_recv()
        self.copy_d(2).wait_recv()

    def settle(self):
        for r in (1, 2, 3):
            self.copy_a(r).wait_send()
        self.all_of(self.pieces, self.sb, self.rb).wait_send()
        self.all_of(self.others(self.joined), self.sc, self.rc).wait_send()
        for k in range(3):
            self.copy_d(k).wait_send()

    @staticmethod
    def scratch(n_dp):
        size = 256 // n_dp
        return [
            VM((1024, 128), BF), VM((3, 256, 128), BF), VM((256, 128), F32), VM((n_dp - 1, size, 128), F32),
            VM((size, 128), F32), VM((256, 128), F32), VM((256, 128), BF), VM((1024, 128), BF),
        ] + [DMA((3,))] * 2 + [DMA] * 4 + [DMA((3,))] * 2


N_IN, N_OUT, N_SUM = 15, 12, 16
STRIP, SPLIT = 16, 8


def kernel(n_dp, factor, *refs):
    (slab, cot, tok_mask, tok_types, pair_mask, gain1, tri_in, tri_gate, gain2, tri_out, gain3, att_bias, att_in,
     att_out, table) = refs[:N_IN]
    (out, grad, o_gain1, o_tri_in, o_tri_gate, o_gain2, o_tri_out, o_gain3, o_att_bias, o_att_in, o_att_out,
     o_table) = refs[N_IN : N_IN + N_OUT]
    rest = refs[N_IN + N_OUT :]
    a, p = lax.axis_index("dap"), lax.axis_index("dp")
    partner, cross, chip, core = a + 1 - 2 * lax.rem(a, 2), lax.rem(a + 2, 4), a // 2, lax.rem(a, 2)
    early = Sum(n_dp, factor, a, p, rest[:N_SUM])
    late = Sum(n_dp, factor, a, p, rest[N_SUM : 2 * N_SUM])
    (live, live_t, tok_t, g1, g2, g3, w1, w1t, wat, wot, woutt, wb, wbt, hot, tab, bt,
     mid, dn3, prod, right, left_f, right_f, gates, pieces, normed, bias_f, bias_b, bias,
     d_bias, d_wa, d_wo, d_wout, d_wb, d_w1, gain_sum,
     db_n, db_in, db_f, d_prod, d_mid, d_gate, work, far, far_in, sent, cross_in, near, near_in,
     slab_t, cot_t, d_gated_t, scales, zs, sem_es, sem_er, sem_is, sem_ir, sem_bs, sem_br, sem_s, sem_r) = rest[2 * N_SUM :]
    part = gates

    barrier = pltpu.get_barrier_semaphore()
    for r in range(1, 4):
        pl.semaphore_signal(barrier, inc=1, device_id={"dap": lax.rem(a + r, 4)}, device_id_type=MESH)
    for r in range(1, n_dp):
        pl.semaphore_signal(barrier, inc=1, device_id={"dp": lax.rem(p + r, n_dp)}, device_id_type=MESH)

    rows_i = lax.broadcasted_iota(jnp.int32, (128, 128), 0)
    unit = (rows_i == lax.broadcasted_iota(jnp.int32, (128, 128), 1)).astype(F32).astype(BF)

    def flip(block):
        return nt(unit, block)

    def flipped(ref, i):
        return jnp.concatenate([flip(ref[i]), flip(ref[i + 1])], axis=1)

    def column(row):
        return jnp.broadcast_to(row, (128, 128)).T

    tokens = tok_mask[...].astype(F32)
    tok_t[...] = column(tokens)
    live[...] = pair_mask[...].astype(F32) * tok_t[at(a, 32), :] * tokens
    live_t[...] = tn(live[...].astype(BF), unit[:32, :32]).astype(BF)
    for gain, row in ((g1, gain1), (g2, gain2), (g3, gain3)):
        gain[...] = column(row[...])
    w1[:, 0:256] = tri_in[:, 0:256]
    w1[:, 256:384] = tri_gate[...]
    w1[:, 384:640] = tri_in[:, 256:512]
    for b in range(5):
        w1t[128 * b : 128 * b + 128, :] = flip(w1[:, lanes(b)]).astype(BF)
    for b in range(4):
        wat[128 * b : 128 * b + 128, :] = flip(att_in[:, lanes(b)]).astype(BF)
    wot[...] = flip(att_out[...]).astype(BF)
    woutt[...] = flip(tri_out[...]).astype(BF)
    wbt[...] = jnp.concatenate([att_bias[...].astype(F32), jnp.zeros((12, 128), F32)], axis=0).astype(BF)
    wb[...] = flip(wbt[...]).astype(BF)
    tab[...] = jnp.zeros_like(tab)
    tab[:, 0:4, 0:4] = table[...]
    hot[...] = (lax.broadcasted_iota(jnp.int32, (16, 128), 0) == tok_types[...]).astype(F32)

    def alive_of(i):
        return jnp.concatenate([live[pl.ds(i, 1), :], live[pl.ds(i + 1, 1), :]], axis=1)


    def edge(kind, c):
        block = right.at[cross if kind == 2 else a]
        spot = block.at[8 * c : 8 * c + 8] if c < 2 else block.at[16:32, 64 * (c - 2) : 64 * (c - 1), :]
        return pltpu.make_async_remote_copy(
            src_ref=spot, dst_ref=spot, send_sem=sem_es.at[kind, c], recv_sem=sem_er.at[kind, c],
            device_id={"dap": cross if kind == 1 else partner}, device_id_type=MESH)

    def project(t):
        i = 2 * t
        x = flipped(slab, i)
        hat, _ = norm_cols(x)
        n = (hat * twice(g1[...])).astype(BF)
        q = mm(w1t[...], n)
        alive = alive_of(i)
        sa, sb = jax.nn.sigmoid(q[128:256]), jax.nn.sigmoid(q[512:])
        fa, fb = sa * alive, sb * alive
        lft, rgt = fa * q[:128], fb * q[384:512]
        ga, gb = lft * (1.0 - sa), rgt * (1.0 - sb)
        lft, rgt = lft.astype(BF).astype(F32), rgt.astype(BF)
        x = x.astype(BF)
        gate = jax.nn.sigmoid(q[256:384])
        for r in range(2):
            normed[i + r] = n[:, lanes(r)]
            slab_t[i + r] = x[:, lanes(r)]
            left_f[pl.ds((i + r) * 129, 128), :] = lft[:, lanes(r)]
            right[a, i + r] = rgt[:, lanes(r)]
            gates[i + r] = gate[:, lanes(r)]
            pieces[i + r, 0:128] = fa[:, lanes(r)]
            pieces[i + r, 128:256] = ga[:, lanes(r)]
            pieces[i + r, 256:384] = fb[:, lanes(r)]
            pieces[i + r, 384:512] = gb[:, lanes(r)]

    loop(4, project, 2)
    pl.semaphore_wait(barrier, 3 + n_dp - 1)
    for c, (low_t, high_t) in enumerate(((0, 0), (4, 8), (8, 16), (0, 0))):
        if high_t > low_t:
            loop(high_t, project, 2, first=low_t)
        edge(1, c).start()
        edge(0, c).start()

    def unpack(block, base, rows=(0, 32), chans=(0, 128)):
        span = slice(*chans)

        def one(j):
            start = (base + j) * 129 + chans[0]
            right_f[pl.ds(start, chans[1] - chans[0]), :] = right[block, j, span].astype(F32)

        loop(rows[1], one, 4, first=rows[0])

    def multiply(half, chans=(0, 128)):
        def one(ch):
            lft = left_f[pl.ds(ch, 32, stride=129), :].astype(BF)
            rgt = right_f[pl.ds(64 * 129 * half + ch, 64, stride=129), :].astype(BF)
            prod[pl.ds(ch * 33, 32), 64 * half : 64 * half + 64] = nt(lft, rgt)
        loop(chans[1], one, 16, first=chans[0])

    for c in range(4):
        edge(0, c).wait_recv()
    low = 2 * chip
    unpack(low, 0)
    unpack(low + 1, 32)
    multiply(0)

    def prepare(t):
        i = 2 * t
        ct = flipped(cot, i).astype(BF)
        dg = mm(att_out[...], ct).astype(BF)
        for r in range(2):
            cot_t[i + r] = ct[:, lanes(r)]
            d_gated_t[i + r] = dg[:, lanes(r)]

    loop(16, prepare, 4)

    beside = cross + 1 - 2 * core
    for c in range(4):
        rows, chans = ((8 * c, 8 * c + 8), (0, 128)) if c < 2 else ((16, 32), (64 * (c - 2), 64 * (c - 1)))
        edge(1, c).wait_recv()
        edge(2, c).start()
        unpack(cross, 64 + 32 * core, rows, chans)
        edge(2, c).wait_recv()
        unpack(beside, 96 - 32 * core, rows, chans)
        if c >= 2:
            multiply(1, chans)

    def second(t):
        i = 2 * t
        xs = []
        for r in range(2):
            rows = pl.ds(i + r, 128, stride=33)
            xs.append(pltpu.roll(prod[rows, :], 64 * chip, axis=1))
        hat, scale_2 = norm_cols(jnp.concatenate(xs, axis=1))
        n = (hat * twice(g2[...])).astype(BF)
        z = mm(woutt[...], n)
        for r in range(2):
            prod[pl.ds(i + r, 128, stride=33), :] = hat[:, lanes(r)]
            scales[pl.ds(32 + i + r, 1), :] = scale_2[:, lanes(r)]
            zs[i + r] = z[:, lanes(r)]
        middle = (pair(slab_t, i).astype(F32) + pair(gates, i) * z).astype(BF)
        hat, _ = norm_cols(middle.astype(F32))
        n = (hat * twice(g3[...])).astype(BF)
        heads = mm(wbt[...], n)
        for r in range(2):
            mid[i + r] = middle[:, lanes(r)]
            for h in range(4):
                bias_f[h, pl.ds(i + r, 1), :] = heads[h : h + 1, lanes(r)]

    loop(16, second, 4)
    bias_b[...] = bias_f[...].astype(BF)

    def share_bias(r):
        return pltpu.make_async_remote_copy(
            src_ref=bias_b, dst_ref=bias.at[:, at(a, 32), :], send_sem=sem_is.at[r - 1], recv_sem=sem_ir.at[r - 1],
            device_id={"dap": lax.rem(a + r, 4)}, device_id_type=MESH)

    for r in (2, 1, 3):
        share_bias(r).start()
    bias[:, at(a, 32), :] = bias_b[...]
    for h in range(4):
        near_types = mm(tab[h].T, hot[...], EXACT)
        bt[:, lanes(h)] = tn(hot[...], near_types, EXACT)
    for ref in (d_bias, d_wa, d_wo, d_wout, d_wb, d_w1, gain_sum):
        ref[...] = jnp.zeros_like(ref)
    for r in (1, 2, 3):
        share_bias(r).wait_recv()
    for h in range(4):
        bt[:, lanes(h)] += flip(bias[h])


    def spread(x):
        zero = jnp.zeros((32, 128), x.dtype)
        cols = [
            jnp.concatenate([x[32 * h : 32 * h + 32] if g == h else zero for g in range(4)], axis=0)
            for h in range(4)
        ]
        return jnp.concatenate(cols, axis=1)

    scale = 32.0 ** -0.5

    def attend(t):
        i = 2 * t
        m = pair(mid, i).astype(F32)
        hat, _ = norm_cols(m)
        n = (hat * twice(g3[...])).astype(BF)
        q3 = mm(wat[...], n)
        qkv = q3[:384].astype(BF)
        gate = jax.nn.sigmoid(q3[384:])
        ct = pair(cot_t, i)
        d_gated = pair(d_gated_t, i).astype(F32)
        d_att = d_gated * gate
        picked = lax.broadcasted_iota(jnp.int32, (32, 256), 0) == (
            i + lax.broadcasted_iota(jnp.int32, (32, 256), 1) // 128)
        alive = mm(live_t[...], picked.astype(F32).astype(BF))
        both = range(2)
        qs, ks, vs = ([qkv[128 * x : 128 * x + 128, lanes(r)] for r in both] for x in range(3))
        kvs = [flip(qkv[128:384, lanes(r)]).astype(BF) for r in both]
        dos = [d_att[:, lanes(r)].astype(BF) for r in both]
        scores = [mm(kvs[r][:, :128], spread(qs[r])) for r in both]
        das = [mm(kvs[r][:, 128:], spread(dos[r])).astype(BF) for r in both]
        exps = [
            jnp.exp(scores[r] * scale + bt[...]) * jnp.concatenate([alive[:, lanes(r)]] * 4, axis=1) for r in both
        ]
        sums = [jnp.sum(e, axis=0, keepdims=True) for e in exps]
        ws = [e * (1.0 / jnp.maximum(s, 1.0)) for e, s in zip(exps, sums)]
        abs_ = [w.astype(BF) for w in ws]
        us = [da.astype(F32) * w for da, w in zip(das, ws)]
        totals = [jnp.sum(u, axis=0, keepdims=True) for u in us]
        totals = [
            jnp.where(s > 1.0, x, jnp.where(s == 1.0, 0.5 * x, 0.0)) for s, x in zip(sums, totals)
        ]
        dss = [u - w * x for u, w, x in zip(us, ws, totals)]
        d_bias[...] += dss[0] + dss[1]
        dsbs = [ds.astype(BF) for ds in dss]

        def heads_of(fn):
            return jnp.concatenate([fn(slice(32 * h, 32 * h + 32), lanes(h)) for h in range(4)], axis=0)

        atts = [heads_of(lambda h, l: mm(vs[r][h], abs_[r][:, l])) for r in both]
        dvs = [heads_of(lambda h, l: nt(dos[r][h], abs_[r][:, l])) for r in both]
        dks = [heads_of(lambda h, l: nt(qs[r][h], dsbs[r][:, l])) * scale for r in both]
        dqs = [heads_of(lambda h, l: mm(ks[r][h], dsbs[r][:, l])) * scale for r in both]
        parts = [jnp.concatenate([dqs[r], dks[r], dvs[r]], axis=0).astype(BF) for r in both]
        att = jnp.concatenate(atts, axis=1)
        d_open = (d_gated * att * gate * (1.0 - gate)).astype(BF)
        dp = jnp.concatenate([jnp.concatenate(parts, axis=1), d_open], axis=0)
        dn = mm(att_in[...], dp).astype(BF)
        d_wa[...] += nt(dp, n)
        gated = (gate * att).astype(BF)
        d_wo[...] += nt(gated, ct)
        res = (m + mm(wot[...], gated)).astype(BF)
        for r in range(2):
            dn3[i + r] = dn[:, lanes(r)]
            out[i + r] = flip(res[:, lanes(r)]).astype(BF)

    loop(16, attend, 4)

    for h in range(4):
        db_n[h] = flip(d_bias[:, lanes(h)].astype(BF)).astype(BF)

    def share_grad(r):
        peer = lax.rem(a + r, 4)
        return pltpu.make_async_remote_copy(
            src_ref=db_n.at[:, at(peer, 32), :], dst_ref=db_in.at[r - 1], send_sem=sem_bs.at[r - 1],
            recv_sem=sem_br.at[r - 1], device_id={"dap": peer}, device_id_type=MESH)

    for r in (2, 1, 3):
        share_grad(r).start()
    early.g[0:512, :] = d_wa[...].astype(BF)
    early.g[512:640, :] = d_wo[...].astype(BF)
    early.g[640:, :] = jnp.zeros((384, 128), BF)
    for h in range(4):
        near_types = mm(hot[...], d_bias[:, lanes(h)])
        early.g[640 + 16 * h : 656 + 16 * h, 0:16] = nt(hot[...], near_types).astype(BF)
    early.start_a()

    for r in (1, 2, 3):
        share_grad(r).wait_recv()
    total = db_n[:, at(a, 32), :].astype(F32)
    for r in range(3):
        total = total + db_in[r].astype(F32)
    db_f[...] = total


    def fold(x):
        return x[:, :128] + x[:, 128:]

    def second_back(t):
        i = 2 * t
        hat3, scale3 = norm_cols(pair(mid, i).astype(F32))
        gain3, gain2 = twice(g3[...]), twice(g2[...])
        n3 = (hat3 * gain3).astype(BF)
        rows = [
            jnp.concatenate([db_f[h, pl.ds(i, 1), :], db_f[h, pl.ds(i + 1, 1), :]], axis=1) for h in range(4)
        ]
        db = jnp.concatenate(rows + [jnp.zeros((12, 256), F32)], axis=0).astype(BF)
        dn = pair(dn3, i).astype(F32) + mm(wb[...], db)
        d_wb[...] += nt(db, n3)
        gain_sum[2] += fold(dn * hat3)
        dm = pair(cot_t, i) + norm_back(dn * gain3, hat3, scale3).astype(BF)
        dmf = dm.astype(F32)
        hat2 = jnp.concatenate([prod[pl.ds(i, 128, stride=33), :], prod[pl.ds(i + 1, 128, stride=33), :]], axis=1)
        scale2 = jnp.concatenate([scales[pl.ds(32 + i, 1), :], scales[pl.ds(33 + i, 1), :]], axis=1)
        n2 = (hat2 * gain2).astype(BF)
        z = pair(zs, i)
        gate = pair(gates, i)
        dz = (dmf * gate).astype(BF)
        d_open = (dmf * z * gate * (1.0 - gate)).astype(BF)
        d_wout[...] += nt(n2, dz)
        dn2 = mm(tri_out[...], dz).astype(BF).astype(F32)
        gain_sum[1] += fold(dn2 * hat2)
        dp = norm_back(dn2 * gain2, hat2, scale2)
        for r in range(2):
            d_prod[pl.ds(i + r, 128, stride=33), :] = pltpu.roll(dp[:, lanes(r)], 64 * chip, axis=1)
            d_mid[i + r] = dm[:, lanes(r)]
            d_gate[i + r] = d_open[:, lanes(r)]

    loop(16, second_back, 4)

    def chunk(ref, q):
        return ref.at[:, at(q, STRIP), :]

    def move(kind, q):
        src, dst, peer = (
            (far.at[1 - core], far_in, partner), (sent, cross_in, cross), (near.at[1 - core], near_in, partner),
        )[kind]
        return pltpu.make_async_remote_copy(
            src_ref=chunk(src, q), dst_ref=chunk(dst, q), send_sem=sem_s.at[kind, q], recv_sem=sem_r.at[kind, q],
            device_id={"dap": peer}, device_id_type=MESH)

    def right_grads(half, q, store):
        def one(c):
            ch = STRIP * q + c
            dp = d_prod[pl.ds(ch * 33, 32), 64 * half : 64 * half + 64].astype(BF)
            work[pl.ds(c, 64, stride=STRIP + 1), :] = tn(dp, left_f[pl.ds(ch, 32, stride=129), :].astype(BF))

        loop(STRIP, one, 16)

        def pack(j):
            store[j // 32, lax.rem(j, 32), at(q, STRIP), :] = work[pl.ds(j * (STRIP + 1), STRIP), :].astype(BF)

        loop(64, pack, 8)

    def add_on(q):
        move(0, q).wait_recv()

        def one(j):
            spot = at(q, STRIP)
            sent[j, spot, :] = (far[core, j, spot, :].astype(F32) + far_in[j, spot, :].astype(F32)).astype(BF)

        loop(32, one, 8)
        move(1, q).start()

    def out_far(q):
        right_grads(1, q, far)
        move(0, q).start()
        pl.when(q > 0)(lambda: add_on(q - 1))

    loop(SPLIT, out_far)
    early.start_b()

    def out_near(q):
        right_grads(0, q, near)
        move(2, q).start()
        pl.when(q == 0)(lambda: add_on(SPLIT - 1))

    loop(SPLIT, out_near)
    early.start_c()

    def left_grad(ch):
        rgt = right_f[pl.ds(ch, 128, stride=129), :].astype(BF)
        left_f[pl.ds(ch, 32, stride=129), :] = mm(d_prod[pl.ds(ch * 33, 32), :].astype(BF), rgt)

    loop(128, left_grad, 16)

    def stored(i, k):
        rows = slice(128 * k, 128 * k + 128)
        return jnp.concatenate([pieces[i, rows], pieces[i + 1, rows]], axis=1)

    def left_part(t):
        i = 2 * t
        dl = jnp.concatenate([left_f[pl.ds(i * 129, 128), :], left_f[pl.ds(i * 129 + 129, 128), :]], axis=1).astype(BF).astype(F32)
        dp = jnp.concatenate(
            [(dl * stored(i, 0)).astype(BF), (dl * stored(i, 1)).astype(BF), pair(d_gate, i)], axis=0)
        d_w1[0:384, :] += nt(dp, pair(normed, i))
        dn = mm(w1[:, 0:384], dp)
        part[i] = dn[:, :128]
        part[i + 1] = dn[:, 128:]

    loop(16, left_part, 4)

    loop(SPLIT, lambda q: move(2, q).wait_recv())

    def settle_near(t):
        i = 2 * t
        hat, scale_1 = norm_cols(pair(slab_t, i).astype(F32))
        for r in range(2):
            right_f[at(i + r, 128), :] = near[core, i + r].astype(F32) + near_in[i + r].astype(F32)
            right_f[at(32 + i + r, 128), :] = hat[:, lanes(r)]
            scales[pl.ds(i + r, 1), :] = scale_1[:, lanes(r)]

    loop(16, settle_near, 2)
    loop(SPLIT, lambda q: move(1, q).wait_recv())
    early.start_d()

    def right_part(t):
        i = 2 * t

        def held(j):
            return jnp.concatenate([right_f[at(j, 128), :], right_f[at(j + 1, 128), :]], axis=1)

        dr = (held(i) + pair(cross_in, i).astype(F32)).astype(BF).astype(F32)
        dp = jnp.concatenate([(dr * stored(i, 2)).astype(BF), (dr * stored(i, 3)).astype(BF)], axis=0)
        d_w1[384:640, :] += nt(dp, pair(normed, i))
        dn = (pair(part, i) + mm(w1[:, 384:640], dp)).astype(BF).astype(F32)
        hat = held(32 + i)
        spread_1 = jnp.concatenate([scales[pl.ds(i, 1), :], scales[pl.ds(i + 1, 1), :]], axis=1)
        gain_sum[0] += fold(dn * hat)
        dx = norm_back(dn * twice(g1[...]), hat, spread_1).astype(BF)
        res = pair(d_mid, i) + dx
        grad[i] = flip(res[:, :128]).astype(BF)
        grad[i + 1] = flip(res[:, 128:]).astype(BF)

    loop(16, right_part, 4)


    late.g[0:640, :] = d_w1[...].astype(BF)
    late.g[640:768, :] = d_wout[...].astype(BF)
    late.g[768:784, :] = d_wb[...].astype(BF)
    late.g[784:, :] = jnp.zeros((240, 128), BF)
    ones = jnp.ones((16, 128), F32)
    for k in range(3):
        late.g[784 + 16 * k : 800 + 16 * k, :] = nt(ones, gain_sum[k], EXACT).astype(BF)
    late.start_a()
    early.finish()
    for b in range(4):
        o_att_in[:, lanes(b)] = flip(early.full[128 * b : 128 * b + 128, :])
    o_att_out[...] = early.full[512:640, :].astype(F32)
    for h in range(4):
        o_table[h] = early.full[640 + 16 * h : 656 + 16 * h, :].astype(F32)[0:4, 0:4]
    late.start_b()
    early.settle()
    late.start_c()
    for r in (1, 2, 3):
        share_bias(r).wait_send()
        share_grad(r).wait_send()
    for kind in range(3):
        for c in range(4):
            edge(kind, c).wait_send()
        loop(SPLIT, lambda q: move(kind, q).wait_send())
    late.start_d()
    late.finish()
    for b, source in enumerate((0, 1, 3, 4)):
        o_tri_in[:, lanes(b)] = flip(late.full[128 * source : 128 * source + 128, :])
    o_tri_gate[...] = flip(late.full[256:384, :])
    o_tri_out[...] = late.full[640:768, :].astype(F32)
    o_att_bias[...] = late.full[768:784, :].astype(F32)[0:4, :]
    for k, ref in enumerate((o_gain1, o_gain2, o_gain3)):
        ref[...] = late.full[784 + 16 * k : 800 + 16 * k, :].astype(F32)[0:1, :]
    late.settle()


def hand_over(*refs):
    held, sems = refs[2 * N_OUT : 3 * N_OUT], refs[3 * N_OUT]
    parts = [(k, pl.ds(8 * c, 8), 4 * k + c) for k in range(2) for c in range(4)]
    parts += [(k, slice(None), 6 + k) for k in range(2, N_OUT)]
    reads = [pltpu.make_async_copy(refs[k].at[s], held[k].at[s], sems.at[0, n]) for k, s, n in parts]
    writes = [pltpu.make_async_copy(held[k].at[s], refs[N_OUT + k].at[s], sems.at[1, n]) for k, s, n in parts]
    for copy in reads:
        copy.start()
    for read, write in zip(reads, writes):
        read.wait()
        write.start()
    for copy in writes:
        copy.wait()


def per_device(*args):
    pair_rep, cotangent, tok_mask, tok_types, pair_mask = args[:5]
    params = [v[None] if v.ndim == 1 else v for v in args[5:]]
    params[6] = params[6].T
    n_dp = lax.axis_size("dp")
    factor = (128 * 128 * n_dp) ** (-0.5)
    block = (32, 128, 128)
    shapes = [v.shape for v in params]
    spec = pl.BlockSpec(memory_space=VM)
    scratch = Sum.scratch(n_dp) * 2 + [
        VM((32, 128), F32), VM((128, 32), BF), VM((128, 128), F32),
        VM((128, 128), F32), VM((128, 128), F32), VM((128, 128), F32),
        VM((128, 640), BF), VM((640, 128), BF), VM((512, 128), BF), VM((128, 128), BF), VM((128, 128), BF),
        VM((128, 16), BF), VM((16, 128), BF), VM((16, 128), F32), VM((4, 16, 16), F32), VM((128, 512), F32),
        VM(block, BF), VM(block, BF), VM((4224, 128), F32), VM((4,) + block, BF), VM((4128, 128), F32),
        VM((16512, 128), F32), VM(block, F32), VM((32, 512, 128), F32), VM(block, BF),
        VM((4, 32, 128), F32), VM((4, 32, 128), BF), VM((4, 128, 128), BF),
        VM((128, 512), F32), VM((512, 128), F32), VM((128, 128), F32), VM((128, 128), F32), VM((16, 128), F32),
        VM((640, 128), F32), VM((3, 128, 128), F32),
        VM((4, 128, 128), BF), VM((3, 4, 32, 128), BF), VM((4, 32, 128), F32), VM((4224, 128), F32),
        VM(block, BF), VM(block, BF), VM((64 * (STRIP + 1), 128), F32),
        VM((2,) + block, BF), VM(block, BF), VM(block, BF), VM(block, BF), VM((2,) + block, BF), VM(block, BF),
        VM(block, BF), VM(block, BF), VM(block, BF), VM((64, 128), F32), VM(block, F32),
        DMA((3, 4)), DMA((3, 4)), DMA((3,)), DMA((3,)), DMA((3,)), DMA((3,)), DMA((3, SPLIT)), DMA((3, SPLIT)),
    ]
    results = pl.pallas_call(
        partial(kernel, n_dp, factor),
        out_shape=[jax.ShapeDtypeStruct(block, BF)] * 2 + [jax.ShapeDtypeStruct(s, F32) for s in shapes],
        in_specs=[spec] * N_IN,
        out_specs=[spec] * N_OUT,
        scratch_shapes=scratch,
        compiler_params=pltpu.CompilerParams(collective_id=0, has_side_effects=True, vmem_limit_bytes=63 << 20),
        name="pairformer",
    )(pair_rep[0], cotangent[0], tok_mask, tok_types, pair_mask[0], *params)
    anywhere = pl.BlockSpec(memory_space=pl.ANY)
    results = pl.pallas_call(
        hand_over,
        out_shape=[jax.ShapeDtypeStruct(r.shape, r.dtype) for r in results],
        in_specs=[anywhere] * N_OUT,
        out_specs=[anywhere] * N_OUT,
        scratch_shapes=[VM(r.shape, r.dtype) for r in results] + [DMA((2, N_OUT + 6))],
        name="hand_over",
    )(*results)
    results = list(results)
    results[8] = results[8].T
    return tuple(
        [results[0][None], results[1][None]]
        + [r[0] if v.ndim == 1 else r for r, v in zip(results[2:], args[5:])]
    )


def solution(mesh):
    return jax.shard_map(
        per_device,
        mesh=mesh,
        in_specs=(
            P("dp", "dap", None, None),
            P("dp", "dap", None, None),
            P("dp", None),
            P("dp", None),
            P("dp", "dap", None),
            P(),
            P(),
            P(),
            P(),
            P(),
            P(),
            P(),
            P(),
            P(),
            P(),
        ),
        out_specs=(
            P("dp", "dap", None, None),
            P("dp", "dap", None, None),
            P(),
            P(),
            P(),
            P(),
            P(),
            P(),
            P(),
            P(),
            P(),
            P(),
        ),
        check_vma=False,
    )
```

```python
from functools import partial

import jax
import jax.numpy as jnp
from jax import lax
from jax.experimental import pallas as pl
from jax.experimental.pallas import tpu as pltpu
from jax.sharding import PartitionSpec as P

EPSILON = 1e-05
MESH = pl.DeviceIdType.MESH
VM = pltpu.VMEM
DMA = pltpu.SemaphoreType.DMA
BF = jnp.bfloat16
F32 = jnp.float32
EXACT = lax.Precision.HIGHEST


def contract(x, y, dims, precision=None):
    return lax.dot_general(x, y, (dims, ((), ())), precision=precision, preferred_element_type=F32)


def mm(x, y, precision=None):
    return contract(x, y, ((1,), (0,)), precision)


def nt(x, y, precision=None):
    return contract(x, y, ((1,), (1,)), precision)


def tn(x, y, precision=None):
    return contract(x, y, ((0,), (0,)), precision)


def norm_cols(x):
    mean = jnp.sum(x, axis=0, keepdims=True) * (1.0 / 128)
    centred = x - mean
    spread = jnp.sum(centred * centred, axis=0, keepdims=True) * (1.0 / 128)
    scale = lax.rsqrt(spread + EPSILON)
    return centred * scale, scale


def norm_back(grad, unit, scale):
    a = jnp.sum(grad, axis=0, keepdims=True) * (1.0 / 128)
    b = jnp.sum(grad * unit, axis=0, keepdims=True) * (1.0 / 128)
    return scale * (grad - a - unit * b)


def loop(n, fn, unroll=1, first=0):
    def body(i, carry):
        fn(i)
        return carry
    lax.fori_loop(first, n, body, 0, unroll=unroll)


def at(i, size):
    return pl.ds(pl.multiple_of(i * size, size), size)


def halves(x):
    return x[:, :128], x[:, 128:]


def twice(x):
    return jnp.concatenate([x, x], axis=1)


def pair(ref, i):
    return jnp.concatenate([ref[i], ref[i + 1]], axis=1)


def lanes(r):
    return slice(128 * r, 128 * r + 128)


class Sum:
    def __init__(self, n_dp, factor, a, p, refs):
        self.n_dp, self.factor, self.a, self.p = n_dp, factor, a, p
        self.partner, self.cross = a + 1 - 2 * lax.rem(a, 2), lax.rem(a + 2, 4)
        (self.g, self.part, self.quarter, self.pieces, self.mine, self.joined, self.joined_b, self.full,
         self.sa, self.ra, self.sb, self.rb, self.sc, self.rc, self.sd, self.rd) = refs
        self.size = 256 // n_dp

    def remote(self, src, dst, s, r, **peer):
        return pltpu.make_async_remote_copy(
            src_ref=src, dst_ref=dst, send_sem=s, recv_sem=r, device_id=peer, device_id_type=MESH)

    def copy_a(self, r, k):
        peer = lax.rem(self.a + r, 4)
        start, size = ((0, CUT), (CUT, 256 - CUT))[k]
        src = self.g.at[pl.ds(pl.multiple_of(peer * 256 + start, 16), size)]
        return self.remote(
            src, self.part.at[r - 1, start : start + size], self.sa.at[k, r - 1], self.ra.at[k, r - 1], dap=peer)

    def rows_of(self, k, first, size):
        span = (CUT, 256 - CUT)[k]
        while size > 0:
            count = min(size, span - first % span)
            row = 256 * (first // span) + CUT * k + first % span
            yield slice(row, row + count), count
            first, size = first + count, size - count

    def put(self, k, first, block):
        done = 0
        for rows, count in self.rows_of(k, first, block.shape[0]):
            self.g[rows, :] = block[done : done + count].astype(BF)
            done += count

    def get(self, k, first, size):
        return jnp.concatenate([self.full[rows, :] for rows, _ in self.rows_of(k, first, size)], axis=0)

    def copy_b(self, r):
        peer = lax.rem(self.p + r, self.n_dp)
        return self.remote(
            self.quarter.at[at(peer, self.size)], self.pieces.at[r - 1], self.sb, self.rb, dp=peer)

    def copy_c(self, r):
        peer = lax.rem(self.p + r, self.n_dp)
        return self.remote(self.mine, self.joined.at[at(self.p, self.size)], self.sc, self.rc, dp=peer)

    def all_of(self, ref, s, r):
        return self.remote(ref, ref, s, r, dp=lax.rem(self.p + 1, self.n_dp))

    def others(self, ref):
        return ref.at[pl.ds(0, (self.n_dp - 1) * self.size)]

    def copy_d(self, k):
        there = at(self.cross if k == 2 else self.a, 256)
        src = self.full.at[there] if k == 2 else self.joined_b
        return self.remote(
            src, self.full.at[there], self.sd.at[k], self.rd.at[k], dap=self.cross if k == 0 else self.partner)

    def start_a(self, k):
        for r in (2, 1, 3):
            self.copy_a(r, k).start()

    def start_b(self):
        total = self.g[at(self.a, 256), :].astype(F32)
        for r in (1, 2, 3):
            for k in range(2):
                self.copy_a(r, k).wait_recv()
            total = total + self.part[r - 1].astype(F32)
        self.quarter[...] = total
        for r in range(1, self.n_dp):
            self.copy_b(r).start()

    def start_c(self):
        self.all_of(self.pieces, self.sb, self.rb).wait_recv()
        total = self.quarter[at(self.p, self.size), :] + jnp.sum(self.pieces[...], axis=0)
        self.mine[...] = total * self.factor
        for r in range(1, self.n_dp):
            self.copy_c(r).start()
        self.joined[at(self.p, self.size), :] = self.mine[...]

    def start_d(self):
        self.all_of(self.others(self.joined), self.sc, self.rc).wait_recv()
        self.joined_b[...] = self.joined[...].astype(BF)
        self.copy_d(0).start()
        self.copy_d(1).start()
        self.full[at(self.a, 256), :] = self.joined_b[...]

    def finish(self):
        self.copy_d(0).wait_recv()
        self.copy_d(2).start()
        self.copy_d(1).wait_recv()
        self.copy_d(2).wait_recv()

    def settle(self):
        for r in (1, 2, 3):
            for k in range(2):
                self.copy_a(r, k).wait_send()
        self.all_of(self.pieces, self.sb, self.rb).wait_send()
        self.all_of(self.others(self.joined), self.sc, self.rc).wait_send()
        for k in range(3):
            self.copy_d(k).wait_send()

    @staticmethod
    def scratch(n_dp):
        size = 256 // n_dp
        return [
            VM((1024, 128), BF), VM((3, 256, 128), BF), VM((256, 128), F32), VM((n_dp - 1, size, 128), F32),
            VM((size, 128), F32), VM((256, 128), F32), VM((256, 128), BF), VM((1024, 128), BF),
        ] + [DMA((2, 3))] * 2 + [DMA] * 4 + [DMA((3,))] * 2


N_IN, N_OUT, N_SUM = 15, 12, 16
STRIP, SPLIT, CUT = 16, 8, 176


def kernel(n_dp, factor, *refs):
    (slab, cot, tok_mask, tok_types, pair_mask, gain1, tri_in, tri_gate, gain2, tri_out, gain3, att_bias, att_in,
     att_out, table) = refs[:N_IN]
    (out, grad, o_gain1, o_tri_in, o_tri_gate, o_gain2, o_tri_out, o_gain3, o_att_bias, o_att_in, o_att_out,
     o_table) = refs[N_IN : N_IN + N_OUT]
    rest = refs[N_IN + N_OUT :]
    a, p = lax.axis_index("dap"), lax.axis_index("dp")
    partner, cross, chip, core = a + 1 - 2 * lax.rem(a, 2), lax.rem(a + 2, 4), a // 2, lax.rem(a, 2)
    early = Sum(n_dp, factor, a, p, rest[:N_SUM])
    late = Sum(n_dp, factor, a, p, rest[N_SUM : 2 * N_SUM])
    (live, live_t, tok_t, g1, g2, g3, w1, w1t, wat, wot, woutt, wb, wbt, hot, tab, bt,
     mid, dn3, prod, right, left_f, right_f, gates, pieces, normed, bias_f, bias_b, bias,
     d_bias, d_wa, d_wo, d_wout, d_wb, d_w1, gain_sum,
     db_n, db_in, db_f, d_prod, d_mid, d_gate, work, far, far_in, sent, cross_in, near, near_in,
     slab_t, cot_t, d_gated_t, scales, zs, sem_es, sem_er, sem_is, sem_ir, sem_bs, sem_br, sem_s, sem_r) = rest[2 * N_SUM :]
    part = gates

    barrier = pltpu.get_barrier_semaphore()
    for r in range(1, 4):
        pl.semaphore_signal(barrier, inc=1, device_id={"dap": lax.rem(a + r, 4)}, device_id_type=MESH)
    for r in range(1, n_dp):
        pl.semaphore_signal(barrier, inc=1, device_id={"dp": lax.rem(p + r, n_dp)}, device_id_type=MESH)

    rows_i = lax.broadcasted_iota(jnp.int32, (128, 128), 0)
    unit = (rows_i == lax.broadcasted_iota(jnp.int32, (128, 128), 1)).astype(F32).astype(BF)

    def flip(block):
        return nt(unit, block)

    def flipped(ref, i):
        return jnp.concatenate([flip(ref[i]), flip(ref[i + 1])], axis=1)

    def column(row):
        return jnp.broadcast_to(row, (128, 128)).T

    tokens = tok_mask[...].astype(F32)
    tok_t[...] = column(tokens)
    live[...] = pair_mask[...].astype(F32) * tok_t[at(a, 32), :] * tokens
    live_t[...] = tn(live[...].astype(BF), unit[:32, :32]).astype(BF)
    for gain, row in ((g1, gain1), (g2, gain2), (g3, gain3)):
        gain[...] = column(row[...])
    w1[:, 0:256] = tri_in[:, 0:256]
    w1[:, 256:384] = tri_gate[...]
    w1[:, 384:640] = tri_in[:, 256:512]
    for b in range(5):
        w1t[128 * b : 128 * b + 128, :] = flip(w1[:, lanes(b)]).astype(BF)
    for b in range(4):
        wat[128 * b : 128 * b + 128, :] = flip(att_in[:, lanes(b)]).astype(BF)
    wot[...] = flip(att_out[...]).astype(BF)
    woutt[...] = flip(tri_out[...]).astype(BF)
    wbt[...] = jnp.concatenate([att_bias[...].astype(F32), jnp.zeros((12, 128), F32)], axis=0).astype(BF)
    wb[...] = flip(wbt[...]).astype(BF)
    tab[...] = jnp.zeros_like(tab)
    tab[:, 0:4, 0:4] = table[...]
    hot[...] = (lax.broadcasted_iota(jnp.int32, (16, 128), 0) == tok_types[...]).astype(F32)

    def alive_of(i):
        return jnp.concatenate([live[pl.ds(i, 1), :], live[pl.ds(i + 1, 1), :]], axis=1)


    def edge(kind, c):
        block = right.at[cross if kind == 2 else a]
        spot = block.at[8 * c : 8 * c + 8] if c < 2 else block.at[16:32, 64 * (c - 2) : 64 * (c - 1), :]
        return pltpu.make_async_remote_copy(
            src_ref=spot, dst_ref=spot, send_sem=sem_es.at[kind, c], recv_sem=sem_er.at[kind, c],
            device_id={"dap": cross if kind == 1 else partner}, device_id_type=MESH)

    def project(t):
        i = 2 * t
        x = flipped(slab, i)
        hat, _ = norm_cols(x)
        n = (hat * twice(g1[...])).astype(BF)
        q = mm(w1t[...], n)
        alive = alive_of(i)
        sa, sb = jax.nn.sigmoid(q[128:256]), jax.nn.sigmoid(q[512:])
        fa, fb = sa * alive, sb * alive
        lft, rgt = fa * q[:128], fb * q[384:512]
        ga, gb = lft * (1.0 - sa), rgt * (1.0 - sb)
        lft, rgt = lft.astype(BF).astype(F32), rgt.astype(BF)
        x = x.astype(BF)
        gate = jax.nn.sigmoid(q[256:384])
        for r in range(2):
            normed[i + r] = n[:, lanes(r)]
            slab_t[i + r] = x[:, lanes(r)]
            left_f[pl.ds((i + r) * 129, 128), :] = lft[:, lanes(r)]
            right[a, i + r] = rgt[:, lanes(r)]
            gates[i + r] = gate[:, lanes(r)]
            pieces[i + r, 0:128] = fa[:, lanes(r)]
            pieces[i + r, 128:256] = ga[:, lanes(r)]
            pieces[i + r, 256:384] = fb[:, lanes(r)]
            pieces[i + r, 384:512] = gb[:, lanes(r)]

    loop(4, project, 2)
    pl.semaphore_wait(barrier, 3 + n_dp - 1)
    for c, (low_t, high_t) in enumerate(((0, 0), (4, 8), (8, 16), (0, 0))):
        if high_t > low_t:
            loop(high_t, project, 2, first=low_t)
        edge(1, c).start()
        edge(0, c).start()

    def unpack(block, base, rows=(0, 32), chans=(0, 128)):
        span = slice(*chans)

        def one(j):
            start = (base + j) * 129 + chans[0]
            right_f[pl.ds(start, chans[1] - chans[0]), :] = right[block, j, span].astype(F32)

        loop(rows[1], one, 4, first=rows[0])

    def multiply(half, chans=(0, 128)):
        def one(ch):
            lft = left_f[pl.ds(ch, 32, stride=129), :].astype(BF)
            rgt = right_f[pl.ds(64 * 129 * half + ch, 64, stride=129), :].astype(BF)
            prod[pl.ds(ch * 33, 32), 64 * half : 64 * half + 64] = nt(lft, rgt)
        loop(chans[1], one, 16, first=chans[0])

    for c in range(4):
        edge(0, c).wait_recv()
    low = 2 * chip
    unpack(low, 0)
    unpack(low + 1, 32)
    multiply(0)

    def prepare(t):
        i = 2 * t
        ct = flipped(cot, i).astype(BF)
        dg = mm(att_out[...], ct).astype(BF)
        for r in range(2):
            cot_t[i + r] = ct[:, lanes(r)]
            d_gated_t[i + r] = dg[:, lanes(r)]

    loop(16, prepare, 4)

    beside = cross + 1 - 2 * core
    for c in range(4):
        rows, chans = ((8 * c, 8 * c + 8), (0, 128)) if c < 2 else ((16, 32), (64 * (c - 2), 64 * (c - 1)))
        edge(1, c).wait_recv()
        edge(2, c).start()
        unpack(cross, 64 + 32 * core, rows, chans)
        edge(2, c).wait_recv()
        unpack(beside, 96 - 32 * core, rows, chans)
        if c >= 2:
            multiply(1, chans)

    def second(t):
        i = 2 * t
        xs = []
        for r in range(2):
            rows = pl.ds(i + r, 128, stride=33)
            xs.append(pltpu.roll(prod[rows, :], 64 * chip, axis=1))
        hat, scale_2 = norm_cols(jnp.concatenate(xs, axis=1))
        n = (hat * twice(g2[...])).astype(BF)
        z = mm(woutt[...], n)
        for r in range(2):
            prod[pl.ds(i + r, 128, stride=33), :] = hat[:, lanes(r)]
            scales[pl.ds(32 + i + r, 1), :] = scale_2[:, lanes(r)]
            zs[i + r] = z[:, lanes(r)]
        middle = (pair(slab_t, i).astype(F32) + pair(gates, i) * z).astype(BF)
        hat, _ = norm_cols(middle.astype(F32))
        n = (hat * twice(g3[...])).astype(BF)
        heads = mm(wbt[...], n)
        for r in range(2):
            mid[i + r] = middle[:, lanes(r)]
            for h in range(4):
                bias_f[h, pl.ds(i + r, 1), :] = heads[h : h + 1, lanes(r)]

    loop(16, second, 4)
    bias_b[...] = bias_f[...].astype(BF)

    def share_bias(r):
        return pltpu.make_async_remote_copy(
            src_ref=bias_b, dst_ref=bias.at[:, at(a, 32), :], send_sem=sem_is.at[r - 1], recv_sem=sem_ir.at[r - 1],
            device_id={"dap": lax.rem(a + r, 4)}, device_id_type=MESH)

    for r in (2, 1, 3):
        share_bias(r).start()
    bias[:, at(a, 32), :] = bias_b[...]
    for h in range(4):
        near_types = mm(tab[h].T, hot[...], EXACT)
        bt[:, lanes(h)] = tn(hot[...], near_types, EXACT)
    for ref in (d_bias, d_wa, d_wo, d_wout, d_wb, d_w1, gain_sum):
        ref[...] = jnp.zeros_like(ref)
    for r in (1, 2, 3):
        share_bias(r).wait_recv()
    for h in range(4):
        bt[:, lanes(h)] += flip(bias[h])


    def spread(x):
        zero = jnp.zeros((32, 128), x.dtype)
        cols = [
            jnp.concatenate([x[32 * h : 32 * h + 32] if g == h else zero for g in range(4)], axis=0)
            for h in range(4)
        ]
        return jnp.concatenate(cols, axis=1)

    scale = 32.0 ** -0.5

    def attend(t):
        i = 2 * t
        m = pair(mid, i).astype(F32)
        hat, _ = norm_cols(m)
        n = (hat * twice(g3[...])).astype(BF)
        q3 = mm(wat[...], n)
        qkv = q3[:384].astype(BF)
        gate = jax.nn.sigmoid(q3[384:])
        ct = pair(cot_t, i)
        d_gated = pair(d_gated_t, i).astype(F32)
        d_att = d_gated * gate
        picked = lax.broadcasted_iota(jnp.int32, (32, 256), 0) == (
            i + lax.broadcasted_iota(jnp.int32, (32, 256), 1) // 128)
        alive = mm(live_t[...], picked.astype(F32).astype(BF))
        both = range(2)
        qs, ks, vs = ([qkv[128 * x : 128 * x + 128, lanes(r)] for r in both] for x in range(3))
        kvs = [flip(qkv[128:384, lanes(r)]).astype(BF) for r in both]
        dos = [d_att[:, lanes(r)].astype(BF) for r in both]
        scores = [mm(kvs[r][:, :128], spread(qs[r])) for r in both]
        das = [mm(kvs[r][:, 128:], spread(dos[r])).astype(BF) for r in both]
        exps = [
            jnp.exp(scores[r] * scale + bt[...]) * jnp.concatenate([alive[:, lanes(r)]] * 4, axis=1) for r in both
        ]
        sums = [jnp.sum(e, axis=0, keepdims=True) for e in exps]
        ws = [e * (1.0 / jnp.maximum(s, 1.0)) for e, s in zip(exps, sums)]
        abs_ = [w.astype(BF) for w in ws]
        us = [da.astype(F32) * w for da, w in zip(das, ws)]
        totals = [jnp.sum(u, axis=0, keepdims=True) for u in us]
        totals = [
            jnp.where(s > 1.0, x, jnp.where(s == 1.0, 0.5 * x, 0.0)) for s, x in zip(sums, totals)
        ]
        dss = [u - w * x for u, w, x in zip(us, ws, totals)]
        d_bias[...] += dss[0] + dss[1]
        dsbs = [ds.astype(BF) for ds in dss]

        def heads_of(fn):
            return jnp.concatenate([fn(slice(32 * h, 32 * h + 32), lanes(h)) for h in range(4)], axis=0)

        atts = [heads_of(lambda h, l: mm(vs[r][h], abs_[r][:, l])) for r in both]
        dvs = [heads_of(lambda h, l: nt(dos[r][h], abs_[r][:, l])) for r in both]
        dks = [heads_of(lambda h, l: nt(qs[r][h], dsbs[r][:, l])) * scale for r in both]
        dqs = [heads_of(lambda h, l: mm(ks[r][h], dsbs[r][:, l])) * scale for r in both]
        parts = [jnp.concatenate([dqs[r], dks[r], dvs[r]], axis=0).astype(BF) for r in both]
        att = jnp.concatenate(atts, axis=1)
        d_open = (d_gated * att * gate * (1.0 - gate)).astype(BF)
        dp = jnp.concatenate([jnp.concatenate(parts, axis=1), d_open], axis=0)
        dn = mm(att_in[...], dp).astype(BF)
        d_wa[...] += nt(dp, n)
        gated = (gate * att).astype(BF)
        d_wo[...] += nt(gated, ct)
        res = (m + mm(wot[...], gated)).astype(BF)
        for r in range(2):
            dn3[i + r] = dn[:, lanes(r)]
            out[i + r] = flip(res[:, lanes(r)]).astype(BF)

    loop(16, attend, 4)

    for h in range(4):
        db_n[h] = flip(d_bias[:, lanes(h)].astype(BF)).astype(BF)

    def share_grad(r):
        peer = lax.rem(a + r, 4)
        return pltpu.make_async_remote_copy(
            src_ref=db_n.at[:, at(peer, 32), :], dst_ref=db_in.at[r - 1], send_sem=sem_bs.at[r - 1],
            recv_sem=sem_br.at[r - 1], device_id={"dap": peer}, device_id_type=MESH)

    for r in (2, 1, 3):
        share_grad(r).start()
    early.g[0:512, :] = d_wa[...].astype(BF)
    early.g[512:640, :] = d_wo[...].astype(BF)
    early.g[640:, :] = jnp.zeros((384, 128), BF)
    for h in range(4):
        near_types = mm(hot[...], d_bias[:, lanes(h)])
        early.g[640 + 16 * h : 656 + 16 * h, 0:16] = nt(hot[...], near_types).astype(BF)
    early.start_a(0)
    early.start_a(1)

    for r in (1, 2, 3):
        share_grad(r).wait_recv()
    total = db_n[:, at(a, 32), :].astype(F32)
    for r in range(3):
        total = total + db_in[r].astype(F32)
    db_f[...] = total


    def fold(x):
        return x[:, :128] + x[:, 128:]

    def second_back(t):
        i = 2 * t
        hat3, scale3 = norm_cols(pair(mid, i).astype(F32))
        gain3, gain2 = twice(g3[...]), twice(g2[...])
        n3 = (hat3 * gain3).astype(BF)
        rows = [
            jnp.concatenate([db_f[h, pl.ds(i, 1), :], db_f[h, pl.ds(i + 1, 1), :]], axis=1) for h in range(4)
        ]
        db = jnp.concatenate(rows + [jnp.zeros((12, 256), F32)], axis=0).astype(BF)
        dn = pair(dn3, i).astype(F32) + mm(wb[...], db)
        d_wb[...] += nt(db, n3)
        gain_sum[2] += fold(dn * hat3)
        dm = pair(cot_t, i) + norm_back(dn * gain3, hat3, scale3).astype(BF)
        dmf = dm.astype(F32)
        hat2 = jnp.concatenate([prod[pl.ds(i, 128, stride=33), :], prod[pl.ds(i + 1, 128, stride=33), :]], axis=1)
        scale2 = jnp.concatenate([scales[pl.ds(32 + i, 1), :], scales[pl.ds(33 + i, 1), :]], axis=1)
        n2 = (hat2 * gain2).astype(BF)
        z = pair(zs, i)
        gate = pair(gates, i)
        dz = (dmf * gate).astype(BF)
        d_open = (dmf * z * gate * (1.0 - gate)).astype(BF)
        d_wout[...] += nt(n2, dz)
        dn2 = mm(tri_out[...], dz).astype(BF).astype(F32)
        gain_sum[1] += fold(dn2 * hat2)
        dp = norm_back(dn2 * gain2, hat2, scale2)
        for r in range(2):
            d_prod[pl.ds(i + r, 128, stride=33), :] = pltpu.roll(dp[:, lanes(r)], 64 * chip, axis=1)
            d_mid[i + r] = dm[:, lanes(r)]
            d_gate[i + r] = d_open[:, lanes(r)]

    loop(16, second_back, 4)

    def chunk(ref, q):
        return ref.at[:, at(q, STRIP), :]

    def move(kind, q):
        src, dst, peer = (
            (far.at[1 - core], far_in, partner), (sent, cross_in, cross), (near.at[1 - core], near_in, partner),
        )[kind]
        return pltpu.make_async_remote_copy(
            src_ref=chunk(src, q), dst_ref=chunk(dst, q), send_sem=sem_s.at[kind, q], recv_sem=sem_r.at[kind, q],
            device_id={"dap": peer}, device_id_type=MESH)

    def right_grads(half, q, store):
        def one(c):
            ch = STRIP * q + c
            dp = d_prod[pl.ds(ch * 33, 32), 64 * half : 64 * half + 64].astype(BF)
            work[pl.ds(c, 64, stride=STRIP + 1), :] = tn(dp, left_f[pl.ds(ch, 32, stride=129), :].astype(BF))

        loop(STRIP, one, 16)

        def pack(j):
            store[j // 32, lax.rem(j, 32), at(q, STRIP), :] = work[pl.ds(j * (STRIP + 1), STRIP), :].astype(BF)

        loop(64, pack, 8)

    def add_on(q):
        move(0, q).wait_recv()

        def one(j):
            spot = at(q, STRIP)
            sent[j, spot, :] = (far[core, j, spot, :].astype(F32) + far_in[j, spot, :].astype(F32)).astype(BF)

        loop(32, one, 8)
        move(1, q).start()

    def out_far(q):
        right_grads(1, q, far)
        move(0, q).start()
        pl.when(q > 0)(lambda: add_on(q - 1))

    loop(SPLIT, out_far)
    early.start_b()

    def out_near(q):
        right_grads(0, q, near)
        move(2, q).start()
        pl.when(q == 0)(lambda: add_on(SPLIT - 1))

    loop(SPLIT, out_near)
    early.start_c()

    def left_grad(ch):
        rgt = right_f[pl.ds(ch, 128, stride=129), :].astype(BF)
        left_f[pl.ds(ch, 32, stride=129), :] = mm(d_prod[pl.ds(ch * 33, 32), :].astype(BF), rgt)

    loop(128, left_grad, 16)

    def stored(i, k):
        rows = slice(128 * k, 128 * k + 128)
        return jnp.concatenate([pieces[i, rows], pieces[i + 1, rows]], axis=1)

    def left_part(t):
        i = 2 * t
        dl = jnp.concatenate([left_f[pl.ds(i * 129, 128), :], left_f[pl.ds(i * 129 + 129, 128), :]], axis=1).astype(BF).astype(F32)
        dp = jnp.concatenate(
            [(dl * stored(i, 0)).astype(BF), (dl * stored(i, 1)).astype(BF), pair(d_gate, i)], axis=0)
        d_w1[0:384, :] += nt(dp, pair(normed, i))
        dn = mm(w1[:, 0:384], dp)
        part[i] = dn[:, :128]
        part[i + 1] = dn[:, 128:]

    loop(16, left_part, 4)

    loop(SPLIT, lambda q: move(2, q).wait_recv())

    def settle_near(t):
        i = 2 * t
        hat, scale_1 = norm_cols(pair(slab_t, i).astype(F32))
        for r in range(2):
            right_f[at(i + r, 128), :] = near[core, i + r].astype(F32) + near_in[i + r].astype(F32)
            right_f[at(32 + i + r, 128), :] = hat[:, lanes(r)]
            scales[pl.ds(i + r, 1), :] = scale_1[:, lanes(r)]

    loop(16, settle_near, 2)
    ones = jnp.ones((16, 128), F32)

    def put_gain(k, first, which):
        late.put(k, first, nt(ones, gain_sum[which], EXACT))

    late.put(0, 0, d_w1[0:384, :])
    late.put(0, 384, d_wout[...])
    late.put(0, 512, d_wb[...])
    put_gain(0, 528, 1)
    put_gain(0, 544, 2)
    late.put(0, 560, jnp.zeros((144, 128), F32))
    loop(SPLIT, lambda q: move(1, q).wait_recv())
    early.start_d()
    late.start_a(0)

    def right_part(t):
        i = 2 * t

        def held(j):
            return jnp.concatenate([right_f[at(j, 128), :], right_f[at(j + 1, 128), :]], axis=1)

        dr = (held(i) + pair(cross_in, i).astype(F32)).astype(BF).astype(F32)
        dp = jnp.concatenate([(dr * stored(i, 2)).astype(BF), (dr * stored(i, 3)).astype(BF)], axis=0)
        d_w1[384:640, :] += nt(dp, pair(normed, i))
        dn = (pair(part, i) + mm(w1[:, 384:640], dp)).astype(BF).astype(F32)
        hat = held(32 + i)
        spread_1 = jnp.concatenate([scales[pl.ds(i, 1), :], scales[pl.ds(i + 1, 1), :]], axis=1)
        gain_sum[0] += fold(dn * hat)
        dx = norm_back(dn * twice(g1[...]), hat, spread_1).astype(BF)
        res = pair(d_mid, i) + dx
        grad[i] = flip(res[:, :128]).astype(BF)
        grad[i + 1] = flip(res[:, 128:]).astype(BF)

    loop(16, right_part, 4)


    late.put(1, 0, d_w1[384:640, :])
    put_gain(1, 256, 0)
    late.put(1, 272, jnp.zeros((48, 128), F32))
    late.start_a(1)
    early.finish()
    for b in range(4):
        o_att_in[:, lanes(b)] = flip(early.full[128 * b : 128 * b + 128, :])
    o_att_out[...] = early.full[512:640, :].astype(F32)
    for h in range(4):
        o_table[h] = early.full[640 + 16 * h : 656 + 16 * h, :].astype(F32)[0:4, 0:4]
    late.start_b()
    early.settle()
    late.start_c()
    for r in (1, 2, 3):
        share_bias(r).wait_send()
        share_grad(r).wait_send()
    for kind in range(3):
        for c in range(4):
            edge(kind, c).wait_send()
        loop(SPLIT, lambda q: move(kind, q).wait_send())
    late.start_d()
    late.finish()
    for b in range(2):
        o_tri_in[:, lanes(b)] = flip(late.get(0, 128 * b, 128))
        o_tri_in[:, lanes(b + 2)] = flip(late.get(1, 128 * b, 128))
    o_tri_gate[...] = flip(late.get(0, 256, 128))
    o_tri_out[...] = late.get(0, 384, 128).astype(F32)
    o_att_bias[...] = late.get(0, 512, 16).astype(F32)[0:4, :]
    for ref, k, first in ((o_gain1, 1, 256), (o_gain2, 0, 528), (o_gain3, 0, 544)):
        ref[...] = late.get(k, first, 16).astype(F32)[0:1, :]
    late.settle()


def hand_over(*refs):
    held, sems = refs[2 * N_OUT : 3 * N_OUT], refs[3 * N_OUT]
    parts = [(k, pl.ds(8 * c, 8), 4 * k + c) for k in range(2) for c in range(4)]
    parts += [(k, slice(None), 6 + k) for k in range(2, N_OUT)]
    reads = [pltpu.make_async_copy(refs[k].at[s], held[k].at[s], sems.at[0, n]) for k, s, n in parts]
    writes = [pltpu.make_async_copy(held[k].at[s], refs[N_OUT + k].at[s], sems.at[1, n]) for k, s, n in parts]
    for copy in reads:
        copy.start()
    for read, write in zip(reads, writes):
        read.wait()
        write.start()
    for copy in writes:
        copy.wait()


def per_device(*args):
    pair_rep, cotangent, tok_mask, tok_types, pair_mask = args[:5]
    params = [v[None] if v.ndim == 1 else v for v in args[5:]]
    params[6] = params[6].T
    n_dp = lax.axis_size("dp")
    factor = (128 * 128 * n_dp) ** (-0.5)
    block = (32, 128, 128)
    shapes = [v.shape for v in params]
    spec = pl.BlockSpec(memory_space=VM)
    scratch = Sum.scratch(n_dp) * 2 + [
        VM((32, 128), F32), VM((128, 32), BF), VM((128, 128), F32),
        VM((128, 128), F32), VM((128, 128), F32), VM((128, 128), F32),
        VM((128, 640), BF), VM((640, 128), BF), VM((512, 128), BF), VM((128, 128), BF), VM((128, 128), BF),
        VM((128, 16), BF), VM((16, 128), BF), VM((16, 128), F32), VM((4, 16, 16), F32), VM((128, 512), F32),
        VM(block, BF), VM(block, BF), VM((4224, 128), F32), VM((4,) + block, BF), VM((4128, 128), F32),
        VM((16512, 128), F32), VM(block, F32), VM((32, 512, 128), F32), VM(block, BF),
        VM((4, 32, 128), F32), VM((4, 32, 128), BF), VM((4, 128, 128), BF),
        VM((128, 512), F32), VM((512, 128), F32), VM((128, 128), F32), VM((128, 128), F32), VM((16, 128), F32),
        VM((640, 128), F32), VM((3, 128, 128), F32),
        VM((4, 128, 128), BF), VM((3, 4, 32, 128), BF), VM((4, 32, 128), F32), VM((4224, 128), F32),
        VM(block, BF), VM(block, BF), VM((64 * (STRIP + 1), 128), F32),
        VM((2,) + block, BF), VM(block, BF), VM(block, BF), VM(block, BF), VM((2,) + block, BF), VM(block, BF),
        VM(block, BF), VM(block, BF), VM(block, BF), VM((64, 128), F32), VM(block, F32),
        DMA((3, 4)), DMA((3, 4)), DMA((3,)), DMA((3,)), DMA((3,)), DMA((3,)), DMA((3, SPLIT)), DMA((3, SPLIT)),
    ]
    results = pl.pallas_call(
        partial(kernel, n_dp, factor),
        out_shape=[jax.ShapeDtypeStruct(block, BF)] * 2 + [jax.ShapeDtypeStruct(s, F32) for s in shapes],
        in_specs=[spec] * N_IN,
        out_specs=[spec] * N_OUT,
        scratch_shapes=scratch,
        compiler_params=pltpu.CompilerParams(collective_id=0, has_side_effects=True, vmem_limit_bytes=63 << 20),
        name="pairformer",
    )(pair_rep[0], cotangent[0], tok_mask, tok_types, pair_mask[0], *params)
    anywhere = pl.BlockSpec(memory_space=pl.ANY)
    results = pl.pallas_call(
        hand_over,
        out_shape=[jax.ShapeDtypeStruct(r.shape, r.dtype) for r in results],
        in_specs=[anywhere] * N_OUT,
        out_specs=[anywhere] * N_OUT,
        scratch_shapes=[VM(r.shape, r.dtype) for r in results] + [DMA((2, N_OUT + 6))],
        name="hand_over",
    )(*results)
    results = list(results)
    results[8] = results[8].T
    return tuple(
        [results[0][None], results[1][None]]
        + [r[0] if v.ndim == 1 else r for r, v in zip(results[2:], args[5:])]
    )


def solution(mesh):
    return jax.shard_map(
        per_device,
        mesh=mesh,
        in_specs=(
            P("dp", "dap", None, None),
            P("dp", "dap", None, None),
            P("dp", None),
            P("dp", None),
            P("dp", "dap", None),
            P(),
            P(),
            P(),
            P(),
            P(),
            P(),
            P(),
            P(),
            P(),
            P(),
        ),
        out_specs=(
            P("dp", "dap", None, None),
            P("dp", "dap", None, None),
            P(),
            P(),
            P(),
            P(),
            P(),
            P(),
            P(),
            P(),
            P(),
            P(),
        ),
        check_vma=False,
    )
```

```python
from functools import partial

import jax
import jax.numpy as jnp
from jax import lax
from jax.experimental import pallas as pl
from jax.experimental.pallas import tpu as pltpu
from jax.sharding import PartitionSpec as P

EPSILON = 1e-05
MESH = pl.DeviceIdType.MESH
VM = pltpu.VMEM
DMA = pltpu.SemaphoreType.DMA
BF = jnp.bfloat16
F32 = jnp.float32
EXACT = lax.Precision.HIGHEST


def contract(x, y, dims, precision=None):
    return lax.dot_general(x, y, (dims, ((), ())), precision=precision, preferred_element_type=F32)


def mm(x, y, precision=None):
    return contract(x, y, ((1,), (0,)), precision)


def nt(x, y, precision=None):
    return contract(x, y, ((1,), (1,)), precision)


def tn(x, y, precision=None):
    return contract(x, y, ((0,), (0,)), precision)


def norm_cols(x):
    mean = jnp.sum(x, axis=0, keepdims=True) * (1.0 / 128)
    centred = x - mean
    spread = jnp.sum(centred * centred, axis=0, keepdims=True) * (1.0 / 128)
    scale = lax.rsqrt(spread + EPSILON)
    return centred * scale, scale


def norm_back(grad, unit, scale):
    a = jnp.sum(grad, axis=0, keepdims=True) * (1.0 / 128)
    b = jnp.sum(grad * unit, axis=0, keepdims=True) * (1.0 / 128)
    return scale * (grad - a - unit * b)


def loop(n, fn, unroll=1, first=0):
    def body(i, carry):
        fn(i)
        return carry
    lax.fori_loop(first, n, body, 0, unroll=unroll)


def at(i, size):
    return pl.ds(pl.multiple_of(i * size, size), size)


def halves(x):
    return x[:, :128], x[:, 128:]


def twice(x):
    return jnp.concatenate([x, x], axis=1)


def pair(ref, i):
    return jnp.concatenate([ref[i], ref[i + 1]], axis=1)


def lanes(r):
    return slice(128 * r, 128 * r + 128)


class Sum:
    def __init__(self, n_dp, factor, a, p, refs):
        self.n_dp, self.factor, self.a, self.p = n_dp, factor, a, p
        self.partner, self.cross = a + 1 - 2 * lax.rem(a, 2), lax.rem(a + 2, 4)
        (self.g, self.part, self.quarter, self.pieces, self.mine, self.joined, self.joined_b, self.full,
         self.sa, self.ra, self.sb, self.rb, self.sc, self.rc, self.sd, self.rd) = refs
        self.size = 256 // n_dp

    def remote(self, src, dst, s, r, **peer):
        return pltpu.make_async_remote_copy(
            src_ref=src, dst_ref=dst, send_sem=s, recv_sem=r, device_id=peer, device_id_type=MESH)

    def copy_a(self, r, k):
        peer = lax.rem(self.a + r, 4)
        start, size = ((0, CUT), (CUT, 256 - CUT))[k]
        src = self.g.at[pl.ds(pl.multiple_of(peer * 256 + start, 16), size)]
        return self.remote(
            src, self.part.at[r - 1, start : start + size], self.sa.at[k, r - 1], self.ra.at[k, r - 1], dap=peer)

    def rows_of(self, k, first, size):
        span = (CUT, 256 - CUT)[k]
        while size > 0:
            count = min(size, span - first % span)
            row = 256 * (first // span) + CUT * k + first % span
            yield slice(row, row + count), count
            first, size = first + count, size - count

    def put(self, k, first, block):
        done = 0
        for rows, count in self.rows_of(k, first, block.shape[0]):
            self.g[rows, :] = block[done : done + count].astype(BF)
            done += count

    def get(self, k, first, size):
        return jnp.concatenate([self.full[rows, :] for rows, _ in self.rows_of(k, first, size)], axis=0)

    def copy_b(self, r):
        peer = lax.rem(self.p + r, self.n_dp)
        return self.remote(
            self.quarter.at[at(peer, self.size)], self.pieces.at[r - 1], self.sb, self.rb, dp=peer)

    def copy_c(self, r):
        peer = lax.rem(self.p + r, self.n_dp)
        return self.remote(self.mine, self.joined.at[at(self.p, self.size)], self.sc, self.rc, dp=peer)

    def all_of(self, ref, s, r):
        return self.remote(ref, ref, s, r, dp=lax.rem(self.p + 1, self.n_dp))

    def others(self, ref):
        return ref.at[pl.ds(0, (self.n_dp - 1) * self.size)]

    def copy_d(self, k):
        there = at(self.cross if k == 2 else self.a, 256)
        src = self.full.at[there] if k == 2 else self.joined_b
        return self.remote(
            src, self.full.at[there], self.sd.at[k], self.rd.at[k], dap=self.cross if k == 0 else self.partner)

    def start_a(self, k):
        for r in (2, 1, 3):
            self.copy_a(r, k).start()

    def start_b(self):
        total = self.g[at(self.a, 256), :].astype(F32)
        for r in (1, 2, 3):
            for k in range(2):
                self.copy_a(r, k).wait_recv()
            total = total + self.part[r - 1].astype(F32)
        self.quarter[...] = total
        for r in range(1, self.n_dp):
            self.copy_b(r).start()

    def start_c(self):
        self.all_of(self.pieces, self.sb, self.rb).wait_recv()
        total = self.quarter[at(self.p, self.size), :] + jnp.sum(self.pieces[...], axis=0)
        self.mine[...] = total * self.factor
        for r in range(1, self.n_dp):
            self.copy_c(r).start()
        self.joined[at(self.p, self.size), :] = self.mine[...]

    def start_d(self):
        self.all_of(self.others(self.joined), self.sc, self.rc).wait_recv()
        self.joined_b[...] = self.joined[...].astype(BF)
        self.copy_d(0).start()
        self.copy_d(1).start()
        self.full[at(self.a, 256), :] = self.joined_b[...]

    def finish(self):
        self.copy_d(0).wait_recv()
        self.copy_d(2).start()
        self.copy_d(1).wait_recv()
        self.copy_d(2).wait_recv()

    def settle(self):
        for r in (1, 2, 3):
            for k in range(2):
                self.copy_a(r, k).wait_send()
        self.all_of(self.pieces, self.sb, self.rb).wait_send()
        self.all_of(self.others(self.joined), self.sc, self.rc).wait_send()
        for k in range(3):
            self.copy_d(k).wait_send()

    @staticmethod
    def scratch(n_dp):
        size = 256 // n_dp
        return [
            VM((1024, 128), BF), VM((3, 256, 128), BF), VM((256, 128), F32), VM((n_dp - 1, size, 128), F32),
            VM((size, 128), F32), VM((256, 128), F32), VM((256, 128), BF), VM((1024, 128), BF),
        ] + [DMA((2, 3))] * 2 + [DMA] * 4 + [DMA((3,))] * 2


N_IN, N_OUT, N_SUM = 15, 12, 16
STRIP, SPLIT, CUT = 16, 8, 176


def kernel(n_dp, factor, *refs):
    (slab, cot, tok_mask, tok_types, pair_mask, gain1, tri_in, tri_gate, gain2, tri_out, gain3, att_bias, att_in,
     att_out, table) = refs[:N_IN]
    (out, grad, o_gain1, o_tri_in, o_tri_gate, o_gain2, o_tri_out, o_gain3, o_att_bias, o_att_in, o_att_out,
     o_table) = refs[N_IN : N_IN + N_OUT]
    rest = refs[N_IN + N_OUT :]
    a, p = lax.axis_index("dap"), lax.axis_index("dp")
    partner, cross, chip, core = a + 1 - 2 * lax.rem(a, 2), lax.rem(a + 2, 4), a // 2, lax.rem(a, 2)
    early = Sum(n_dp, factor, a, p, rest[:N_SUM])
    late = Sum(n_dp, factor, a, p, rest[N_SUM : 2 * N_SUM])
    (live, live_t, tok_t, g1, g2, g3, w1, w1t, wat, wot, woutt, wb, wbt, hot, tab, bt,
     mid, dn3, prod, right, left_f, right_f, gates, pieces, normed, bias_f, bias_b, bias,
     d_bias, d_wa, d_wo, d_wout, d_wb, d_w1, gain_sum,
     db_n, db_in, db_f, d_prod, d_mid, d_gate, work, far, far_in, sent, cross_in, near, near_in,
     slab_t, cot_t, d_gated_t, scales, zs, sem_es, sem_er, sem_is, sem_ir, sem_bs, sem_br, sem_s, sem_r) = rest[2 * N_SUM :]
    part = gates

    barrier = pltpu.get_barrier_semaphore()
    for r in range(1, 4):
        pl.semaphore_signal(barrier, inc=1, device_id={"dap": lax.rem(a + r, 4)}, device_id_type=MESH)
    for r in range(1, n_dp):
        pl.semaphore_signal(barrier, inc=1, device_id={"dp": lax.rem(p + r, n_dp)}, device_id_type=MESH)

    rows_i = lax.broadcasted_iota(jnp.int32, (128, 128), 0)
    unit = (rows_i == lax.broadcasted_iota(jnp.int32, (128, 128), 1)).astype(F32).astype(BF)

    def flip(block):
        return nt(unit, block)

    def flipped(ref, i):
        return jnp.concatenate([flip(ref[i]), flip(ref[i + 1])], axis=1)

    def column(row):
        return jnp.broadcast_to(row, (128, 128)).T

    tokens = tok_mask[...].astype(F32)
    tok_t[...] = column(tokens)
    live[...] = pair_mask[...].astype(F32) * tok_t[at(a, 32), :] * tokens
    live_t[...] = tn(live[...].astype(BF), unit[:32, :32]).astype(BF)
    for gain, row in ((g1, gain1), (g2, gain2), (g3, gain3)):
        gain[...] = column(row[...])
    w1[:, 0:256] = tri_in[:, 0:256]
    w1[:, 256:384] = tri_gate[...]
    w1[:, 384:640] = tri_in[:, 256:512]
    for b in range(5):
        w1t[128 * b : 128 * b + 128, :] = flip(w1[:, lanes(b)]).astype(BF)
    for b in range(4):
        wat[128 * b : 128 * b + 128, :] = flip(att_in[:, lanes(b)]).astype(BF)
    wot[...] = flip(att_out[...]).astype(BF)
    woutt[...] = flip(tri_out[...]).astype(BF)
    wbt[...] = jnp.concatenate([att_bias[...].astype(F32), jnp.zeros((12, 128), F32)], axis=0).astype(BF)
    wb[...] = flip(wbt[...]).astype(BF)
    tab[...] = jnp.zeros_like(tab)
    tab[:, 0:4, 0:4] = table[...]
    hot[...] = (lax.broadcasted_iota(jnp.int32, (16, 128), 0) == tok_types[...]).astype(F32)

    def alive_of(i):
        return jnp.concatenate([live[pl.ds(i, 1), :], live[pl.ds(i + 1, 1), :]], axis=1)


    def edge(kind, c):
        block = right.at[cross if kind == 2 else a]
        spot = block.at[8 * c : 8 * c + 8] if c < 2 else block.at[16:32, 64 * (c - 2) : 64 * (c - 1), :]
        return pltpu.make_async_remote_copy(
            src_ref=spot, dst_ref=spot, send_sem=sem_es.at[kind, c], recv_sem=sem_er.at[kind, c],
            device_id={"dap": cross if kind == 1 else partner}, device_id_type=MESH)

    def project(t):
        i = 2 * t
        x = flipped(slab, i)
        hat, _ = norm_cols(x)
        n = (hat * twice(g1[...])).astype(BF)
        q = mm(w1t[...], n)
        alive = alive_of(i)
        sa, sb = jax.nn.sigmoid(q[128:256]), jax.nn.sigmoid(q[512:])
        fa, fb = sa * alive, sb * alive
        lft, rgt = fa * q[:128], fb * q[384:512]
        ga, gb = lft * (1.0 - sa), rgt * (1.0 - sb)
        lft, rgt = lft.astype(BF).astype(F32), rgt.astype(BF)
        x = x.astype(BF)
        gate = jax.nn.sigmoid(q[256:384])
        for r in range(2):
            normed[i + r] = n[:, lanes(r)]
            slab_t[i + r] = x[:, lanes(r)]
            left_f[pl.ds((i + r) * 129, 128), :] = lft[:, lanes(r)]
            right[a, i + r] = rgt[:, lanes(r)]
            gates[i + r] = gate[:, lanes(r)]
            pieces[i + r, 0:128] = fa[:, lanes(r)]
            pieces[i + r, 128:256] = ga[:, lanes(r)]
            pieces[i + r, 256:384] = fb[:, lanes(r)]
            pieces[i + r, 384:512] = gb[:, lanes(r)]

    loop(4, project, 2)
    pl.semaphore_wait(barrier, 3 + n_dp - 1)
    for c, (low_t, high_t) in enumerate(((0, 0), (4, 8), (8, 16), (0, 0))):
        if high_t > low_t:
            loop(high_t, project, 2, first=low_t)
        edge(1, c).start()
        edge(0, c).start()

    def unpack(block, base, rows=(0, 32), chans=(0, 128)):
        span = slice(*chans)

        def one(j):
            start = (base + j) * 129 + chans[0]
            right_f[pl.ds(start, chans[1] - chans[0]), :] = right[block, j, span].astype(F32)

        loop(rows[1], one, 4, first=rows[0])

    def multiply(half, chans=(0, 128)):
        def one(ch):
            lft = left_f[pl.ds(ch, 32, stride=129), :].astype(BF)
            rgt = right_f[pl.ds(64 * 129 * half + ch, 64, stride=129), :].astype(BF)
            prod[pl.ds(ch * 33, 32), 64 * half : 64 * half + 64] = nt(lft, rgt)
        loop(chans[1], one, 16, first=chans[0])

    for c in range(4):
        edge(0, c).wait_recv()
    low = 2 * chip
    unpack(low, 0)
    unpack(low + 1, 32)
    multiply(0)

    def prepare(t):
        i = 2 * t
        ct = flipped(cot, i).astype(BF)
        dg = mm(att_out[...], ct).astype(BF)
        for r in range(2):
            cot_t[i + r] = ct[:, lanes(r)]
            d_gated_t[i + r] = dg[:, lanes(r)]

    loop(16, prepare, 4)

    beside = cross + 1 - 2 * core
    for c in range(4):
        rows, chans = ((8 * c, 8 * c + 8), (0, 128)) if c < 2 else ((16, 32), (64 * (c - 2), 64 * (c - 1)))
        edge(1, c).wait_recv()
        edge(2, c).start()
        unpack(cross, 64 + 32 * core, rows, chans)
        edge(2, c).wait_recv()
        unpack(beside, 96 - 32 * core, rows, chans)
        if c >= 2:
            multiply(1, chans)

    def second(t):
        i = 2 * t
        xs = []
        for r in range(2):
            rows = pl.ds(i + r, 128, stride=33)
            xs.append(pltpu.roll(prod[rows, :], 64 * chip, axis=1))
        hat, scale_2 = norm_cols(jnp.concatenate(xs, axis=1))
        n = (hat * twice(g2[...])).astype(BF)
        z = mm(woutt[...], n)
        for r in range(2):
            prod[pl.ds(i + r, 128, stride=33), :] = hat[:, lanes(r)]
            scales[pl.ds(32 + i + r, 1), :] = scale_2[:, lanes(r)]
            zs[i + r] = z[:, lanes(r)]
        middle = (pair(slab_t, i).astype(F32) + pair(gates, i) * z).astype(BF)
        hat, _ = norm_cols(middle.astype(F32))
        n = (hat * twice(g3[...])).astype(BF)
        heads = mm(wbt[...], n)
        for r in range(2):
            mid[i + r] = middle[:, lanes(r)]
            for h in range(4):
                bias_f[h, pl.ds(i + r, 1), :] = heads[h : h + 1, lanes(r)]

    loop(16, second, 8)
    bias_b[...] = bias_f[...].astype(BF)

    def share_bias(r):
        return pltpu.make_async_remote_copy(
            src_ref=bias_b, dst_ref=bias.at[:, at(a, 32), :], send_sem=sem_is.at[r - 1], recv_sem=sem_ir.at[r - 1],
            device_id={"dap": lax.rem(a + r, 4)}, device_id_type=MESH)

    for r in (2, 1, 3):
        share_bias(r).start()
    bias[:, at(a, 32), :] = bias_b[...]
    for h in range(4):
        near_types = mm(tab[h].T, hot[...], EXACT)
        bt[:, lanes(h)] = tn(hot[...], near_types, EXACT)
    for ref in (d_bias, d_wa, d_wo, d_wout, d_wb, d_w1, gain_sum):
        ref[...] = jnp.zeros_like(ref)
    for r in (1, 2, 3):
        share_bias(r).wait_recv()
    for h in range(4):
        bt[:, lanes(h)] += flip(bias[h])


    def spread(x):
        zero = jnp.zeros((32, 128), x.dtype)
        cols = [
            jnp.concatenate([x[32 * h : 32 * h + 32] if g == h else zero for g in range(4)], axis=0)
            for h in range(4)
        ]
        return jnp.concatenate(cols, axis=1)

    scale = 32.0 ** -0.5

    def attend(t):
        i = 2 * t
        m = pair(mid, i).astype(F32)
        hat, _ = norm_cols(m)
        n = (hat * twice(g3[...])).astype(BF)
        q3 = mm(wat[...], n)
        qkv = q3[:384].astype(BF)
        gate = jax.nn.sigmoid(q3[384:])
        ct = pair(cot_t, i)
        d_gated = pair(d_gated_t, i).astype(F32)
        d_att = d_gated * gate
        picked = lax.broadcasted_iota(jnp.int32, (32, 256), 0) == (
            i + lax.broadcasted_iota(jnp.int32, (32, 256), 1) // 128)
        alive = mm(live_t[...], picked.astype(F32).astype(BF))
        both = range(2)
        qs, ks, vs = ([qkv[128 * x : 128 * x + 128, lanes(r)] for r in both] for x in range(3))
        kvs = [flip(qkv[128:384, lanes(r)]).astype(BF) for r in both]
        dos = [d_att[:, lanes(r)].astype(BF) for r in both]
        scores = [mm(kvs[r][:, :128], spread(qs[r])) for r in both]
        das = [mm(kvs[r][:, 128:], spread(dos[r])).astype(BF) for r in both]
        exps = [
            jnp.exp(scores[r] * scale + bt[...]) * jnp.concatenate([alive[:, lanes(r)]] * 4, axis=1) for r in both
        ]
        sums = [jnp.sum(e, axis=0, keepdims=True) for e in exps]
        ws = [e * (1.0 / jnp.maximum(s, 1.0)) for e, s in zip(exps, sums)]
        abs_ = [w.astype(BF) for w in ws]
        us = [da.astype(F32) * w for da, w in zip(das, ws)]
        totals = [jnp.sum(u, axis=0, keepdims=True) for u in us]
        totals = [
            jnp.where(s > 1.0, x, jnp.where(s == 1.0, 0.5 * x, 0.0)) for s, x in zip(sums, totals)
        ]
        dss = [u - w * x for u, w, x in zip(us, ws, totals)]
        d_bias[...] += dss[0] + dss[1]
        dsbs = [ds.astype(BF) for ds in dss]

        def heads_of(fn):
            return jnp.concatenate([fn(slice(32 * h, 32 * h + 32), lanes(h)) for h in range(4)], axis=0)

        atts = [heads_of(lambda h, l: mm(vs[r][h], abs_[r][:, l])) for r in both]
        dvs = [heads_of(lambda h, l: nt(dos[r][h], abs_[r][:, l])) for r in both]
        dks = [heads_of(lambda h, l: nt(qs[r][h], dsbs[r][:, l])) * scale for r in both]
        dqs = [heads_of(lambda h, l: mm(ks[r][h], dsbs[r][:, l])) * scale for r in both]
        parts = [jnp.concatenate([dqs[r], dks[r], dvs[r]], axis=0).astype(BF) for r in both]
        att = jnp.concatenate(atts, axis=1)
        d_open = (d_gated * att * gate * (1.0 - gate)).astype(BF)
        dp = jnp.concatenate([jnp.concatenate(parts, axis=1), d_open], axis=0)
        dn = mm(att_in[...], dp).astype(BF)
        d_wa[...] += nt(dp, n)
        gated = (gate * att).astype(BF)
        d_wo[...] += nt(gated, ct)
        res = (m + mm(wot[...], gated)).astype(BF)
        for r in range(2):
            dn3[i + r] = dn[:, lanes(r)]
            out[i + r] = flip(res[:, lanes(r)]).astype(BF)

    loop(16, attend, 8)

    for h in range(4):
        db_n[h] = flip(d_bias[:, lanes(h)].astype(BF)).astype(BF)

    def share_grad(r):
        peer = lax.rem(a + r, 4)
        return pltpu.make_async_remote_copy(
            src_ref=db_n.at[:, at(peer, 32), :], dst_ref=db_in.at[r - 1], send_sem=sem_bs.at[r - 1],
            recv_sem=sem_br.at[r - 1], device_id={"dap": peer}, device_id_type=MESH)

    for r in (2, 1, 3):
        share_grad(r).start()
    early.g[0:512, :] = d_wa[...].astype(BF)
    early.g[512:640, :] = d_wo[...].astype(BF)
    early.g[640:, :] = jnp.zeros((384, 128), BF)
    for h in range(4):
        near_types = mm(hot[...], d_bias[:, lanes(h)])
        early.g[640 + 16 * h : 656 + 16 * h, 0:16] = nt(hot[...], near_types).astype(BF)
    early.start_a(0)
    early.start_a(1)

    for r in (1, 2, 3):
        share_grad(r).wait_recv()
    total = db_n[:, at(a, 32), :].astype(F32)
    for r in range(3):
        total = total + db_in[r].astype(F32)
    db_f[...] = total


    def fold(x):
        return x[:, :128] + x[:, 128:]

    def second_back(t):
        i = 2 * t
        hat3, scale3 = norm_cols(pair(mid, i).astype(F32))
        gain3, gain2 = twice(g3[...]), twice(g2[...])
        n3 = (hat3 * gain3).astype(BF)
        rows = [
            jnp.concatenate([db_f[h, pl.ds(i, 1), :], db_f[h, pl.ds(i + 1, 1), :]], axis=1) for h in range(4)
        ]
        db = jnp.concatenate(rows + [jnp.zeros((12, 256), F32)], axis=0).astype(BF)
        dn = pair(dn3, i).astype(F32) + mm(wb[...], db)
        d_wb[...] += nt(db, n3)
        gain_sum[2] += fold(dn * hat3)
        dm = pair(cot_t, i) + norm_back(dn * gain3, hat3, scale3).astype(BF)
        dmf = dm.astype(F32)
        hat2 = jnp.concatenate([prod[pl.ds(i, 128, stride=33), :], prod[pl.ds(i + 1, 128, stride=33), :]], axis=1)
        scale2 = jnp.concatenate([scales[pl.ds(32 + i, 1), :], scales[pl.ds(33 + i, 1), :]], axis=1)
        n2 = (hat2 * gain2).astype(BF)
        z = pair(zs, i)
        gate = pair(gates, i)
        dz = (dmf * gate).astype(BF)
        d_open = (dmf * z * gate * (1.0 - gate)).astype(BF)
        d_wout[...] += nt(n2, dz)
        dn2 = mm(tri_out[...], dz).astype(BF).astype(F32)
        gain_sum[1] += fold(dn2 * hat2)
        dp = norm_back(dn2 * gain2, hat2, scale2)
        for r in range(2):
            d_prod[pl.ds(i + r, 128, stride=33), :] = pltpu.roll(dp[:, lanes(r)], 64 * chip, axis=1)
            d_mid[i + r] = dm[:, lanes(r)]
            d_gate[i + r] = d_open[:, lanes(r)]

    loop(16, second_back, 8)

    def chunk(ref, q):
        return ref.at[:, at(q, STRIP), :]

    def move(kind, q):
        src, dst, peer = (
            (far.at[1 - core], far_in, partner), (sent, cross_in, cross), (near.at[1 - core], near_in, partner),
        )[kind]
        return pltpu.make_async_remote_copy(
            src_ref=chunk(src, q), dst_ref=chunk(dst, q), send_sem=sem_s.at[kind, q], recv_sem=sem_r.at[kind, q],
            device_id={"dap": peer}, device_id_type=MESH)

    def right_grads(half, q, store):
        def one(c):
            ch = STRIP * q + c
            dp = d_prod[pl.ds(ch * 33, 32), 64 * half : 64 * half + 64].astype(BF)
            work[pl.ds(c, 64, stride=STRIP + 1), :] = tn(dp, left_f[pl.ds(ch, 32, stride=129), :].astype(BF))

        loop(STRIP, one, 16)

        def pack(j):
            store[j // 32, lax.rem(j, 32), at(q, STRIP), :] = work[pl.ds(j * (STRIP + 1), STRIP), :].astype(BF)

        loop(64, pack, 8)

    def add_on(q):
        move(0, q).wait_recv()

        def one(j):
            spot = at(q, STRIP)
            sent[j, spot, :] = (far[core, j, spot, :].astype(F32) + far_in[j, spot, :].astype(F32)).astype(BF)

        loop(32, one, 8)
        move(1, q).start()

    def out_far(q):
        right_grads(1, q, far)
        move(0, q).start()
        pl.when(q > 0)(lambda: add_on(q - 1))

    loop(SPLIT, out_far)
    early.start_b()

    def out_near(q):
        right_grads(0, q, near)
        move(2, q).start()
        pl.when(q == 0)(lambda: add_on(SPLIT - 1))

    loop(SPLIT, out_near)
    early.start_c()

    def left_grad(ch):
        rgt = right_f[pl.ds(ch, 128, stride=129), :].astype(BF)
        left_f[pl.ds(ch, 32, stride=129), :] = mm(d_prod[pl.ds(ch * 33, 32), :].astype(BF), rgt)

    loop(128, left_grad, 16)

    def stored(i, k):
        rows = slice(128 * k, 128 * k + 128)
        return jnp.concatenate([pieces[i, rows], pieces[i + 1, rows]], axis=1)

    def left_part(t):
        i = 2 * t
        dl = jnp.concatenate([left_f[pl.ds(i * 129, 128), :], left_f[pl.ds(i * 129 + 129, 128), :]], axis=1).astype(BF).astype(F32)
        dp = jnp.concatenate(
            [(dl * stored(i, 0)).astype(BF), (dl * stored(i, 1)).astype(BF), pair(d_gate, i)], axis=0)
        d_w1[0:384, :] += nt(dp, pair(normed, i))
        dn = mm(w1[:, 0:384], dp)
        part[i] = dn[:, :128]
        part[i + 1] = dn[:, 128:]

    loop(16, left_part, 4)

    loop(SPLIT, lambda q: move(2, q).wait_recv())

    def settle_near(t):
        i = 2 * t
        hat, scale_1 = norm_cols(pair(slab_t, i).astype(F32))
        for r in range(2):
            right_f[at(i + r, 128), :] = near[core, i + r].astype(F32) + near_in[i + r].astype(F32)
            right_f[at(32 + i + r, 128), :] = hat[:, lanes(r)]
            scales[pl.ds(i + r, 1), :] = scale_1[:, lanes(r)]

    loop(16, settle_near, 2)
    ones = jnp.ones((16, 128), F32)

    def put_gain(k, first, which):
        late.put(k, first, nt(ones, gain_sum[which], EXACT))

    late.put(0, 0, d_w1[0:384, :])
    late.put(0, 384, d_wout[...])
    late.put(0, 512, d_wb[...])
    put_gain(0, 528, 1)
    put_gain(0, 544, 2)
    late.put(0, 560, jnp.zeros((144, 128), F32))
    loop(SPLIT, lambda q: move(1, q).wait_recv())
    early.start_d()
    late.start_a(0)

    def right_part(t):
        i = 2 * t

        def held(j):
            return jnp.concatenate([right_f[at(j, 128), :], right_f[at(j + 1, 128), :]], axis=1)

        dr = (held(i) + pair(cross_in, i).astype(F32)).astype(BF).astype(F32)
        dp = jnp.concatenate([(dr * stored(i, 2)).astype(BF), (dr * stored(i, 3)).astype(BF)], axis=0)
        d_w1[384:640, :] += nt(dp, pair(normed, i))
        dn = (pair(part, i) + mm(w1[:, 384:640], dp)).astype(BF).astype(F32)
        hat = held(32 + i)
        spread_1 = jnp.concatenate([scales[pl.ds(i, 1), :], scales[pl.ds(i + 1, 1), :]], axis=1)
        gain_sum[0] += fold(dn * hat)
        dx = norm_back(dn * twice(g1[...]), hat, spread_1).astype(BF)
        res = pair(d_mid, i) + dx
        grad[i] = flip(res[:, :128]).astype(BF)
        grad[i + 1] = flip(res[:, 128:]).astype(BF)

    loop(16, right_part, 8)


    late.put(1, 0, d_w1[384:640, :])
    put_gain(1, 256, 0)
    late.put(1, 272, jnp.zeros((48, 128), F32))
    late.start_a(1)
    early.finish()
    for b in range(4):
        o_att_in[:, lanes(b)] = flip(early.full[128 * b : 128 * b + 128, :])
    o_att_out[...] = early.full[512:640, :].astype(F32)
    for h in range(4):
        o_table[h] = early.full[640 + 16 * h : 656 + 16 * h, :].astype(F32)[0:4, 0:4]
    late.start_b()
    early.settle()
    late.start_c()
    for r in (1, 2, 3):
        share_bias(r).wait_send()
        share_grad(r).wait_send()
    for kind in range(3):
        for c in range(4):
            edge(kind, c).wait_send()
        loop(SPLIT, lambda q: move(kind, q).wait_send())
    late.start_d()
    late.finish()
    for b in range(2):
        o_tri_in[:, lanes(b)] = flip(late.get(0, 128 * b, 128))
        o_tri_in[:, lanes(b + 2)] = flip(late.get(1, 128 * b, 128))
    o_tri_gate[...] = flip(late.get(0, 256, 128))
    o_tri_out[...] = late.get(0, 384, 128).astype(F32)
    o_att_bias[...] = late.get(0, 512, 16).astype(F32)[0:4, :]
    for ref, k, first in ((o_gain1, 1, 256), (o_gain2, 0, 528), (o_gain3, 0, 544)):
        ref[...] = late.get(k, first, 16).astype(F32)[0:1, :]
    late.settle()


def hand_over(*refs):
    held, sems = refs[2 * N_OUT : 3 * N_OUT], refs[3 * N_OUT]
    parts = [(k, pl.ds(8 * c, 8), 4 * k + c) for k in range(2) for c in range(4)]
    parts += [(k, slice(None), 6 + k) for k in range(2, N_OUT)]
    reads = [pltpu.make_async_copy(refs[k].at[s], held[k].at[s], sems.at[0, n]) for k, s, n in parts]
    writes = [pltpu.make_async_copy(held[k].at[s], refs[N_OUT + k].at[s], sems.at[1, n]) for k, s, n in parts]
    for copy in reads:
        copy.start()
    for read, write in zip(reads, writes):
        read.wait()
        write.start()
    for copy in writes:
        copy.wait()


def per_device(*args):
    pair_rep, cotangent, tok_mask, tok_types, pair_mask = args[:5]
    params = [v[None] if v.ndim == 1 else v for v in args[5:]]
    params[6] = params[6].T
    n_dp = lax.axis_size("dp")
    factor = (128 * 128 * n_dp) ** (-0.5)
    block = (32, 128, 128)
    shapes = [v.shape for v in params]
    spec = pl.BlockSpec(memory_space=VM)
    scratch = Sum.scratch(n_dp) * 2 + [
        VM((32, 128), F32), VM((128, 32), BF), VM((128, 128), F32),
        VM((128, 128), F32), VM((128, 128), F32), VM((128, 128), F32),
        VM((128, 640), BF), VM((640, 128), BF), VM((512, 128), BF), VM((128, 128), BF), VM((128, 128), BF),
        VM((128, 16), BF), VM((16, 128), BF), VM((16, 128), F32), VM((4, 16, 16), F32), VM((128, 512), F32),
        VM(block, BF), VM(block, BF), VM((4224, 128), F32), VM((4,) + block, BF), VM((4128, 128), F32),
        VM((16512, 128), F32), VM(block, F32), VM((32, 512, 128), F32), VM(block, BF),
        VM((4, 32, 128), F32), VM((4, 32, 128), BF), VM((4, 128, 128), BF),
        VM((128, 512), F32), VM((512, 128), F32), VM((128, 128), F32), VM((128, 128), F32), VM((16, 128), F32),
        VM((640, 128), F32), VM((3, 128, 128), F32),
        VM((4, 128, 128), BF), VM((3, 4, 32, 128), BF), VM((4, 32, 128), F32), VM((4224, 128), F32),
        VM(block, BF), VM(block, BF), VM((64 * (STRIP + 1), 128), F32),
        VM((2,) + block, BF), VM(block, BF), VM(block, BF), VM(block, BF), VM((2,) + block, BF), VM(block, BF),
        VM(block, BF), VM(block, BF), VM(block, BF), VM((64, 128), F32), VM(block, F32),
        DMA((3, 4)), DMA((3, 4)), DMA((3,)), DMA((3,)), DMA((3,)), DMA((3,)), DMA((3, SPLIT)), DMA((3, SPLIT)),
    ]
    results = pl.pallas_call(
        partial(kernel, n_dp, factor),
        out_shape=[jax.ShapeDtypeStruct(block, BF)] * 2 + [jax.ShapeDtypeStruct(s, F32) for s in shapes],
        in_specs=[spec] * N_IN,
        out_specs=[spec] * N_OUT,
        scratch_shapes=scratch,
        compiler_params=pltpu.CompilerParams(collective_id=0, has_side_effects=True, vmem_limit_bytes=63 << 20),
        name="pairformer",
    )(pair_rep[0], cotangent[0], tok_mask, tok_types, pair_mask[0], *params)
    anywhere = pl.BlockSpec(memory_space=pl.ANY)
    results = pl.pallas_call(
        hand_over,
        out_shape=[jax.ShapeDtypeStruct(r.shape, r.dtype) for r in results],
        in_specs=[anywhere] * N_OUT,
        out_specs=[anywhere] * N_OUT,
        scratch_shapes=[VM(r.shape, r.dtype) for r in results] + [DMA((2, N_OUT + 6))],
        name="hand_over",
    )(*results)
    results = list(results)
    results[8] = results[8].T
    return tuple(
        [results[0][None], results[1][None]]
        + [r[0] if v.ndim == 1 else r for r, v in zip(results[2:], args[5:])]
    )


def solution(mesh):
    return jax.shard_map(
        per_device,
        mesh=mesh,
        in_specs=(
            P("dp", "dap", None, None),
            P("dp", "dap", None, None),
            P("dp", None),
            P("dp", None),
            P("dp", "dap", None),
            P(),
            P(),
            P(),
            P(),
            P(),
            P(),
            P(),
            P(),
            P(),
            P(),
        ),
        out_specs=(
            P("dp", "dap", None, None),
            P("dp", "dap", None, None),
            P(),
            P(),
            P(),
            P(),
            P(),
            P(),
            P(),
            P(),
            P(),
            P(),
        ),
        check_vma=False,
    )
```
